256 devices in a mesh: head: 8 (over z), pool: 32 (over y, x, core).
Axes of the slice: x: 4, y: 4, z: 8, core: 2. Of those that a mesh axis runs over, the one named last changes fastest.
Arguments:
- queries: bfloat16 [320, 2048], P('pool', 'head'), may hold values from -6 to 6
- fresh_pair: bfloat16 [320, 2, 2048], P('pool', None, 'head'), may hold values from -6 to 6
- cache_blocks: bfloat16 [1152, 2, 64, 2048], P('pool', None, None, 'head'), may hold values from -6 to 6
- block_table: int32 [320, 256], replicated, may hold values from -1 to 1151, as said below
- lengths: int32 [320], replicated, may hold values from 65 to 16384, as said below
- residual: bfloat16 [320, 2048], P('pool'), may hold values from -6 to 6
- w_output: bfloat16 [2048, 2048], P('head'), may hold values from -0.125 to 0.125
- norm_gain: bfloat16 [2048], replicated, may hold values from 0.5 to 1.5
- routes: int32 [320, 6], replicated, may hold values from 0 to 63, all different within a row; in each aligned block of 10 rows (0 to 9, 10 to 19, ...) at most 2 rows name the same one
- route_gates: float32 [320, 6], replicated, may hold values from 0.1 to 0.6
- w_gate_up: bfloat16 [64, 2048, 2, 1408], P('pool', 'head'), may hold values from -0.125 to 0.125
- w_down: bfloat16 [64, 1408, 2048], P('pool', None, 'head'), may hold values from -0.15625 to 0.15625
- shared_gate_up: bfloat16 [1, 2048, 2, 1408], P(None, 'head'), may hold values from -0.125 to 0.125
- shared_down: bfloat16 [1, 1408, 2048], P(None, None, 'head'), may hold values from -0.15625 to 0.15625
- next_gain: bfloat16 [2048], replicated, may hold values from 0.5 to 1.5
- w_query_key_value: bfloat16 [2048, 6144], P(None, 'head'), may hold values from -0.125 to 0.125
Outputs:
- next_hidden: bfloat16 [320, 2048], P('pool')
- next_query_key_value: bfloat16 [320, 6144], P('pool', 'head')
The draws below stay inside these ranges and needn't reach their ends.
Inputs may be any that keep to these rules, and one draw needn't show every extreme that they name: `block_table`: row r lists request r's blocks in order, then -1; 2 requests have 256 blocks and the others 2; no block is listed twice; block g lies on pool device g // 36. `lengths`: A request with n blocks holds (n - 1) * 64 + 1 to n * 64 tokens; some request holds 16384. `routes`: each row names 6 different experts; within the 10 rows of one pool device no expert is named more than 2 times, a bound that some block reaches.
All inputs are finite; a program needn't handle non-finite values.
Results may differ from the reference program's by a relative error of at most 0.025.
Values may be sent and summed in bfloat16 or wider, within the bound.
A program may use at most 128 MiB of HBM per device.

```python
import math
import jax
import jax.numpy as jnp
import numpy as np
from jax import lax

D = 2048
H = 16
HD = 128
EXP = 64
FFE = 1408
TOPK = 6
NSH = 1
BS = 64
SB = 2
R_LONG = 2
REQ_DEV = 10
MOST = 2
REQ = 320
LONG_BLOCKS = 256
BLK_DEV = 36
NBLK = 1152
N_POOL = 32


def table_and_lengths(key):
    base = jax.random.fold_in(key, 301)
    order = jax.random.permutation(jax.random.fold_in(base, 1), REQ).astype(jnp.int32)
    is_long = jnp.zeros((REQ,), jnp.int32).at[order[:R_LONG]].set(1)
    counts = jnp.where(is_long == 1, LONG_BLOCKS, SB).astype(jnp.int32)
    offsets = jnp.cumsum(counts) - counts
    shuffled = jax.random.permutation(jax.random.fold_in(base, 2), NBLK).astype(jnp.int32)
    columns = jnp.arange(LONG_BLOCKS, dtype=jnp.int32)
    picks = jnp.minimum(offsets[:, None] + columns[None, :], NBLK - 1).astype(jnp.int32)
    table = jnp.where(columns[None, :] < counts[:, None], shuffled[picks], -1).astype(jnp.int32)
    tail = jax.random.randint(jax.random.fold_in(base, 3), (REQ,), 1, BS + 1).astype(jnp.int32)
    token_counts = (counts - 1) * BS + tail
    full_one = order[0]
    token_counts = jnp.where(jnp.arange(REQ, dtype=jnp.int32) == full_one, counts * BS, token_counts)
    return (table, token_counts.astype(jnp.int32))


def draw_block_table(key, part):
    return table_and_lengths(key)[0]


def draw_lengths(key, part):
    return table_and_lengths(key)[1]


def draw_queries(key, part):
    noise = jax.random.normal(jax.random.fold_in(key, 11), (REQ, H * HD), jnp.float32)
    values = noise
    return jnp.clip(values, -6.0, 6.0).astype(jnp.bfloat16)


def draw_cache_blocks(key, part):
    values = jax.random.normal(jax.random.fold_in(key, 21), (NBLK, 2, BS, H * HD), jnp.float32)
    return jnp.clip(values, -6.0, 6.0).astype(jnp.bfloat16)


def block_scale(rng, extent, pieces, least, top_value):
    def one(axis_at, blocks):
        draws = jax.random.uniform(jax.random.fold_in(jax.random.fold_in(rng, 6), axis_at), (blocks,), jnp.float32, least / len(pieces), top_value / len(pieces))
        return jnp.repeat(jnp.exp(draws), extent[axis_at] // blocks).reshape((-1,) + (1,) * (len(extent) - axis_at - 1))

    factor_of = one(*pieces[0])
    for cut in pieces[1:]:
        factor_of = factor_of * one(*cut)
    return factor_of


def routed_block(stream_key, own, number, rows, count, top, limit, lean):
    sequence = jax.random.permutation(stream_key, count)
    packed, common = load_shares(count, rows * top, limit, lean, True), load_shares(count, rows * top, limit, lean, False)
    places = jnp.arange(count)

    def named(sizes, turn):
        used = int((sizes > 0).sum())
        fixed = max(1, used // 4)
        shifted = fixed + (places - fixed + turn * (used - fixed)) % max(1, count - fixed)
        return jnp.zeros((count,), jnp.int32).at[sequence[jnp.where(places < fixed, places, shifted)]].set(jnp.asarray(sizes, jnp.int32))

    sizes = jnp.where(number % 4 == 0, named(packed, number // 4), named(common, number - number // 4 - 1))
    mixed = jax.random.permutation(jax.random.fold_in(own, 3), count)
    donor, receiver = mixed[0:count // 2 * 2:2], mixed[1:count // 2 * 2:2]
    margin = jnp.minimum(sizes[donor] - 1, limit - sizes[receiver]) // 2
    margin = jnp.where((donor == sequence[0]) | (receiver == sequence[0]) | (sizes[receiver] == 0), 0, jnp.maximum(margin, 0))
    shifted = jax.random.randint(jax.random.fold_in(own, 4), (count // 2,), 0, 1 << 20) % (margin + 1)
    sizes = sizes.at[donor].add(-shifted).at[receiver].add(shifted)
    items = jnp.searchsorted(jnp.cumsum(sizes), jnp.arange(rows * top), side="right").astype(jnp.int32)
    listing = items.reshape(top, rows).T
    listing = listing[jax.random.permutation(jax.random.fold_in(own, 1), rows)]
    turn = jax.random.randint(jax.random.fold_in(own, 2), (rows, 1), 0, top)
    return jnp.take_along_axis(listing, (jnp.arange(top)[None, :] + turn) % top, axis=1)


def load_shares(number_of, total, limit, lean, full):
    weights = [(1 << 20) // math.isqrt(standing ** lean) + 1 for standing in range(1, number_of + 1)]
    largest = limit if full else min(limit, max(-(-total // number_of), total * weights[0] // sum(weights)))
    least = 1 if total - largest >= number_of - 1 else 0
    given, spare = [largest] + [least] * (number_of - 1), total - largest - least * (number_of - 1)
    while spare > 0:
        candidates = [i for i in range(1, number_of) if given[i] < largest] or [i for i in range(1, number_of) if given[i] < limit]
        pool, budget = sum([weights[i] for i in candidates]), spare
        for i in candidates:
            more = min(limit - given[i], max(1, budget * weights[i] // pool), spare)
            given[i] = given[i] + more
            spare = spare - more
    return np.array(given)


def scatter_about(stream_key, shape, scale, limit, shards=(), kind=jnp.bfloat16):
    result = jax.random.normal(stream_key, shape, jnp.float32) * scale
    if len(shards) > 0:
        result = block_scale(stream_key, shape, shards, -0.22, 0.18) * result
    return jnp.clip(result, min=-limit, max=limit).astype(kind)


def setup_inputs(seed: int = 0) -> dict:
    key_list = jax.random.split(jax.random.key(seed), 17)
    queries = draw_queries(jax.random.fold_in(key_list[16], 71), 0)
    fresh_pair = scatter_about(key_list[1], (REQ, 2, H * HD), 1.0, 6.0, ((0, 32), (2, 8)))
    cache_blocks = draw_cache_blocks(jax.random.fold_in(key_list[16], 71), 0)
    block_table = draw_block_table(jax.random.fold_in(key_list[16], 71), 0)
    lengths = draw_lengths(jax.random.fold_in(key_list[16], 71), 0)
    residual = scatter_about(key_list[5], (REQ, D), 1.0, 6.0, ((0, 32),))
    w_output = scatter_about(key_list[6], (H * HD, D), (H * HD) ** -0.5, 0.125, ((0, 8),))
    norm_gain = jnp.clip(1.0 + 0.1 * jax.random.normal(key_list[7], (D,), jnp.float32), 0.5, 1.5).astype(jnp.bfloat16)
    routes_keys = jax.random.split(jax.random.fold_in(key_list[8], 1), REQ // REQ_DEV)
    routes_turns = jax.random.permutation(jax.random.fold_in(key_list[8], 3), REQ // REQ_DEV)
    routes = jax.vmap(lambda own, number: routed_block(jax.random.fold_in(key_list[8], 2), own, number, REQ_DEV, EXP, TOPK, MOST, 2))(routes_keys, routes_turns).reshape((REQ, TOPK))
    route_gates = jnp.clip(jax.random.uniform(key_list[9], (REQ, TOPK), jnp.float32, 0.1, 0.6), 0.1, 0.6)
    w_gate_up = scatter_about(key_list[10], (EXP, D, 2, FFE), D ** -0.5, 0.125, ((0, 32), (1, 8)))
    w_down = scatter_about(key_list[11], (EXP, FFE, D), FFE ** -0.5, 0.15625, ((0, 32), (2, 8)))
    shared_gate_up = scatter_about(key_list[12], (NSH, D, 2, FFE), D ** -0.5, 0.125, ((1, 8),))
    shared_down = scatter_about(key_list[13], (NSH, FFE, D), FFE ** -0.5, 0.15625, ((2, 8),))
    next_gain = jnp.clip(1.0 + 0.1 * jax.random.normal(key_list[14], (D,), jnp.float32), 0.5, 1.5).astype(jnp.bfloat16)
    w_query_key_value = scatter_about(key_list[15], (D, 3 * H * HD), D ** -0.5, 0.125, ((1, 8),))
    return {"queries": queries, "fresh_pair": fresh_pair, "cache_blocks": cache_blocks, "block_table": block_table, "lengths": lengths, "residual": residual, "w_output": w_output, "norm_gain": norm_gain, "routes": routes, "route_gates": route_gates, "w_gate_up": w_gate_up, "w_down": w_down, "shared_gate_up": shared_gate_up, "shared_down": shared_down, "next_gain": next_gain, "w_query_key_value": w_query_key_value}


epsilon = 1e-06
floor_score = -1e+30

def norm_rows(values, gain):
    mean_square = lax.optimization_barrier(jnp.mean(values * values, axis=-1, keepdims=True))
    return values * lax.rsqrt(mean_square + epsilon) * gain.astype(jnp.float32)

def block_owners(block_table):
    req_total, list_len = block_table.shape
    row_ids = jnp.broadcast_to(jnp.arange(req_total, dtype=jnp.int32)[:, None], (req_total, list_len)).reshape(-1)
    col_ids = jnp.broadcast_to(jnp.arange(list_len, dtype=jnp.int32)[None, :], (req_total, list_len)).reshape(-1)
    target = jnp.where(block_table >= 0, block_table, NBLK).reshape(-1).astype(jnp.int32)
    owners = jnp.full((NBLK + 1,), req_total, jnp.int32).at[target].set(row_ids)[:NBLK]
    ranks = jnp.zeros((NBLK + 1,), jnp.int32).at[target].set(col_ids)[:NBLK]
    return (owners, ranks)

def attention(queries, fresh_pair, cache_blocks, block_table, lengths):
    owners, ranks = block_owners(block_table)
    score_scale = 1.0 / math.sqrt(HD)
    query_rows = queries.astype(jnp.float32).reshape(REQ, H, HD)
    fresh_keys = fresh_pair[:, 0].astype(jnp.float32).reshape(REQ, H, HD)
    fresh_values = fresh_pair[:, 1].astype(jnp.float32).reshape(REQ, H, HD)
    fresh_score = lax.optimization_barrier(jnp.sum(query_rows * fresh_keys, axis=-1)) * score_scale
    safe_owner = jnp.minimum(owners, REQ - 1).astype(jnp.int32)
    token_pos = ranks[:, None] * BS + jnp.arange(BS, dtype=jnp.int32)[None, :]
    usable = jnp.logical_and(owners[:, None] < REQ, token_pos < lengths[safe_owner][:, None])
    grouped = cache_blocks.reshape(N_POOL, BLK_DEV, 2, BS, H, HD)
    owner_groups = safe_owner.reshape(N_POOL, BLK_DEV)
    usable_groups = usable.reshape(N_POOL, BLK_DEV, BS)

    def group_scores(blocks, owner_ids, alive):
        picked = query_rows[owner_ids]
        raw = jnp.einsum('bjhd,bhd->bjh', blocks[:, 0].astype(jnp.float32), picked) * score_scale
        return jnp.where(alive[:, :, None], raw, floor_score)

    def group_max(args):
        return lax.optimization_barrier(jnp.max(group_scores(args[0], args[1], args[2]), axis=1))
    block_max = lax.map(group_max, (grouped, owner_groups, usable_groups)).reshape(NBLK, H)
    is_owner = owners[None, :] == jnp.arange(REQ, dtype=jnp.int32)[:, None]
    top = lax.optimization_barrier(jnp.max(jnp.where(is_owner[:, :, None], block_max[None], floor_score), axis=1))
    top = jnp.maximum(top, fresh_score)
    top_groups = top[owner_groups]

    def group_sums(args):
        blocks, owner_ids, alive, shift = args
        weights_exp = jnp.where(alive[:, :, None], jnp.exp(group_scores(blocks, owner_ids, alive) - shift[:, None, :]), 0.0)
        block_total = lax.optimization_barrier(jnp.sum(weights_exp, axis=1))
        block_acc = jnp.einsum('bjh,bjhd->bhd', weights_exp, blocks[:, 1].astype(jnp.float32))
        return (block_total, block_acc)
    block_total, block_acc = lax.map(group_sums, (grouped, owner_groups, usable_groups, top_groups))
    segment = jnp.where(owners < REQ, owners, REQ).astype(jnp.int32)
    fresh_weight = jnp.exp(fresh_score - top)
    denom = jax.ops.segment_sum(block_total.reshape(NBLK, H), segment, num_segments=REQ + 1)[:REQ] + fresh_weight
    numer = jax.ops.segment_sum(block_acc.reshape(NBLK, H, HD), segment, num_segments=REQ + 1)[:REQ]
    numer = numer + fresh_weight[:, :, None] * fresh_values
    return (numer / denom[:, :, None]).astype(jnp.bfloat16).reshape(REQ, H * HD)

def routed_terms(normed, routes, route_gates, w_gate_up, w_down):

    def one_token(args):
        row, chosen, weights = args
        preact = jnp.einsum('d,kdcf->kcf', row.astype(jnp.float32), w_gate_up[chosen].astype(jnp.float32))
        hidden = (jax.nn.silu(preact[:, 0]) * preact[:, 1]).astype(jnp.bfloat16)
        expert_out = jnp.einsum('kf,kfd->kd', hidden.astype(jnp.float32), w_down[chosen].astype(jnp.float32))
        return lax.optimization_barrier(jnp.sum(expert_out * weights[:, None], axis=0))
    return lax.map(one_token, (normed, routes, route_gates))

def shared_terms(normed, shared_gate_up, shared_down):
    preact = jnp.einsum('td,sdcf->tscf', normed.astype(jnp.float32), shared_gate_up.astype(jnp.float32))
    shared_hidden = (jax.nn.silu(preact[:, :, 0]) * preact[:, :, 1]).astype(jnp.bfloat16)
    return jnp.einsum('tsf,sfd->td', shared_hidden.astype(jnp.float32), shared_down.astype(jnp.float32))

def reference(queries, fresh_pair, cache_blocks, block_table, lengths, residual, w_output, norm_gain, routes, route_gates, w_gate_up, w_down, shared_gate_up, shared_down, next_gain, w_query_key_value):
    attended = attention(queries, fresh_pair, cache_blocks, block_table, lengths)
    after_attention = residual.astype(jnp.float32) + jnp.dot(attended, w_output, preferred_element_type=jnp.float32)
    normed = norm_rows(after_attention, norm_gain).astype(jnp.bfloat16)
    routed = routed_terms(normed, routes, route_gates, w_gate_up, w_down)
    shared_out = shared_terms(normed, shared_gate_up, shared_down)
    after_ffn = after_attention + routed + shared_out
    next_normed = norm_rows(after_ffn, next_gain).astype(jnp.bfloat16)
    projected = jnp.dot(next_normed, w_query_key_value, preferred_element_type=jnp.float32).astype(jnp.bfloat16)
    return (after_ffn.astype(jnp.bfloat16), projected)
```

```python
import math

import jax
import jax.numpy as jnp
from jax import lax
from jax.experimental import pallas as pl
from jax.experimental.pallas import tpu as pltpu
from jax.sharding import PartitionSpec as P

HD = 128
NP = 32
NH = 8
T = 10
TP = 16
CW = 256
FFE = 1408
BLK = 36
BP = 40
BS = 64
TOK = BLK * BS
EW = 2 * FFE + 128 + 512
FW = FFE + 256
epsilon = 1e-06
low = -1e30
f32 = jnp.float32
bf16 = jnp.bfloat16
i32 = jnp.int32
MESH = pl.DeviceIdType.MESH


def iota(shape, dim):
    return lax.broadcasted_iota(i32, shape, dim)


def dot(a, b):
    return jnp.dot(a, b, preferred_element_type=f32)


def dot_t(a, b):
    return lax.dot_general(a, b, (((0,), (0,)), ((), ())), preferred_element_type=f32)


def hot(cond):
    return jnp.where(cond, 1.0, 0.0).astype(bf16)


def kernel(
    small_ref,
    len_ref,
    routes_ref,
    gates_ref,
    table_hbm,
    cache_hbm,
    wout_hbm,
    wgu_hbm,
    wdn_hbm,
    sgu_hbm,
    sdn_hbm,
    wqkv_hbm,
    hid_ref,
    qkv_ref,
    table_v,
    cache_v,
    wout_v,
    wgu_v,
    wdn_v,
    sgu_v,
    sdn_v,
    wqkv_v,
    wgu2,
    sgu2,
    abuf,
    bsend,
    bbuf,
    csend,
    cbuf,
    dsend,
    dbuf,
    esend,
    ebuf,
    fsend,
    fbuf,
    gsend,
    gbuf,
    hsend,
    hbuf,
    lsem,
    ssem,
    rsem,
):
    p = lax.axis_index("pool")
    h = lax.axis_index("head")

    loads = [
        pltpu.make_async_copy(src, dst, lsem.at[n])
        for n, (src, dst) in enumerate(
            [
                (table_hbm, table_v.at[pl.ds(0, 320)]),
                (cache_hbm, cache_v),
                (sgu_hbm, sgu_v),
                (wout_hbm, wout_v),
                (wgu_hbm, wgu_v),
                (wdn_hbm, wdn_v),
                (sdn_hbm, sdn_v),
                (wqkv_hbm, wqkv_v),
            ]
        )
    ]
    for load in loads:
        load.start()

    barrier = pltpu.get_barrier_semaphore()

    def greet_pool(k, carry):
        pl.semaphore_signal(
            barrier, inc=1, device_id={"pool": lax.rem(p + k, NP)}, device_id_type=MESH
        )
        return carry

    def greet_head(k, carry):
        pl.semaphore_signal(
            barrier, inc=1, device_id={"head": lax.rem(h + k, NH)}, device_id_type=MESH
        )
        return carry

    lax.fori_loop(1, NP, greet_pool, 0)
    lax.fori_loop(1, NH, greet_head, 0)

    def send_pool(src, buf, n):
        def one(k, carry):
            j = lax.rem(p + k, NP)
            pltpu.make_async_remote_copy(
                src_ref=src(j),
                dst_ref=buf.at[p],
                send_sem=ssem.at[n],
                recv_sem=rsem.at[n],
                device_id={"pool": j},
                device_id_type=MESH,
            ).start()
            return carry

        lax.fori_loop(1, NP, one, 0)

    def send_head(src, buf, n):
        def one(k, carry):
            j = lax.rem(h + k, NH)
            pltpu.make_async_remote_copy(
                src_ref=src(j),
                dst_ref=buf.at[h],
                send_sem=ssem.at[n],
                recv_sem=rsem.at[n],
                device_id={"head": j},
                device_id_type=MESH,
            ).start()
            return carry

        lax.fori_loop(1, NH, one, 0)

    def wait(buf, sem, n, count):
        view = buf.at[pl.ds(0, count)]
        pltpu.make_async_copy(view, view, sem.at[n]).wait()

    abuf[p] = small_ref[0]
    pl.semaphore_wait(barrier, NP - 1 + NH - 1)
    send_pool(lambda j: small_ref.at[0], abuf, 0)

    table_v[pl.ds(320, 64), :] = jnp.zeros((64, 256), i32)
    loads[0].wait()
    table = table_v[...].astype(f32)
    heads_t = jnp.transpose(table[:, 0:128])
    lane = iota((1, 384), 1)
    real = lane < 320
    blk = iota((BP, 1), 0)
    ids = jnp.where(blk < BLK, blk + BLK * p, -7).astype(f32)
    len_row = jnp.concatenate(
        [len_ref[...].astype(f32), jnp.zeros((1, 64), f32)], axis=1
    )
    hot0 = jnp.where((heads_t[0:1] == ids) & real, 1.0, 0.0)
    hot1 = jnp.where((heads_t[1:2] == ids) & real, 1.0, 0.0)
    is_long = (heads_t[2:3] >= 0.0) & real
    lane_f = lane.astype(f32)
    first = jnp.min(jnp.where(is_long, lane_f, 1e6), axis=1, keepdims=True)
    last = jnp.max(jnp.where(is_long, lane_f, -1.0), axis=1, keepdims=True)
    row_f = iota((384, 1), 0).astype(f32)
    col = iota((1, 256), 1)
    owned = hot0 + hot1
    rank = jnp.sum(hot1, axis=1, keepdims=True)
    for which in (first, last):
        listed = jnp.sum(jnp.where(row_f == which, table, 0.0), axis=0, keepdims=True)
        match = jnp.where((listed == ids) & (col >= 2), 1.0, 0.0)
        found = jnp.max(match, axis=1, keepdims=True)
        rank = rank + jnp.sum(match * col.astype(f32), axis=1, keepdims=True)
        owned = owned + found * jnp.where(lane_f == which, 1.0, 0.0)
    owner_len = jnp.sum(owned * len_row, axis=1, keepdims=True)
    live = jnp.clip(owner_len - BS * rank, 0.0, float(BS))
    r_in = iota((384, 512), 0)
    spread = hot(
        (iota((384, 512), 1) == r_in + 6 * lax.shift_right_logical(r_in * 205, 11))
        & (r_in < 320)
    )
    hot_f = dot(owned.astype(bf16), spread)
    hot_b = hot_f.astype(bf16)
    mine = hot_f > 0.5
    blk_f = blk.astype(f32)
    lead = jnp.min(jnp.where(mine, blk_f, 99.0), axis=0, keepdims=True)
    rep = jnp.max(jnp.where(mine & (lead == blk_f), 1.0, 0.0), axis=1, keepdims=True)
    tok = iota((BP, TOK), 1)
    start = blk * BS
    usable = (tok >= start) & (tok < start + live.astype(i32))

    loads[2].wait()
    for t in range(11):
        sgu2[:, t * 128 : (t + 1) * 128] = sgu_v[0, :, :, t * 128 : (t + 1) * 128].reshape(
            2 * CW, 128
        )
    loads[1].wait()

    wait(abuf, rsem, 0, NP - 1)
    scale = 1.0 / math.sqrt(HD)
    picked = dot(hot_b, abuf[...].reshape(NP * TP, CW)).astype(bf16)
    parts = []
    shifts = []
    totals = []
    for hd in range(2):
        cols = slice(hd * HD, (hd + 1) * HD)
        keys = cache_v[:, 0, :, cols].reshape(TOK, HD)
        scores = (
            lax.dot_general(
                picked[:, cols], keys, (((1,), (1,)), ((), ())), preferred_element_type=f32
            )
            * scale
        )
        scores = jnp.where(usable, scores, low)
        top = jnp.max(scores, axis=1, keepdims=True)
        req_top = jnp.max(jnp.where(mine, top, low), axis=0, keepdims=True)
        shift = jnp.max(jnp.where(mine, req_top, low), axis=1, keepdims=True)
        shift = shift.astype(bf16).astype(f32)
        weights = jnp.where(usable, jnp.exp(scores - shift), 0.0)
        totals.append(jnp.sum(weights, axis=1, keepdims=True))
        shifts.append(shift)
        values = cache_v[:, 1, :, cols].reshape(TOK, HD)
        parts.append(dot(weights.astype(bf16), values))
    lane_b = iota((BP, 128), 1)
    stats = jnp.where(
        lane_b == 0,
        jnp.where(rep > 0.5, shifts[0], 0.0),
        jnp.where(
            lane_b == 1,
            jnp.where(rep > 0.5, shifts[1], 0.0),
            jnp.where(lane_b == 2, totals[0], jnp.where(lane_b == 3, totals[1], 0.0)),
        ),
    )
    message = jnp.concatenate(parts + [stats], axis=1).astype(bf16)
    bsend[...] = dot_t(hot_b, message).astype(bf16).reshape(NP, TP, 384)
    bbuf[p] = bsend[p]
    send_pool(lambda j: bsend.at[j], bbuf, 1)

    own_lane = iota((TP, 320), 1)
    own_row = iota((TP, 320), 0)
    own = (own_lane == own_row + T * p) & (own_row < T)
    row16 = iota((TP, 1), 0)
    lane_e = iota((TP, 128), 1)
    named = jnp.zeros((TP, 128), f32)
    gate = jnp.zeros((TP, 128), f32)
    routes_t = routes_ref[...].astype(f32)
    gates_t = gates_ref[...]
    for k in range(6):
        pick = jnp.sum(jnp.where(own, routes_t[k : k + 1], 0.0), axis=1, keepdims=True)
        pick = jnp.where(row16 < T, pick, -1.0).astype(i32)
        amount = jnp.sum(jnp.where(own, gates_t[k : k + 1], 0.0), axis=1, keepdims=True)
        named = named + jnp.where(lane_e == pick, 1.0, 0.0)
        gate = gate + jnp.where(lane_e == pick, amount, 0.0)
    earlier = hot(iota((TP, TP), 1) < iota((TP, TP), 0))
    order = dot(earlier, named.astype(bf16))
    gate_hi = gate.astype(bf16)
    gate_lo = (gate - gate_hi.astype(f32)).astype(bf16)
    l_d = iota((128, 512), 1)
    exp_d = hot(
        iota((128, 512), 0)
        == 2 * lax.shift_right_logical(l_d, 4) + (lax.shift_right_logical(l_d, 1) & 1)
    )
    table_nr = jnp.concatenate([named, order], axis=0).astype(bf16)
    wide = dot(table_nr, exp_d)
    l16 = iota((TP, 512), 1)
    sel = (wide[0:TP] > 0.5) & (wide[TP:].astype(i32) == (l16 & 1))
    quarter = lax.shift_right_logical(l16, 2) & 3
    sel48 = jnp.concatenate([hot(sel & (quarter == c)) for c in range(3)], axis=0)
    l_g = iota((128, 256), 1)
    exp_g = hot(
        iota((128, 256), 0)
        == 2 * lax.shift_right_logical(l_g, 3) + (lax.shift_right_logical(l_g, 1) & 1)
    )
    wide = dot(jnp.concatenate([table_nr, gate_hi, gate_lo], axis=0), exp_g)
    l8 = iota((TP, 256), 1)
    sel = (wide[0:TP] > 0.5) & (wide[TP : 2 * TP].astype(i32) == (l8 & 1))
    half = lax.shift_right_logical(l8, 2) & 1
    combine = jnp.concatenate(
        [
            jnp.where(sel & (half == c), wide[(2 + part) * TP : (3 + part) * TP], 0.0)
            for c in range(2)
            for part in range(2)
        ],
        axis=0,
    ).astype(bf16)
    loads[4].wait()
    for t in range(11):
        wgu2[0, :, t * 128 : (t + 1) * 128] = wgu_v[0, :, :, t * 128 : (t + 1) * 128].reshape(
            2 * CW, 128
        )
    loads[3].wait()

    q_own = small_ref[0].astype(f32)
    k_own = small_ref[1].astype(f32)
    v_own = small_ref[2].astype(f32)
    wait(bbuf, rsem, 1, NP - 1)
    joined = []
    for hd in range(2):
        cols = slice(hd * HD, (hd + 1) * HD)
        fresh = jnp.sum(q_own[:, cols] * k_own[:, cols], axis=1, keepdims=True) * scale
        tops = bbuf[:, :, 256 + hd : 257 + hd].astype(f32)
        sums = bbuf[:, :, 258 + hd : 259 + hd].astype(f32)
        tops = jnp.where(sums > 0.0, tops, low)
        peak = jnp.maximum(jnp.max(tops, axis=0), fresh)
        share = jnp.exp(tops - peak[None])
        fresh_w = jnp.exp(fresh - peak)
        denom = jnp.sum(share * sums, axis=0) + fresh_w
        numer = jnp.sum(share * bbuf[:, :, cols].astype(f32), axis=0) + fresh_w * v_own[:, cols]
        joined.append(numer / denom)
    attended = jnp.concatenate(joined, axis=1).astype(bf16)
    for j in range(NH):
        csend[j] = dot(attended, wout_v[:, j * CW : (j + 1) * CW]).astype(bf16)
    cbuf[h] = csend[h]
    send_head(lambda j: csend.at[j], cbuf, 2)

    for t in range(6):
        wgu2[1, :, t * 128 : (t + 1) * 128] = wgu_v[1, :, :, t * 128 : (t + 1) * 128].reshape(
            2 * CW, 128
        )

    wait(cbuf, rsem, 2, NH - 1)
    after = small_ref[3].astype(f32)
    for j in range(NH):
        after = after + cbuf[j].astype(f32)
    gains = small_ref[4].astype(f32)
    scaled = (after * gains[0:1]).astype(bf16)
    square = jnp.sum(after * after, axis=1, keepdims=True)
    square_hi = square.astype(bf16).astype(f32)
    lane_t = iota((TP, 128), 1)
    squares = jnp.where(lane_t == 0, square_hi, jnp.where(lane_t == 1, square - square_hi, 0.0))
    rows48 = jnp.concatenate([scaled[:, 0:128], scaled[:, 128:256], squares.astype(bf16)], axis=0)
    dsend[...] = dot_t(sel48, rows48).astype(bf16).reshape(NP, TP, 128)
    dbuf[p] = dsend[p]
    send_pool(lambda j: dsend.at[j], dbuf, 3)

    d_in = iota((CW, 2 * CW), 0)
    d_out = iota((CW, 2 * CW), 1)
    to_gate = hot(d_out == 2 * d_in)
    to_up = hot(d_out == 2 * d_in + 1)
    spread_own = jnp.concatenate([dot(scaled, to_gate), dot(scaled, to_up)], axis=0).astype(bf16)
    shared = dot(spread_own, sgu2[...]).astype(bf16)
    for j in range(NH):
        width = min(CW, max(0, FFE - j * CW))
        base = 2 * FFE + 128
        for c in range(2):
            at = base + c * CW
            if width > 0:
                esend[j, :, at : at + width] = shared[
                    c * TP : (c + 1) * TP, j * CW : j * CW + width
                ]
            if width < CW:
                esend[j, :, at + width : at + CW] = jnp.zeros((TP, CW - width), bf16)
    for t in range(6, 11):
        wgu2[1, :, t * 128 : (t + 1) * 128] = wgu_v[1, :, :, t * 128 : (t + 1) * 128].reshape(
            2 * CW, 128
        )
    slot = iota((128, 512), 0)
    from_row = (
        (lax.shift_right_logical(slot, 1) & 31) * TP
        + lax.shift_right_logical(slot, 6) * 2
        + (slot & 1)
    )
    source = iota((128, 512), 1)
    gathers = [hot(source == from_row + 4 * c) for c in range(3)]

    wait(dbuf, rsem, 3, NP - 1)
    arrived = dbuf[...].reshape(NP * TP, 128)
    rows = jnp.concatenate([dot(gathers[0], arrived), dot(gathers[1], arrived)], axis=1).astype(bf16)
    row_squares = dot(gathers[2], arrived)
    for_gate = dot(rows, to_gate).astype(bf16)
    for_up = dot(rows, to_up).astype(bf16)
    own_squares = pltpu.roll(squares, 2, 1)
    for j in range(NH):
        esend[j, :, 2 * FFE : 2 * FFE + 128] = (
            row_squares[j * TP : (j + 1) * TP] + own_squares
        ).astype(bf16)
    for e in range(2):
        both = jnp.concatenate(
            [for_gate[e * 64 : (e + 1) * 64], for_up[e * 64 : (e + 1) * 64]], axis=0
        )
        partial = dot(both, wgu2[e]).astype(bf16)
        for j in range(4):
            for c in range(2):
                esend[4 * e + j, :, c * FFE : (c + 1) * FFE] = partial[
                    c * 64 + j * TP : c * 64 + (j + 1) * TP
                ]
    ebuf[h] = esend[h]
    send_head(lambda j: esend.at[j], ebuf, 4)

    wait(ebuf, rsem, 4, NH - 1)
    total = ebuf[0].astype(f32)
    for j in range(1, NH):
        total = total + ebuf[j].astype(f32)
    ss = total[:, 2 * FFE : 2 * FFE + 128]
    r_row = lax.rsqrt((ss[:, 0:1] + ss[:, 1:2]) * (1.0 / 2048) + epsilon)
    r_own = lax.rsqrt((ss[:, 2:3] + ss[:, 3:4]) * (1.0 / 2048) + epsilon)
    g = total[:, 0:FFE] * r_row
    u = total[:, FFE : 2 * FFE] * r_row
    fsend[:, 0:FFE] = (g / (1.0 + jnp.exp(-g)) * u).astype(bf16)
    base = 2 * FFE + 128
    g = total[:, base : base + CW] * r_own
    u = total[:, base + CW : base + 2 * CW] * r_own
    fsend[:, FFE:] = (g / (1.0 + jnp.exp(-g)) * u).astype(bf16)
    fbuf[h] = fsend[...]
    send_head(lambda j: fsend, fbuf, 5)
    loads[5].wait()
    loads[6].wait()
    loads[7].wait()
    back = iota((256, 256), 0)
    kk = iota((256, 256), 1)
    slot_of = (
        (lax.shift_right_logical(back, 1) & 1) * 64
        + lax.shift_right_logical(back, 3) * 2
        + (back & 1)
        + (lax.shift_right_logical(back, 2) & 1) * 128
    )
    returns = hot(kk == slot_of)

    wait(fbuf, rsem, 5, NH - 1)
    outs = [
        dot(fbuf[4 * e : 4 * e + 4, :, 0:FFE].reshape(64, FFE), wdn_v[e]).astype(bf16)
        for e in range(2)
    ]
    stacked = jnp.concatenate(
        [outs[0][:, 0:128], outs[1][:, 0:128], outs[0][:, 128:256], outs[1][:, 128:256]], axis=0
    )
    gsend[...] = dot(returns, stacked).reshape(NP, 8, 128)
    gbuf[p] = gsend[p]
    send_pool(lambda j: gsend.at[j], gbuf, 6)
    for j in range(6):
        width = min(CW, FFE - j * CW)
        after = after + dot(fbuf[j, :, FFE : FFE + width], sdn_v[0, j * CW : j * CW + width, :])
    wait(gbuf, rsem, 6, NP - 1)
    routed = dot(combine, gbuf[...].reshape(NP * 8, 128).astype(bf16))
    routed = jnp.concatenate(
        [routed[0:TP] + routed[TP : 2 * TP], routed[2 * TP : 3 * TP] + routed[3 * TP :]], axis=1
    )
    hsend[...] = (after + routed).astype(bf16)
    hbuf[h] = hsend[...]
    send_head(lambda j: hsend, hbuf, 7)

    wait(hbuf, rsem, 7, NH - 1)
    mean = jnp.zeros((TP, 1), f32)
    for j in range(NH):
        piece = hbuf[j].astype(f32)
        hid_ref[:, j * CW : (j + 1) * CW] = hbuf[j][0:T]
        mean = mean + jnp.sum(piece * piece, axis=1, keepdims=True)
    r_next = lax.rsqrt(mean * (1.0 / 2048) + epsilon)
    projected = jnp.zeros((TP, 768), f32)
    for j in range(NH):
        piece = (hbuf[j].astype(f32) * r_next * gains[8 + j : 9 + j]).astype(bf16)
        projected = projected + dot(piece, wqkv_v[j * CW : (j + 1) * CW, :])
    qkv_ref[...] = projected[0:T].astype(bf16)

    wait(abuf, ssem, 0, NP - 1)
    wait(bbuf, ssem, 1, NP - 1)
    wait(cbuf, ssem, 2, NH - 1)
    wait(dbuf, ssem, 3, NP - 1)
    wait(ebuf, ssem, 4, NH - 1)
    wait(fbuf, ssem, 5, NH - 1)
    wait(gbuf, ssem, 6, NP - 1)
    wait(hbuf, ssem, 7, NH - 1)


def per_device(
    queries,
    fresh_pair,
    cache_blocks,
    block_table,
    lengths,
    residual,
    w_output,
    norm_gain,
    routes,
    route_gates,
    w_gate_up,
    w_down,
    shared_gate_up,
    shared_down,
    next_gain,
    w_query_key_value,
):
    start = lax.axis_index("head") * CW
    pad = ((0, TP - T), (0, 0))
    small = jnp.concatenate(
        [
            jnp.pad(queries, pad),
            jnp.pad(fresh_pair[:, 0], pad),
            jnp.pad(fresh_pair[:, 1], pad),
            jnp.pad(lax.dynamic_slice_in_dim(residual, start, CW, 1), pad),
            jnp.pad(lax.dynamic_slice_in_dim(norm_gain, start, CW, 0)[None], ((0, 7), (0, 0))),
            next_gain.reshape(NH, CW),
        ],
        axis=0,
    ).reshape(5, TP, CW)
    vmem = pl.BlockSpec(memory_space=pltpu.VMEM)
    hbm = pl.BlockSpec(memory_space=pl.ANY)
    return pl.pallas_call(
        kernel,
        out_shape=(
            jax.ShapeDtypeStruct((T, 2048), bf16),
            jax.ShapeDtypeStruct((T, 768), bf16),
        ),
        in_specs=[vmem] * 4 + [hbm] * 8,
        out_specs=(vmem, vmem),
        scratch_shapes=[
            pltpu.VMEM((384, 256), i32),
            pltpu.VMEM((BLK, 2, BS, CW), bf16),
            pltpu.VMEM((CW, 2048), bf16),
            pltpu.VMEM((2, CW, 2, FFE), bf16),
            pltpu.VMEM((2, FFE, CW), bf16),
            pltpu.VMEM((1, CW, 2, FFE), bf16),
            pltpu.VMEM((1, FFE, CW), bf16),
            pltpu.VMEM((2048, 768), bf16),
            pltpu.VMEM((2, 2 * CW, FFE), bf16),
            pltpu.VMEM((2 * CW, FFE), bf16),
            pltpu.VMEM((NP, TP, CW), bf16),
            pltpu.VMEM((NP, TP, 384), bf16),
            pltpu.VMEM((NP, TP, 384), bf16),
            pltpu.VMEM((NH, TP, CW), bf16),
            pltpu.VMEM((NH, TP, CW), bf16),
            pltpu.VMEM((NP, TP, 128), bf16),
            pltpu.VMEM((NP, TP, 128), bf16),
            pltpu.VMEM((NH, TP, EW), bf16),
            pltpu.VMEM((NH, TP, EW), bf16),
            pltpu.VMEM((TP, FW), bf16),
            pltpu.VMEM((NH, TP, FW), bf16),
            pltpu.VMEM((NP, 8, 128), f32),
            pltpu.VMEM((NP, 8, 128), f32),
            pltpu.VMEM((TP, CW), bf16),
            pltpu.VMEM((NH, TP, CW), bf16),
            pltpu.SemaphoreType.DMA((8,)),
            pltpu.SemaphoreType.DMA((8,)),
            pltpu.SemaphoreType.DMA((8,)),
        ],
        compiler_params=pltpu.CompilerParams(
            collective_id=0, has_side_effects=True, vmem_limit_bytes=56 << 20
        ),
    )(
        small,
        lengths.reshape(1, 320),
        routes.T,
        route_gates.T,
        block_table,
        cache_blocks,
        w_output,
        w_gate_up,
        w_down,
        shared_gate_up,
        shared_down,
        w_query_key_value,
    )


def solution(mesh):
    in_specs = (
        P("pool", "head"),
        P("pool", None, "head"),
        P("pool", None, None, "head"),
        P(),
        P(),
        P("pool", None),
        P("head", None),
        P(),
        P(),
        P(),
        P("pool", "head", None, None),
        P("pool", None, "head"),
        P(None, "head", None, None),
        P(None, None, "head"),
        P(),
        P(None, "head"),
    )
    out_specs = (P("pool", None), P("pool", "head"))
    return jax.shard_map(
        per_device, mesh=mesh, in_specs=in_specs, out_specs=out_specs, check_vma=False
    )
```

```python
import math

import jax
import jax.numpy as jnp
from jax import lax
from jax.experimental import pallas as pl
from jax.experimental.pallas import tpu as pltpu
from jax.sharding import PartitionSpec as P

HD = 128
NP = 32
NH = 8
T = 10
TP = 16
CW = 256
FFE = 1408
BLK = 36
BP = 40
BS = 64
TOK = BLK * BS
EW = 2 * FFE + 128 + 512
FW = FFE + 256
epsilon = 1e-06
low = -1e30
f32 = jnp.float32
bf16 = jnp.bfloat16
i32 = jnp.int32
MESH = pl.DeviceIdType.MESH


def iota(shape, dim):
    return lax.broadcasted_iota(i32, shape, dim)


def dot(a, b):
    return jnp.dot(a, b, preferred_element_type=f32)


def dot_t(a, b):
    return lax.dot_general(a, b, (((0,), (0,)), ((), ())), preferred_element_type=f32)


def hot(cond):
    return jnp.where(cond, 1.0, 0.0).astype(bf16)


def kernel(
    queries_hbm,
    fresh_hbm,
    residual_hbm,
    gain_hbm,
    next_gain_hbm,
    len_hbm,
    routes_hbm,
    gates_hbm,
    table_hbm,
    cache_hbm,
    wout_hbm,
    wgu_hbm,
    wdn_hbm,
    sgu_hbm,
    sdn_hbm,
    wqkv_hbm,
    hid_ref,
    qkv_ref,
    queries_v,
    fresh_v,
    residual_v,
    gain_v,
    next_gain_v,
    len_v,
    routes_v,
    gates_v,
    table_v,
    cache_v,
    wout_v,
    wgu_v,
    wdn_v,
    sgu_v,
    sdn_v,
    wqkv_v,
    wgu2,
    sgu2,
    abuf,
    bsend,
    bbuf,
    csend,
    cbuf,
    dsend,
    dbuf,
    esend,
    edown,
    eup,
    fbuf,
    gsend,
    gbuf,
    hbuf,
    lsem,
    ssem,
    rsem,
    essem,
    ersem,
    fssem,
    frsem,
):
    p = lax.axis_index("pool")
    h = lax.axis_index("head")

    loads = {
        name: pltpu.make_async_copy(src, dst, lsem.at[n])
        for n, (name, src, dst) in enumerate(
            [
                ("queries", queries_hbm, queries_v),
                ("table", table_hbm, table_v.at[pl.ds(0, 320)]),
                ("len", len_hbm, len_v),
                ("cache", cache_hbm, cache_v),
                ("routes", routes_hbm, routes_v),
                ("gates", gates_hbm, gates_v),
                ("fresh", fresh_hbm, fresh_v),
                ("sgu", sgu_hbm, sgu_v),
                ("wgu", wgu_hbm, wgu_v),
                ("wout", wout_hbm, wout_v),
                ("residual", residual_hbm, residual_v),
                ("gain", gain_hbm, gain_v),
                ("wdn", wdn_hbm, wdn_v),
                ("sdn", sdn_hbm, sdn_v),
                ("next_gain", next_gain_hbm, next_gain_v),
                ("wqkv", wqkv_hbm, wqkv_v),
            ]
        )
    }
    loads["queries"].start()

    barrier = pltpu.get_barrier_semaphore()

    def greet_pool(k, carry):
        pl.semaphore_signal(
            barrier, inc=1, device_id={"pool": lax.rem(p + k, NP)}, device_id_type=MESH
        )
        return carry

    def greet_head(k, carry):
        pl.semaphore_signal(
            barrier, inc=1, device_id={"head": lax.rem(h + k, NH)}, device_id_type=MESH
        )
        return carry

    lax.fori_loop(1, NP, greet_pool, 0)
    lax.fori_loop(1, NH, greet_head, 0)
    for name in ("table", "len", "cache"):
        loads[name].start()

    waited = set()
    pending = []

    def arrive(*names):
        for name in names:
            loads[name].wait()
            waited.add(name)


    def send_pool(src, buf, n):
        def one(k, carry):
            j = lax.rem(p + k, NP)
            pltpu.make_async_remote_copy(
                src_ref=src(j),
                dst_ref=buf.at[p],
                send_sem=ssem.at[n],
                recv_sem=rsem.at[n],
                device_id={"pool": j},
                device_id_type=MESH,
            ).start()
            return carry

        lax.fori_loop(1, NP, one, 0)
        pending.append(lambda: wait(buf, ssem, n, NP - 1))

    def send_head(src, buf, n):
        def one(k, carry):
            j = lax.rem(h + k, NH)
            pltpu.make_async_remote_copy(
                src_ref=src(j),
                dst_ref=buf.at[h],
                send_sem=ssem.at[n],
                recv_sem=rsem.at[n],
                device_id={"head": j},
                device_id_type=MESH,
            ).start()
            return carry

        lax.fori_loop(1, NH, one, 0)
        pending.append(lambda: wait(buf, ssem, n, NH - 1))

    def wait(buf, sem, n, count):
        view = buf.at[pl.ds(0, count)]
        pltpu.make_async_copy(view, view, sem.at[n]).wait()

    arrive("queries")
    rows_pad = jnp.zeros((TP - T, CW), f32)
    q_own = jnp.concatenate([queries_v[...].astype(f32), rows_pad], axis=0)
    abuf[p] = q_own.astype(bf16)
    pl.semaphore_wait(barrier, NP - 1 + NH - 1)
    send_pool(lambda j: abuf.at[p], abuf, 0)
    for name in loads:
        if name not in ("queries", "table", "len", "cache"):
            loads[name].start()

    table_v[pl.ds(320, 64), :] = jnp.zeros((64, 256), i32)
    arrive("table", "len")
    table = table_v[...].astype(f32)
    heads_t = jnp.transpose(table[:, 0:128])
    lane = iota((1, 384), 1)
    real = lane < 320
    blk = iota((BP, 1), 0)
    ids = jnp.where(blk < BLK, blk + BLK * p, -7).astype(f32)
    len_row = jnp.concatenate(
        [len_v[...].reshape(1, 320).astype(f32), jnp.zeros((1, 64), f32)], axis=1
    )
    hot0 = jnp.where((heads_t[0:1] == ids) & real, 1.0, 0.0)
    hot1 = jnp.where((heads_t[1:2] == ids) & real, 1.0, 0.0)
    is_long = (heads_t[2:3] >= 0.0) & real
    lane_f = lane.astype(f32)
    first = jnp.min(jnp.where(is_long, lane_f, 1e6), axis=1, keepdims=True)
    last = jnp.max(jnp.where(is_long, lane_f, -1.0), axis=1, keepdims=True)
    row_f = iota((384, 1), 0).astype(f32)
    col = iota((1, 256), 1)
    owned = hot0 + hot1
    rank = jnp.sum(hot1, axis=1, keepdims=True)
    for which in (first, last):
        listed = jnp.sum(jnp.where(row_f == which, table, 0.0), axis=0, keepdims=True)
        match = jnp.where((listed == ids) & (col >= 2), 1.0, 0.0)
        found = jnp.max(match, axis=1, keepdims=True)
        rank = rank + jnp.sum(match * col.astype(f32), axis=1, keepdims=True)
        owned = owned + found * jnp.where(lane_f == which, 1.0, 0.0)
    owner_len = jnp.sum(owned * len_row, axis=1, keepdims=True)
    live = jnp.clip(owner_len - BS * rank, 0.0, float(BS))
    r_in = iota((384, 512), 0)
    spread = hot(
        (iota((384, 512), 1) == r_in + 6 * lax.shift_right_logical(r_in * 205, 11))
        & (r_in < 320)
    )
    hot_f = dot(owned.astype(bf16), spread)
    hot_b = hot_f.astype(bf16)
    mine = hot_f > 0.5
    blk_f = blk.astype(f32)
    lead = jnp.min(jnp.where(mine, blk_f, 99.0), axis=0, keepdims=True)
    rep = jnp.max(jnp.where(mine & (lead == blk_f), 1.0, 0.0), axis=1, keepdims=True)
    tok = iota((BP, TOK), 1)
    start = blk * BS
    usable = (tok >= start) & (tok < start + live.astype(i32))

    arrive("sgu")
    for t in range(11):
        sgu2[:, t * 128 : (t + 1) * 128] = sgu_v[0, :, :, t * 128 : (t + 1) * 128].reshape(
            2 * CW, 128
        )
    arrive("cache")

    wait(abuf, rsem, 0, NP - 1)
    scale = 1.0 / math.sqrt(HD)
    picked = dot(hot_b, abuf[...].reshape(NP * TP, CW)).astype(bf16)
    parts = []
    shifts = []
    totals = []
    for hd in range(2):
        cols = slice(hd * HD, (hd + 1) * HD)
        keys = cache_v[:, 0, :, cols].reshape(TOK, HD)
        scores = (
            lax.dot_general(
                picked[:, cols], keys, (((1,), (1,)), ((), ())), preferred_element_type=f32
            )
            * scale
        )
        scores = jnp.where(usable, scores, low)
        top = jnp.max(scores, axis=1, keepdims=True)
        req_top = jnp.max(jnp.where(mine, top, low), axis=0, keepdims=True)
        shift = jnp.max(jnp.where(mine, req_top, low), axis=1, keepdims=True)
        shift = shift.astype(bf16).astype(f32)
        weights = jnp.where(usable, jnp.exp(scores - shift), 0.0)
        totals.append(jnp.sum(weights, axis=1, keepdims=True))
        shifts.append(shift)
        values = cache_v[:, 1, :, cols].reshape(TOK, HD)
        parts.append(dot(weights.astype(bf16), values))
    lane_b = iota((BP, 128), 1)
    stats = jnp.where(
        lane_b == 0,
        jnp.where(rep > 0.5, shifts[0], 0.0),
        jnp.where(
            lane_b == 1,
            jnp.where(rep > 0.5, shifts[1], 0.0),
            jnp.where(lane_b == 2, totals[0], jnp.where(lane_b == 3, totals[1], 0.0)),
        ),
    )
    message = jnp.concatenate(parts + [stats], axis=1).astype(bf16)
    bsend[...] = dot_t(hot_b, message).astype(bf16).reshape(NP, TP, 384)
    bbuf[p] = bsend[p]
    send_pool(lambda j: bsend.at[j], bbuf, 1)

    arrive("routes", "gates")
    own_lane = iota((TP, 320), 1)
    own_row = iota((TP, 320), 0)
    own = (own_lane == own_row + T * p) & (own_row < T)
    row16 = iota((TP, 1), 0)
    lane_e = iota((TP, 128), 1)
    named = jnp.zeros((TP, 128), f32)
    gate = jnp.zeros((TP, 128), f32)
    routes_t = routes_v[...].astype(f32)
    gates_t = gates_v[...]
    for k in range(6):
        pick = jnp.sum(jnp.where(own, routes_t[k : k + 1], 0.0), axis=1, keepdims=True)
        pick = jnp.where(row16 < T, pick, -1.0).astype(i32)
        amount = jnp.sum(jnp.where(own, gates_t[k : k + 1], 0.0), axis=1, keepdims=True)
        named = named + jnp.where(lane_e == pick, 1.0, 0.0)
        gate = gate + jnp.where(lane_e == pick, amount, 0.0)
    earlier = hot(iota((TP, TP), 1) < iota((TP, TP), 0))
    order = dot(earlier, named.astype(bf16))
    gate_hi = gate.astype(bf16)
    gate_lo = (gate - gate_hi.astype(f32)).astype(bf16)
    l_d = iota((128, 512), 1)
    exp_d = hot(
        iota((128, 512), 0)
        == 2 * lax.shift_right_logical(l_d, 4) + (lax.shift_right_logical(l_d, 1) & 1)
    )
    table_nr = jnp.concatenate([named, order], axis=0).astype(bf16)
    wide = dot(table_nr, exp_d)
    l16 = iota((TP, 512), 1)
    sel = (wide[0:TP] > 0.5) & (wide[TP:].astype(i32) == (l16 & 1))
    quarter = lax.shift_right_logical(l16, 2) & 3
    sel48 = jnp.concatenate([hot(sel & (quarter == c)) for c in range(3)], axis=0)
    l_g = iota((128, 256), 1)
    exp_g = hot(
        iota((128, 256), 0)
        == 2 * lax.shift_right_logical(l_g, 3) + (lax.shift_right_logical(l_g, 1) & 1)
    )
    wide = dot(jnp.concatenate([table_nr, gate_hi, gate_lo], axis=0), exp_g)
    l8 = iota((TP, 256), 1)
    sel = (wide[0:TP] > 0.5) & (wide[TP : 2 * TP].astype(i32) == (l8 & 1))
    half = lax.shift_right_logical(l8, 2) & 1
    combine = jnp.concatenate(
        [
            jnp.where(sel & (half == c), wide[(2 + part) * TP : (3 + part) * TP], 0.0)
            for c in range(2)
            for part in range(2)
        ],
        axis=0,
    ).astype(bf16)
    arrive("wgu")
    for t in range(11):
        wgu2[0, :, t * 128 : (t + 1) * 128] = wgu_v[0, :, :, t * 128 : (t + 1) * 128].reshape(
            2 * CW, 128
        )
    arrive("wout", "fresh", "residual", "gain")

    k_own = jnp.concatenate([fresh_v[:, 0, :].astype(f32), rows_pad], axis=0)
    v_own = jnp.concatenate([fresh_v[:, 1, :].astype(f32), rows_pad], axis=0)
    wait(bbuf, rsem, 1, NP - 1)
    joined = []
    for hd in range(2):
        cols = slice(hd * HD, (hd + 1) * HD)
        fresh = jnp.sum(q_own[:, cols] * k_own[:, cols], axis=1, keepdims=True) * scale
        tops = bbuf[:, :, 256 + hd : 257 + hd].astype(f32)
        sums = bbuf[:, :, 258 + hd : 259 + hd].astype(f32)
        tops = jnp.where(sums > 0.0, tops, low)
        peak = jnp.maximum(jnp.max(tops, axis=0), fresh)
        share = jnp.exp(tops - peak[None])
        fresh_w = jnp.exp(fresh - peak)
        denom = jnp.sum(share * sums, axis=0) + fresh_w
        numer = jnp.sum(share * bbuf[:, :, cols].astype(f32), axis=0) + fresh_w * v_own[:, cols]
        joined.append(numer / denom)
    attended = jnp.concatenate(joined, axis=1).astype(bf16)
    for j in range(NH):
        csend[j] = dot(attended, wout_v[:, j * CW : (j + 1) * CW]).astype(bf16)
    cbuf[h] = csend[h]
    send_head(lambda j: csend.at[j], cbuf, 2)

    for t in range(6):
        wgu2[1, :, t * 128 : (t + 1) * 128] = wgu_v[1, :, :, t * 128 : (t + 1) * 128].reshape(
            2 * CW, 128
        )

    wait(cbuf, rsem, 2, NH - 1)
    own_cols = pl.ds(pl.multiple_of(h * CW, CW), CW)
    after = jnp.concatenate([residual_v[:, own_cols].astype(f32), rows_pad], axis=0)
    for j in range(NH):
        after = after + cbuf[j].astype(f32)
    scaled = (after * gain_v[own_cols].astype(f32).reshape(1, CW)).astype(bf16)
    square = jnp.sum(after * after, axis=1, keepdims=True)
    square_hi = square.astype(bf16).astype(f32)
    lane_t = iota((TP, 128), 1)
    squares = jnp.where(lane_t == 0, square_hi, jnp.where(lane_t == 1, square - square_hi, 0.0))
    rows48 = jnp.concatenate([scaled[:, 0:128], scaled[:, 128:256], squares.astype(bf16)], axis=0)
    dsend[...] = dot_t(sel48, rows48).astype(bf16).reshape(NP, TP, 128)
    dbuf[p] = dsend[p]
    send_pool(lambda j: dsend.at[j], dbuf, 3)

    d_in = iota((CW, 2 * CW), 0)
    d_out = iota((CW, 2 * CW), 1)
    to_gate = hot(d_out == 2 * d_in)
    to_up = hot(d_out == 2 * d_in + 1)
    spread_own = jnp.concatenate([dot(scaled, to_gate), dot(scaled, to_up)], axis=0).astype(bf16)
    shared = dot(spread_own, sgu2[...]).astype(bf16)
    for j in range(NH):
        width = min(CW, max(0, FFE - j * CW))
        base = 2 * FFE + 128
        for c in range(2):
            at = base + c * CW
            if width > 0:
                esend[j, :, at : at + width] = shared[
                    c * TP : (c + 1) * TP, j * CW : j * CW + width
                ]
            if width < CW:
                esend[j, :, at + width : at + CW] = jnp.zeros((TP, CW - width), bf16)
    for t in range(6, 11):
        wgu2[1, :, t * 128 : (t + 1) * 128] = wgu_v[1, :, :, t * 128 : (t + 1) * 128].reshape(
            2 * CW, 128
        )
    slot = iota((128, 512), 0)
    from_row = (
        (lax.shift_right_logical(slot, 1) & 31) * TP
        + lax.shift_right_logical(slot, 6) * 2
        + (slot & 1)
    )
    source = iota((128, 512), 1)
    gathers = [hot(source == from_row + 4 * c) for c in range(3)]

    wait(dbuf, rsem, 3, NP - 1)
    arrived = dbuf[...].reshape(NP * TP, 128)
    rows = jnp.concatenate([dot(gathers[0], arrived), dot(gathers[1], arrived)], axis=1).astype(bf16)
    row_squares = dot(gathers[2], arrived)
    for_gate = dot(rows, to_gate).astype(bf16)
    for_up = dot(rows, to_up).astype(bf16)
    own_squares = pltpu.roll(squares, 2, 1)
    for j in range(NH):
        esend[j, :, 2 * FFE : 2 * FFE + 128] = (
            row_squares[j * TP : (j + 1) * TP] + own_squares
        ).astype(bf16)
    for e in range(2):
        both = jnp.concatenate(
            [for_gate[e * 64 : (e + 1) * 64], for_up[e * 64 : (e + 1) * 64]], axis=0
        )
        partial = dot(both, wgu2[e]).astype(bf16)
        for j in range(4):
            for c in range(2):
                esend[4 * e + j, :, c * FFE : (c + 1) * FFE] = partial[
                    c * 64 + j * TP : c * 64 + (j + 1) * TP
                ]
    def ring_copy(src, dst, send_sem, recv_sem, to):
        return pltpu.make_async_remote_copy(
            src_ref=src,
            dst_ref=dst,
            send_sem=send_sem,
            recv_sem=recv_sem,
            device_id={"head": to},
            device_id_type=MESH,
        )

    down = lax.rem(h + NH - 1, NH)
    up = lax.rem(h + 1, NH)
    e_parts = [(a * 128, b * 128) for a, b in ((0, 7), (7, 14), (14, 21), (21, 27))]
    sides = ((down, edown, -1), (up, eup, 1))

    def off(by):
        return lax.rem(h + by + NH, NH)

    def e_copy(n, way, chunk, slot, to):
        lo, hi = e_parts[n]
        land = sides[way][1]
        return ring_copy(
            esend.at[chunk, :, pl.ds(lo, hi - lo)],
            land.at[slot, :, pl.ds(lo, hi - lo)],
            essem.at[way, n],
            ersem.at[way, slot, n],
            to,
        )

    def e_take(n, way, slot):
        lo, hi = e_parts[n]
        e_copy(n, way, h, slot, down).wait_recv()
        return sides[way][1][slot, :, lo:hi].astype(f32)

    for n in range(len(e_parts)):
        for way, (_, _, sign) in enumerate(sides):
            if n % 2 == way:
                e_copy(n, way, off(4 * sign), 1, off(2 * sign)).start()
            e_copy(n, way, off(3 * sign), 0, off(sign)).start()
    for n in range(len(e_parts)):
        for way, (_, _, sign) in enumerate(sides):
            e_copy(n, way, off(sign), 2, off(sign)).start()
    for n, (lo, hi) in enumerate(e_parts):
        for way, (_, _, sign) in enumerate(sides):
            chunk = off(2 * sign)
            passed = esend[chunk, :, lo:hi].astype(f32) + e_take(n, way, 0)
            if n % 2 == way:
                passed = passed + e_take(n, way, 1)
            esend[chunk, :, lo:hi] = passed.astype(bf16)
            e_copy(n, way, chunk, 3, chunk).start()

    def e_drain():
        for way, land in enumerate((edown, eup)):
            for n, (lo, hi) in enumerate(e_parts):
                view = land.at[pl.ds(0, 4 if n % 2 == way else 3), :, pl.ds(lo, hi - lo)]
                pltpu.make_async_copy(view, view, essem.at[way, n]).wait()

    pending.append(e_drain)
    pieces = []
    for n, (lo, hi) in enumerate(e_parts):
        piece = esend[h, :, lo:hi].astype(f32)
        for way in range(2):
            piece = piece + e_take(n, way, 2) + e_take(n, way, 3)
        pieces.append(piece)
    total = jnp.concatenate(pieces, axis=1)
    ss = total[:, 2 * FFE : 2 * FFE + 128]
    r_row = lax.rsqrt((ss[:, 0:1] + ss[:, 1:2]) * (1.0 / 2048) + epsilon)
    r_own = lax.rsqrt((ss[:, 2:3] + ss[:, 3:4]) * (1.0 / 2048) + epsilon)
    g = total[:, 0:FFE] * r_row
    u = total[:, FFE : 2 * FFE] * r_row
    fbuf[h, :, 0:FFE] = (g / (1.0 + jnp.exp(-g)) * u).astype(bf16)
    base = 2 * FFE + 128
    g = total[:, base : base + CW] * r_own
    u = total[:, base + CW : base + 2 * CW] * r_own
    fbuf[h, :, FFE:] = (g / (1.0 + jnp.exp(-g)) * u).astype(bf16)
    f_parts = [(0, 7 * 128), (7 * 128, FW)]

    def f_send(n, way, origin, hop):
        lo, hi = f_parts[n]
        sign = sides[way][2]
        view = fbuf.at[off(-sign * origin), :, pl.ds(lo, hi - lo)]
        ring_copy(
            view, view, fssem.at[way, n], frsem.at[way, origin + hop - 1, n], off(sign * hop)
        ).start()

    def f_wait(n, way, origin):
        lo, hi = f_parts[n]
        view = fbuf.at[off(-sides[way][2] * origin), :, pl.ds(lo, hi - lo)]
        ring_copy(
            view, view, fssem.at[way, n], frsem.at[way, origin - 1, n], down
        ).wait_recv()

    for hop in (2, 1):
        for n in range(2):
            for way in range(2):
                f_send(n, way, 0, hop)
    for n in range(2):
        for way in range(2):
            f_wait(n, way, 2)
            if n == way:
                f_send(n, way, 2, 2)
            f_send(n, way, 2, 1)

    def f_drain():
        for way in range(2):
            for n, (lo, hi) in enumerate(f_parts):
                view = fbuf.at[pl.ds(0, 4 if n == way else 3), :, pl.ds(lo, hi - lo)]
                pltpu.make_async_copy(view, view, fssem.at[way, n]).wait()

    pending.append(f_drain)
    arrive("wdn", "sdn", "next_gain", "wqkv")
    back = iota((256, 256), 0)
    kk = iota((256, 256), 1)
    slot_of = (
        (lax.shift_right_logical(back, 1) & 1) * 64
        + lax.shift_right_logical(back, 3) * 2
        + (back & 1)
        + (lax.shift_right_logical(back, 2) & 1) * 128
    )
    returns = hot(kk == slot_of)

    for n in range(2):
        for way in range(2):
            for origin in (1, 3, 4) if n == way else (1, 3):
                f_wait(n, way, origin)
    outs = [
        dot(fbuf[4 * e : 4 * e + 4, :, 0:FFE].reshape(64, FFE), wdn_v[e]).astype(bf16)
        for e in range(2)
    ]
    stacked = jnp.concatenate(
        [outs[0][:, 0:128], outs[1][:, 0:128], outs[0][:, 128:256], outs[1][:, 128:256]], axis=0
    )
    gsend[...] = dot(returns, stacked).reshape(NP, 8, 128)
    gbuf[p] = gsend[p]
    send_pool(lambda j: gsend.at[j], gbuf, 4)
    for j in range(6):
        width = min(CW, FFE - j * CW)
        after = after + dot(fbuf[j, :, FFE : FFE + width], sdn_v[0, j * CW : j * CW + width, :])
    wait(gbuf, rsem, 4, NP - 1)
    routed = dot(combine, gbuf[...].reshape(NP * 8, 128).astype(bf16))
    routed = jnp.concatenate(
        [routed[0:TP] + routed[TP : 2 * TP], routed[2 * TP : 3 * TP] + routed[3 * TP :]], axis=1
    )
    hbuf[h] = (after + routed).astype(bf16)
    send_head(lambda j: hbuf.at[h], hbuf, 5)
    next_gain = next_gain_v[...].astype(f32).reshape(NH, CW)

    wait(hbuf, rsem, 5, NH - 1)
    mean = jnp.zeros((TP, 1), f32)
    for j in range(NH):
        piece = hbuf[j].astype(f32)
        hid_ref[:, j * CW : (j + 1) * CW] = hbuf[j][0:T]
        mean = mean + jnp.sum(piece * piece, axis=1, keepdims=True)
    r_next = lax.rsqrt(mean * (1.0 / 2048) + epsilon)
    projected = jnp.zeros((TP, 768), f32)
    for j in range(NH):
        piece = (hbuf[j].astype(f32) * r_next * next_gain[j : j + 1]).astype(bf16)
        projected = projected + dot(piece, wqkv_v[j * CW : (j + 1) * CW, :])
    qkv_ref[...] = projected[0:T].astype(bf16)

    for finish in pending:
        finish()


def hand_over(hid_in, qkv_in, hid_out, qkv_out, sem):
    copies = [
        pltpu.make_async_copy(hid_in, hid_out, sem.at[0]),
        pltpu.make_async_copy(qkv_in, qkv_out, sem.at[1]),
    ]
    for copy in copies:
        copy.start()
    for copy in copies:
        copy.wait()


def per_device(
    queries,
    fresh_pair,
    cache_blocks,
    block_table,
    lengths,
    residual,
    w_output,
    norm_gain,
    routes,
    route_gates,
    w_gate_up,
    w_down,
    shared_gate_up,
    shared_down,
    next_gain,
    w_query_key_value,
):
    vmem = pl.BlockSpec(memory_space=pltpu.VMEM)
    hbm = pl.BlockSpec(memory_space=pltpu.HBM)
    results = pl.pallas_call(
        kernel,
        out_shape=(
            jax.ShapeDtypeStruct((T, 2048), bf16),
            jax.ShapeDtypeStruct((T, 768), bf16),
        ),
        in_specs=[hbm] * 16,
        out_specs=(vmem, vmem),
        scratch_shapes=[
            pltpu.VMEM((T, CW), bf16),
            pltpu.VMEM((T, 2, CW), bf16),
            pltpu.VMEM((T, 2048), bf16),
            pltpu.VMEM((2048,), bf16),
            pltpu.VMEM((2048,), bf16),
            pltpu.VMEM((320,), i32),
            pltpu.VMEM((6, 320), i32),
            pltpu.VMEM((6, 320), f32),
            pltpu.VMEM((384, 256), i32),
            pltpu.VMEM((BLK, 2, BS, CW), bf16),
            pltpu.VMEM((CW, 2048), bf16),
            pltpu.VMEM((2, CW, 2, FFE), bf16),
            pltpu.VMEM((2, FFE, CW), bf16),
            pltpu.VMEM((1, CW, 2, FFE), bf16),
            pltpu.VMEM((1, FFE, CW), bf16),
            pltpu.VMEM((2048, 768), bf16),
            pltpu.VMEM((2, 2 * CW, FFE), bf16),
            pltpu.VMEM((2 * CW, FFE), bf16),
            pltpu.VMEM((NP, TP, CW), bf16),
            pltpu.VMEM((NP, TP, 384), bf16),
            pltpu.VMEM((NP, TP, 384), bf16),
            pltpu.VMEM((NH, TP, CW), bf16),
            pltpu.VMEM((NH, TP, CW), bf16),
            pltpu.VMEM((NP, TP, 128), bf16),
            pltpu.VMEM((NP, TP, 128), bf16),
            pltpu.VMEM((NH, TP, EW), bf16),
            pltpu.VMEM((4, TP, EW), bf16),
            pltpu.VMEM((4, TP, EW), bf16),
            pltpu.VMEM((NH, TP, FW), bf16),
            pltpu.VMEM((NP, 8, 128), f32),
            pltpu.VMEM((NP, 8, 128), f32),
            pltpu.VMEM((NH, TP, CW), bf16),
            pltpu.SemaphoreType.DMA((16,)),
            pltpu.SemaphoreType.DMA((6,)),
            pltpu.SemaphoreType.DMA((6,)),
            pltpu.SemaphoreType.DMA((2, 4)),
            pltpu.SemaphoreType.DMA((2, 4, 4)),
            pltpu.SemaphoreType.DMA((2, 2)),
            pltpu.SemaphoreType.DMA((2, 4, 2)),
        ],
        compiler_params=pltpu.CompilerParams(
            collective_id=0, has_side_effects=True, vmem_limit_bytes=58 << 20
        ),
    )(
        queries,
        fresh_pair,
        residual,
        norm_gain,
        next_gain,
        lengths,
        routes.T,
        route_gates.T,
        block_table,
        cache_blocks,
        w_output,
        w_gate_up,
        w_down,
        shared_gate_up,
        shared_down,
        w_query_key_value,
    )
    return pl.pallas_call(
        hand_over,
        out_shape=(
            jax.ShapeDtypeStruct((T, 2048), bf16),
            jax.ShapeDtypeStruct((T, 768), bf16),
        ),
        in_specs=[hbm] * 2,
        out_specs=(hbm, hbm),
        scratch_shapes=[pltpu.SemaphoreType.DMA((2,))],
    )(*results)


def solution(mesh):
    in_specs = (
        P("pool", "head"),
        P("pool", None, "head"),
        P("pool", None, None, "head"),
        P(),
        P(),
        P("pool", None),
        P("head", None),
        P(),
        P(),
        P(),
        P("pool", "head", None, None),
        P("pool", None, "head"),
        P(None, "head", None, None),
        P(None, None, "head"),
        P(),
        P(None, "head"),
    )
    out_specs = (P("pool", None), P("pool", "head"))
    return jax.shard_map(
        per_device, mesh=mesh, in_specs=in_specs, out_specs=out_specs, check_vma=False
    )
```

```python
import math

import jax
import jax.numpy as jnp
from jax import lax
from jax.experimental import pallas as pl
from jax.experimental.pallas import tpu as pltpu
from jax.sharding import PartitionSpec as P

HD = 128
NP = 32
NH = 8
T = 10
TP = 16
CW = 256
FFE = 1408
BLK = 36
BP = 40
BS = 64
TOK = BLK * BS
RP = 24
EW = 2 * FFE + 128
SW = 2 * CW + 128
epsilon = 1e-06
low = -1e30
f32 = jnp.float32
bf16 = jnp.bfloat16
i32 = jnp.int32
MESH = pl.DeviceIdType.MESH


def iota(shape, dim):
    return lax.broadcasted_iota(i32, shape, dim)


def dot(a, b):
    return jnp.dot(a, b, preferred_element_type=f32)


def dot_t(a, b):
    return lax.dot_general(a, b, (((0,), (0,)), ((), ())), preferred_element_type=f32)


def hot(cond):
    return jnp.where(cond, 1.0, 0.0).astype(bf16)


def kernel(
    queries_hbm,
    fresh_hbm,
    residual_hbm,
    gain_hbm,
    next_gain_hbm,
    len_hbm,
    routes_hbm,
    gates_hbm,
    table_hbm,
    cache_hbm,
    wout_hbm,
    wgu_hbm,
    wdn_hbm,
    sgu_hbm,
    sdn_hbm,
    wqkv_hbm,
    hid_ref,
    qkv_ref,
    queries_v,
    fresh_v,
    residual_v,
    gain_v,
    next_gain_v,
    len_v,
    routes_v,
    gates_v,
    table_v,
    cache_v,
    wout_v,
    wgu_v,
    wdn_v,
    sgu_v,
    sdn_v,
    wqkv_v,
    wgu2,
    sgu2,
    abuf,
    bsend,
    bbuf,
    csend,
    cbuf,
    dsend,
    dbuf,
    esend,
    edown,
    eup,
    fbuf,
    sbuf,
    ssend,
    tbuf,
    gsend,
    gbuf,
    hbuf,
    lsem,
    ssem,
    rsem,
    essem,
    ersem,
    fssem,
    frsem,
):
    p = lax.axis_index("pool")
    h = lax.axis_index("head")

    loads = {
        name: pltpu.make_async_copy(src, dst, lsem.at[n])
        for n, (name, src, dst) in enumerate(
            [
                ("queries", queries_hbm, queries_v),
                ("table", table_hbm, table_v.at[pl.ds(0, 320)]),
                ("len", len_hbm, len_v),
                ("cache", cache_hbm, cache_v),
                ("routes", routes_hbm, routes_v),
                ("gates", gates_hbm, gates_v),
                ("fresh", fresh_hbm, fresh_v),
                ("sgu", sgu_hbm, sgu_v),
                ("wgu", wgu_hbm, wgu_v),
                ("wout", wout_hbm, wout_v),
                ("residual", residual_hbm, residual_v),
                ("gain", gain_hbm, gain_v),
                ("wdn", wdn_hbm, wdn_v),
                ("sdn", sdn_hbm, sdn_v),
                ("next_gain", next_gain_hbm, next_gain_v),
                ("wqkv", wqkv_hbm, wqkv_v),
            ]
        )
    }
    loads["queries"].start()

    barrier = pltpu.get_barrier_semaphore()

    def greet_pool(k, carry):
        pl.semaphore_signal(
            barrier, inc=1, device_id={"pool": lax.rem(p + k, NP)}, device_id_type=MESH
        )
        return carry

    def greet_head(k, carry):
        pl.semaphore_signal(
            barrier, inc=1, device_id={"head": lax.rem(h + k, NH)}, device_id_type=MESH
        )
        return carry

    lax.fori_loop(1, NP, greet_pool, 0)
    lax.fori_loop(1, NH, greet_head, 0)
    for name in ("table", "len"):
        loads[name].start()

    waited = set()
    pending = []

    def arrive(*names):
        for name in names:
            loads[name].wait()
            waited.add(name)


    def send_pool(src, buf, n):
        def one(k, carry):
            j = lax.rem(p + k, NP)
            pltpu.make_async_remote_copy(
                src_ref=src(j),
                dst_ref=buf.at[p],
                send_sem=ssem.at[n],
                recv_sem=rsem.at[n],
                device_id={"pool": j},
                device_id_type=MESH,
            ).start()
            return carry

        lax.fori_loop(1, NP, one, 0)
        pending.append(lambda: wait(buf, ssem, n, NP - 1))

    def send_head(src, buf, n):
        def one(k, carry):
            j = lax.rem(h + k, NH)
            pltpu.make_async_remote_copy(
                src_ref=src(j),
                dst_ref=buf.at[h],
                send_sem=ssem.at[n],
                recv_sem=rsem.at[n],
                device_id={"head": j},
                device_id_type=MESH,
            ).start()
            return carry

        lax.fori_loop(1, NH, one, 0)
        pending.append(lambda: wait(buf, ssem, n, NH - 1))

    def wait(buf, sem, n, count):
        view = buf.at[pl.ds(0, count)]
        pltpu.make_async_copy(view, view, sem.at[n]).wait()

    arrive("queries")
    rows_pad = jnp.zeros((TP - T, CW), f32)
    q_own = jnp.concatenate([queries_v[...].astype(f32), rows_pad], axis=0)
    abuf[p] = jnp.concatenate(
        [q_own[0:T, 0:HD], q_own[0:T, HD:CW], rows_pad[0:4, 0:HD]], axis=0
    ).astype(bf16)
    pl.semaphore_wait(barrier, NP - 1 + NH - 1)
    send_pool(lambda j: abuf.at[p], abuf, 0)
    for name in loads:
        if name not in ("queries", "table", "len"):
            loads[name].start()

    table_v[pl.ds(320, 64), :] = jnp.zeros((64, 256), i32)
    arrive("table", "len")
    table = table_v[...].astype(f32)
    heads_t = jnp.transpose(table[:, 0:128])
    lane = iota((1, 384), 1)
    real = lane < 320
    blk = iota((BP, 1), 0)
    ids = jnp.where(blk < BLK, blk + BLK * p, -7).astype(f32)
    len_row = jnp.concatenate(
        [len_v[...].reshape(1, 320).astype(f32), jnp.zeros((1, 64), f32)], axis=1
    )
    hot0 = jnp.where((heads_t[0:1] == ids) & real, 1.0, 0.0)
    hot1 = jnp.where((heads_t[1:2] == ids) & real, 1.0, 0.0)
    is_long = (heads_t[2:3] >= 0.0) & real
    lane_f = lane.astype(f32)
    first = jnp.min(jnp.where(is_long, lane_f, 1e6), axis=1, keepdims=True)
    last = jnp.max(jnp.where(is_long, lane_f, -1.0), axis=1, keepdims=True)
    row_f = iota((384, 1), 0).astype(f32)
    col = iota((1, 256), 1)
    owned = hot0 + hot1
    rank = jnp.sum(hot1, axis=1, keepdims=True)
    for which in (first, last):
        listed = jnp.sum(jnp.where(row_f == which, table, 0.0), axis=0, keepdims=True)
        match = jnp.where((listed == ids) & (col >= 2), 1.0, 0.0)
        found = jnp.max(match, axis=1, keepdims=True)
        rank = rank + jnp.sum(match * col.astype(f32), axis=1, keepdims=True)
        owned = owned + found * jnp.where(lane_f == which, 1.0, 0.0)
    owner_len = jnp.sum(owned * len_row, axis=1, keepdims=True)
    live = jnp.clip(owner_len - BS * rank, 0.0, float(BS))
    mine = owned > 0.5
    blk_f = blk.astype(f32)
    lead = jnp.min(jnp.where(mine, blk_f, 99.0), axis=0, keepdims=True)
    rep = jnp.max(jnp.where(mine & (lead == blk_f), 1.0, 0.0), axis=1, keepdims=True)
    r_in = iota((384, NP * RP), 0)
    group = lax.shift_right_logical(r_in * 205, 11)
    l_out = iota((384, NP * RP), 1)
    owned_b = owned.astype(bf16)
    hot_a = dot(owned_b, hot((l_out == r_in + 14 * group) & (r_in < 320)))
    hot_q = dot(owned_b, hot((l_out == RP * group + 20) & (r_in < 320)))
    hot_b = pltpu.roll(hot_a, T, 1)
    place = jnp.concatenate(
        [hot_a, hot_b, hot_q] + [pltpu.roll(hot_q, q, 1) for q in (1, 2, 3)], axis=0
    ).astype(bf16)
    lane_k = lane - 10 * lax.shift_right_logical(lane * 205, 11)
    which_row = jnp.sum(owned * lane_k.astype(f32), axis=1, keepdims=True)
    at_row = iota((BP, 128), 1) == which_row.astype(i32)
    tok = iota((BP, TOK), 1)
    start = blk * BS
    usable = (tok >= start) & (tok < start + live.astype(i32))

    arrive("sgu")
    for t in range(11):
        sgu2[:, t * 128 : (t + 1) * 128] = sgu_v[0, :, :, t * 128 : (t + 1) * 128].reshape(
            2 * CW, 128
        )
    arrive("cache")

    wait(abuf, rsem, 0, NP - 1)
    scale = 1.0 / math.sqrt(HD)
    all_queries = abuf[...].reshape(NP * RP, HD)
    picked = [
        dot(place[hd * BP : (hd + 1) * BP], all_queries).astype(bf16) for hd in range(2)
    ]
    parts = []
    shifts = []
    totals = []
    for hd in range(2):
        cols = slice(hd * HD, (hd + 1) * HD)
        keys = cache_v[:, 0, :, cols].reshape(TOK, HD)
        scores = (
            lax.dot_general(
                picked[hd], keys, (((1,), (1,)), ((), ())), preferred_element_type=f32
            )
            * scale
        )
        scores = jnp.where(usable, scores, low)
        top = jnp.max(scores, axis=1, keepdims=True)
        req_top = jnp.max(jnp.where(mine, top, low), axis=0, keepdims=True)
        shift = jnp.max(jnp.where(mine, req_top, low), axis=1, keepdims=True)
        shift = shift.astype(bf16).astype(f32)
        weights = jnp.where(usable, jnp.exp(scores - shift), 0.0)
        totals.append(jnp.sum(weights, axis=1, keepdims=True))
        shifts.append(shift)
        values = cache_v[:, 1, :, cols].reshape(TOK, HD)
        parts.append(dot(weights.astype(bf16), values))
    tails = [jnp.where(rep > 0.5, shift, 0.0) for shift in shifts] + totals
    message = jnp.concatenate(
        parts + [jnp.where(at_row, tail, 0.0) for tail in tails], axis=0
    ).astype(bf16)
    bsend[...] = dot_t(place, message).astype(bf16).reshape(NP, RP, 128)
    bbuf[p] = bsend[p]
    send_pool(lambda j: bsend.at[j], bbuf, 1)

    arrive("routes", "gates")
    own_lane = iota((TP, 320), 1)
    own_row = iota((TP, 320), 0)
    own = (own_lane == own_row + T * p) & (own_row < T)
    row16 = iota((TP, 1), 0)
    lane_e = iota((TP, 128), 1)
    named = jnp.zeros((TP, 128), f32)
    gate = jnp.zeros((TP, 128), f32)
    routes_t = routes_v[...].astype(f32)
    gates_t = gates_v[...]
    for k in range(6):
        pick = jnp.sum(jnp.where(own, routes_t[k : k + 1], 0.0), axis=1, keepdims=True)
        pick = jnp.where(row16 < T, pick, -1.0).astype(i32)
        amount = jnp.sum(jnp.where(own, gates_t[k : k + 1], 0.0), axis=1, keepdims=True)
        named = named + jnp.where(lane_e == pick, 1.0, 0.0)
        gate = gate + jnp.where(lane_e == pick, amount, 0.0)
    earlier = hot(iota((TP, TP), 1) < iota((TP, TP), 0))
    order = dot(earlier, named.astype(bf16))
    gate_hi = gate.astype(bf16)
    gate_lo = (gate - gate_hi.astype(f32)).astype(bf16)
    l_d = iota((128, 512), 1)
    exp_d = hot(
        iota((128, 512), 0)
        == 2 * lax.shift_right_logical(l_d, 4) + (lax.shift_right_logical(l_d, 1) & 1)
    )
    table_nr = jnp.concatenate([named, order], axis=0).astype(bf16)
    wide = dot(table_nr, exp_d)
    l16 = iota((TP, 512), 1)
    sel = (wide[0:TP] > 0.5) & (wide[TP:].astype(i32) == (l16 & 1))
    quarter = lax.shift_right_logical(l16, 2) & 3
    sel48 = jnp.concatenate([hot(sel & (quarter == c)) for c in range(3)], axis=0)
    l_g = iota((128, 256), 1)
    exp_g = hot(
        iota((128, 256), 0)
        == 2 * lax.shift_right_logical(l_g, 3) + (lax.shift_right_logical(l_g, 1) & 1)
    )
    wide = dot(jnp.concatenate([table_nr, gate_hi, gate_lo], axis=0), exp_g)
    l8 = iota((TP, 256), 1)
    sel = (wide[0:TP] > 0.5) & (wide[TP : 2 * TP].astype(i32) == (l8 & 1))
    half = lax.shift_right_logical(l8, 2) & 1
    combine = jnp.concatenate(
        [
            jnp.where(sel & (half == c), wide[(2 + part) * TP : (3 + part) * TP], 0.0)
            for c in range(2)
            for part in range(2)
        ],
        axis=0,
    ).astype(bf16)
    arrive("wgu")
    for t in range(11):
        wgu2[0, :, t * 128 : (t + 1) * 128] = wgu_v[0, :, :, t * 128 : (t + 1) * 128].reshape(
            2 * CW, 128
        )
    arrive("wout", "fresh", "residual", "gain")

    l_row = iota((128, NP * RP), 1)
    r_row = iota((128, NP * RP), 0)
    take_sums = hot(l_row == (r_row & 31) * RP + 20 + lax.shift_right_logical(r_row, 5))
    l_row = iota((64, NP * RP), 1)
    r_row = iota((64, NP * RP), 0)
    source = lax.shift_right_logical(l_row * 2731, 16)
    keep = (l_row - RP * source) == (r_row & 15) + T * lax.shift_right_logical(r_row, 5)
    widen = hot(source[0:NP] == r_row[0:NP])
    diagonal = iota((TP, 128), 0) == iota((TP, 128), 1)
    k_own = jnp.concatenate([fresh_v[:, 0, :].astype(f32), rows_pad], axis=0)
    v_own = jnp.concatenate([fresh_v[:, 1, :].astype(f32), rows_pad], axis=0)
    wait(bbuf, rsem, 1, NP - 1)
    received = bbuf[...].reshape(NP * RP, 128)
    sums = dot(take_sums, received)
    columns = []
    fresh_ws = []
    for hd in range(2):
        cols = slice(hd * HD, (hd + 1) * HD)
        fresh = jnp.sum(q_own[:, cols] * k_own[:, cols], axis=1, keepdims=True) * scale
        fresh = jnp.sum(jnp.where(diagonal, fresh, 0.0), axis=0, keepdims=True)
        total = sums[(2 + hd) * NP : (3 + hd) * NP]
        tops = jnp.where(total > 0.0, sums[hd * NP : (hd + 1) * NP], low)
        peak = jnp.maximum(jnp.max(tops, axis=0, keepdims=True), fresh)
        share = jnp.exp(tops - peak)
        fresh_w = jnp.exp(fresh - peak)
        denom = jnp.sum(share * total, axis=0, keepdims=True) + fresh_w
        share = (share / denom)[:, 0:TP]
        share_hi = share.astype(bf16).astype(f32)
        columns += [share_hi, share - share_hi]
        fresh_ws.append(
            jnp.sum(jnp.where(diagonal, fresh_w / denom, 0.0), axis=1, keepdims=True)
        )
    spread_w = dot_t(jnp.concatenate(columns, axis=1).astype(bf16), widen)
    mixed = dot(jnp.where(keep, spread_w, 0.0).astype(bf16), received)
    joined = [
        mixed[2 * hd * TP : (2 * hd + 1) * TP]
        + mixed[(2 * hd + 1) * TP : (2 * hd + 2) * TP]
        + fresh_ws[hd] * v_own[:, hd * HD : (hd + 1) * HD]
        for hd in range(2)
    ]
    attended = jnp.concatenate(joined, axis=1).astype(bf16)
    for j in range(NH):
        csend[j] = dot(attended, wout_v[:, j * CW : (j + 1) * CW]).astype(bf16)
    cbuf[h] = csend[h]
    send_head(lambda j: csend.at[j], cbuf, 2)

    for t in range(6):
        wgu2[1, :, t * 128 : (t + 1) * 128] = wgu_v[1, :, :, t * 128 : (t + 1) * 128].reshape(
            2 * CW, 128
        )

    wait(cbuf, rsem, 2, NH - 1)
    own_cols = pl.ds(pl.multiple_of(h * CW, CW), CW)
    after = jnp.concatenate([residual_v[:, own_cols].astype(f32), rows_pad], axis=0)
    for j in range(NH):
        after = after + cbuf[j].astype(f32)
    scaled = (after * gain_v[own_cols].astype(f32).reshape(1, CW)).astype(bf16)
    square = jnp.sum(after * after, axis=1, keepdims=True)
    square_hi = square.astype(bf16).astype(f32)
    lane_t = iota((TP, 128), 1)
    squares = jnp.where(lane_t == 0, square_hi, jnp.where(lane_t == 1, square - square_hi, 0.0))
    rows48 = jnp.concatenate([scaled[:, 0:128], scaled[:, 128:256], squares.astype(bf16)], axis=0)
    dsend[...] = dot_t(sel48, rows48).astype(bf16).reshape(NP, TP, 128)
    dbuf[p] = dsend[p]
    send_pool(lambda j: dsend.at[j], dbuf, 3)

    d_in = iota((CW, 2 * CW), 0)
    d_out = iota((CW, 2 * CW), 1)
    to_gate = hot(d_out == 2 * d_in)
    to_up = hot(d_out == 2 * d_in + 1)
    spread_own = jnp.concatenate([dot(scaled, to_gate), dot(scaled, to_up)], axis=0).astype(bf16)
    shared = dot(spread_own, sgu2[...]).astype(bf16)
    for j in range(NH):
        width = min(CW, max(0, FFE - j * CW))
        for c in range(2):
            at = c * CW
            if width > 0:
                ssend[j, :, at : at + width] = shared[
                    c * TP : (c + 1) * TP, j * CW : j * CW + width
                ]
            if width < CW:
                ssend[j, :, at + width : at + CW] = jnp.zeros((TP, CW - width), bf16)
        ssend[j, :, 2 * CW :] = squares.astype(bf16)
    sbuf[h] = ssend[h]
    send_head(lambda j: ssend.at[j], sbuf, 6)
    for t in range(6, 11):
        wgu2[1, :, t * 128 : (t + 1) * 128] = wgu_v[1, :, :, t * 128 : (t + 1) * 128].reshape(
            2 * CW, 128
        )
    slot = iota((128, 512), 0)
    from_row = (
        (lax.shift_right_logical(slot, 1) & 31) * TP
        + lax.shift_right_logical(slot, 6) * 2
        + (slot & 1)
    )
    source = iota((128, 512), 1)
    gathers = [hot(source == from_row + 4 * c) for c in range(3)]

    wait(dbuf, rsem, 3, NP - 1)
    arrived = dbuf[...].reshape(NP * TP, 128)
    rows = jnp.concatenate([dot(gathers[0], arrived), dot(gathers[1], arrived)], axis=1).astype(bf16)
    row_squares = dot(gathers[2], arrived)
    for_gate = dot(rows, to_gate).astype(bf16)
    for_up = dot(rows, to_up).astype(bf16)
    boths = [
        jnp.concatenate([for_gate[e * 64 : (e + 1) * 64], for_up[e * 64 : (e + 1) * 64]], axis=0)
        for e in range(2)
    ]

    def ring_copy(src, dst, send_sem, recv_sem, to):
        return pltpu.make_async_remote_copy(
            src_ref=src,
            dst_ref=dst,
            send_sem=send_sem,
            recv_sem=recv_sem,
            device_id={"head": to},
            device_id_type=MESH,
        )

    down = lax.rem(h + NH - 1, NH)
    up = lax.rem(h + 1, NH)
    e_parts = [(0, 896), (896, 1664), (1664, 2432), (2432, 2944)]
    f_cols = [(0, 384), (384, 768), (768, 1152), (1152, 1408)]
    sides = ((down, edown, -1), (up, eup, 1))

    def off(by):
        return lax.rem(h + by + NH, NH)

    def e_copy(n, way, chunk, slot, to):
        lo, hi = e_parts[n]
        land = sides[way][1]
        return ring_copy(
            esend.at[chunk, :, pl.ds(lo, hi - lo)],
            land.at[slot, :, pl.ds(lo, hi - lo)],
            essem.at[way, n],
            ersem.at[way, slot, n],
            to,
        )

    def e_take(n, way, slot):
        lo, hi = e_parts[n]
        e_copy(n, way, h, slot, down).wait_recv()
        return sides[way][1][slot, :, lo:hi].astype(f32)

    for n, (lo, _) in enumerate(e_parts):
        c_lo, c_hi = f_cols[n]
        wide = c_hi - c_lo
        for e in range(2):
            partial = dot(boths[e], wgu2[e, :, c_lo:c_hi]).astype(bf16)
            for j in range(4):
                for c in range(2):
                    esend[4 * e + j, :, lo + c * wide : lo + (c + 1) * wide] = partial[
                        c * 64 + j * TP : c * 64 + (j + 1) * TP
                    ]
        if n == 0:
            for j in range(NH):
                esend[j, :, 768:896] = row_squares[j * TP : (j + 1) * TP].astype(bf16)
        for way, (_, _, sign) in enumerate(sides):
            if n % 2 == way:
                e_copy(n, way, off(4 * sign), 1, off(2 * sign)).start()
            e_copy(n, way, off(3 * sign), 0, off(sign)).start()
            e_copy(n, way, off(sign), 2, off(sign)).start()

    wait(sbuf, rsem, 6, NH - 1)
    total = sbuf[0].astype(f32)
    for j in range(1, NH):
        total = total + sbuf[j].astype(f32)
    ss = total[:, 2 * CW :]
    r_own = lax.rsqrt((ss[:, 0:1] + ss[:, 1:2]) * (1.0 / 2048) + epsilon)
    g = total[:, 0:CW] * r_own
    u = total[:, CW : 2 * CW] * r_own
    tbuf[h] = (g / (1.0 + jnp.exp(-g)) * u).astype(bf16)
    send_head(lambda j: tbuf.at[h], tbuf, 7)

    for n, (lo, hi) in enumerate(e_parts):
        for way, (_, _, sign) in enumerate(sides):
            chunk = off(2 * sign)
            passed = esend[chunk, :, lo:hi].astype(f32) + e_take(n, way, 0)
            if n % 2 == way:
                passed = passed + e_take(n, way, 1)
            esend[chunk, :, lo:hi] = passed.astype(bf16)
            e_copy(n, way, chunk, 3, chunk).start()

    def e_drain():
        for way, land in enumerate((edown, eup)):
            for n, (lo, hi) in enumerate(e_parts):
                view = land.at[pl.ds(0, 4 if n % 2 == way else 3), :, pl.ds(lo, hi - lo)]
                pltpu.make_async_copy(view, view, essem.at[way, n]).wait()

    pending.append(e_drain)
    f_parts = [(0, 768), (768, FFE)]

    def f_send(n, way, origin, hop):
        lo, hi = f_parts[n]
        sign = sides[way][2]
        view = fbuf.at[off(-sign * origin), :, pl.ds(lo, hi - lo)]
        ring_copy(
            view, view, fssem.at[way, n], frsem.at[way, origin + hop - 1, n], off(sign * hop)
        ).start()

    def f_wait(n, way, origin):
        lo, hi = f_parts[n]
        view = fbuf.at[off(-sides[way][2] * origin), :, pl.ds(lo, hi - lo)]
        ring_copy(
            view, view, fssem.at[way, n], frsem.at[way, origin - 1, n], down
        ).wait_recv()

    r_slot = None
    for n, (lo, hi) in enumerate(e_parts):
        piece = esend[h, :, lo:hi].astype(f32)
        for way in range(2):
            piece = piece + e_take(n, way, 2) + e_take(n, way, 3)
        c_lo, c_hi = f_cols[n]
        wide = c_hi - c_lo
        if n == 0:
            r_slot = lax.rsqrt((piece[:, 768:769] + piece[:, 769:770]) * (1.0 / 2048) + epsilon)
        g = piece[:, 0:wide] * r_slot
        u = piece[:, wide : 2 * wide] * r_slot
        fbuf[h, :, c_lo:c_hi] = (g / (1.0 + jnp.exp(-g)) * u).astype(bf16)
        if n % 2 == 1:
            for hop in (2, 1):
                for way in range(2):
                    f_send(n // 2, way, 0, hop)
    for n in range(2):
        for way in range(2):
            f_wait(n, way, 2)
            if n == way:
                f_send(n, way, 2, 2)
            f_send(n, way, 2, 1)

    def f_drain():
        for way in range(2):
            for n, (lo, hi) in enumerate(f_parts):
                view = fbuf.at[pl.ds(0, 4 if n == way else 3), :, pl.ds(lo, hi - lo)]
                pltpu.make_async_copy(view, view, fssem.at[way, n]).wait()

    pending.append(f_drain)
    arrive("wdn", "sdn", "next_gain", "wqkv")
    back = iota((256, 256), 0)
    kk = iota((256, 256), 1)
    slot_of = (
        (lax.shift_right_logical(back, 1) & 1) * 64
        + lax.shift_right_logical(back, 3) * 2
        + (back & 1)
        + (lax.shift_right_logical(back, 2) & 1) * 128
    )
    returns = hot(kk == slot_of)

    for n in range(2):
        for way in range(2):
            for origin in (1, 3, 4) if n == way else (1, 3):
                f_wait(n, way, origin)
    outs = [
        dot(fbuf[4 * e : 4 * e + 4].reshape(64, FFE), wdn_v[e]).astype(bf16)
        for e in range(2)
    ]
    stacked = jnp.concatenate(
        [outs[0][:, 0:128], outs[1][:, 0:128], outs[0][:, 128:256], outs[1][:, 128:256]], axis=0
    )
    gsend[...] = dot(returns, stacked).reshape(NP, 8, 128)
    gbuf[p] = gsend[p]
    send_pool(lambda j: gsend.at[j], gbuf, 4)
    wait(tbuf, rsem, 7, NH - 1)
    for j in range(6):
        width = min(CW, FFE - j * CW)
        after = after + dot(tbuf[j, :, 0:width], sdn_v[0, j * CW : j * CW + width, :])
    wait(gbuf, rsem, 4, NP - 1)
    routed = dot(combine, gbuf[...].reshape(NP * 8, 128).astype(bf16))
    routed = jnp.concatenate(
        [routed[0:TP] + routed[TP : 2 * TP], routed[2 * TP : 3 * TP] + routed[3 * TP :]], axis=1
    )
    hbuf[h] = (after + routed).astype(bf16)
    send_head(lambda j: hbuf.at[h], hbuf, 5)
    next_gain = next_gain_v[...].astype(f32).reshape(NH, CW)

    wait(hbuf, rsem, 5, NH - 1)
    mean = jnp.zeros((TP, 1), f32)
    for j in range(NH):
        piece = hbuf[j].astype(f32)
        hid_ref[:, j * CW : (j + 1) * CW] = hbuf[j][0:T]
        mean = mean + jnp.sum(piece * piece, axis=1, keepdims=True)
    r_next = lax.rsqrt(mean * (1.0 / 2048) + epsilon)
    projected = jnp.zeros((TP, 768), f32)
    for j in range(NH):
        piece = (hbuf[j].astype(f32) * r_next * next_gain[j : j + 1]).astype(bf16)
        projected = projected + dot(piece, wqkv_v[j * CW : (j + 1) * CW, :])
    qkv_ref[...] = projected[0:T].astype(bf16)

    for finish in pending:
        finish()


def hand_over(hid_in, qkv_in, hid_out, qkv_out, sem):
    copies = [
        pltpu.make_async_copy(hid_in, hid_out, sem.at[0]),
        pltpu.make_async_copy(qkv_in, qkv_out, sem.at[1]),
    ]
    for copy in copies:
        copy.start()
    for copy in copies:
        copy.wait()


def per_device(
    queries,
    fresh_pair,
    cache_blocks,
    block_table,
    lengths,
    residual,
    w_output,
    norm_gain,
    routes,
    route_gates,
    w_gate_up,
    w_down,
    shared_gate_up,
    shared_down,
    next_gain,
    w_query_key_value,
):
    vmem = pl.BlockSpec(memory_space=pltpu.VMEM)
    hbm = pl.BlockSpec(memory_space=pltpu.HBM)
    return pl.pallas_call(
        kernel,
        out_shape=(pltpu.VMEM((T, 2048), bf16), pltpu.VMEM((T, 768), bf16)),
        in_specs=[hbm] * 16,
        out_specs=(vmem, vmem),
        scratch_shapes=[
            pltpu.VMEM((T, CW), bf16),
            pltpu.VMEM((T, 2, CW), bf16),
            pltpu.VMEM((T, 2048), bf16),
            pltpu.VMEM((2048,), bf16),
            pltpu.VMEM((2048,), bf16),
            pltpu.VMEM((320,), i32),
            pltpu.VMEM((6, 320), i32),
            pltpu.VMEM((6, 320), f32),
            pltpu.VMEM((384, 256), i32),
            pltpu.VMEM((BLK, 2, BS, CW), bf16),
            pltpu.VMEM((CW, 2048), bf16),
            pltpu.VMEM((2, CW, 2, FFE), bf16),
            pltpu.VMEM((2, FFE, CW), bf16),
            pltpu.VMEM((1, CW, 2, FFE), bf16),
            pltpu.VMEM((1, FFE, CW), bf16),
            pltpu.VMEM((2048, 768), bf16),
            pltpu.VMEM((2, 2 * CW, FFE), bf16),
            pltpu.VMEM((2 * CW, FFE), bf16),
            pltpu.VMEM((NP, RP, 128), bf16),
            pltpu.VMEM((NP, RP, 128), bf16),
            pltpu.VMEM((NP, RP, 128), bf16),
            pltpu.VMEM((NH, TP, CW), bf16),
            pltpu.VMEM((NH, TP, CW), bf16),
            pltpu.VMEM((NP, TP, 128), bf16),
            pltpu.VMEM((NP, TP, 128), bf16),
            pltpu.VMEM((NH, TP, EW), bf16),
            pltpu.VMEM((4, TP, EW), bf16),
            pltpu.VMEM((4, TP, EW), bf16),
            pltpu.VMEM((NH, TP, FFE), bf16),
            pltpu.VMEM((NH, TP, SW), bf16),
            pltpu.VMEM((NH, TP, SW), bf16),
            pltpu.VMEM((NH, TP, CW), bf16),
            pltpu.VMEM((NP, 8, 128), f32),
            pltpu.VMEM((NP, 8, 128), f32),
            pltpu.VMEM((NH, TP, CW), bf16),
            pltpu.SemaphoreType.DMA((16,)),
            pltpu.SemaphoreType.DMA((8,)),
            pltpu.SemaphoreType.DMA((8,)),
            pltpu.SemaphoreType.DMA((2, 4)),
            pltpu.SemaphoreType.DMA((2, 4, 4)),
            pltpu.SemaphoreType.DMA((2, 2)),
            pltpu.SemaphoreType.DMA((2, 4, 2)),
        ],
        compiler_params=pltpu.CompilerParams(
            collective_id=0, has_side_effects=True, vmem_limit_bytes=58 << 20
        ),
    )(
        queries,
        fresh_pair,
        residual,
        norm_gain,
        next_gain,
        lengths,
        routes.T,
        route_gates.T,
        block_table,
        cache_blocks,
        w_output,
        w_gate_up,
        w_down,
        shared_gate_up,
        shared_down,
        w_query_key_value,
    )


def solution(mesh):
    in_specs = (
        P("pool", "head"),
        P("pool", None, "head"),
        P("pool", None, None, "head"),
        P(),
        P(),
        P("pool", None),
        P("head", None),
        P(),
        P(),
        P(),
        P("pool", "head", None, None),
        P("pool", None, "head"),
        P(None, "head", None, None),
        P(None, None, "head"),
        P(),
        P(None, "head"),
    )
    out_specs = (P("pool", None), P("pool", "head"))
    return jax.shard_map(
        per_device, mesh=mesh, in_specs=in_specs, out_specs=out_specs, check_vma=False
    )
```

```python
import math

import jax
import jax.numpy as jnp
from jax import lax
from jax.experimental import pallas as pl
from jax.experimental.pallas import tpu as pltpu
from jax.sharding import PartitionSpec as P

HD = 128
NP = 32
NH = 8
T = 10
TP = 16
CW = 256
FFE = 1408
BLK = 36
BP = 40
BS = 64
TOK = BLK * BS
RP = 24
EW = 2 * FFE + 128
SW = 2 * CW + 128
epsilon = 1e-06
low = -1e30
f32 = jnp.float32
bf16 = jnp.bfloat16
i32 = jnp.int32
MESH = pl.DeviceIdType.MESH


def iota(shape, dim):
    return lax.broadcasted_iota(i32, shape, dim)


def dot(a, b):
    return jnp.dot(a, b, preferred_element_type=f32)


def dot_t(a, b):
    return lax.dot_general(a, b, (((0,), (0,)), ((), ())), preferred_element_type=f32)


def hot(cond):
    return jnp.where(cond, 1.0, 0.0).astype(bf16)


def kernel(
    queries_hbm,
    fresh_hbm,
    residual_hbm,
    gain_hbm,
    next_gain_hbm,
    len_hbm,
    routes_hbm,
    gates_hbm,
    table_hbm,
    cache_hbm,
    wout_hbm,
    wgu_hbm,
    wdn_hbm,
    sgu_hbm,
    sdn_hbm,
    wqkv_hbm,
    hid_ref,
    qkv_ref,
    queries_v,
    fresh_v,
    residual_v,
    gain_v,
    next_gain_v,
    len_v,
    routes_v,
    gates_v,
    table_v,
    cache_v,
    wout_v,
    wgu_v,
    wdn_v,
    sgu_v,
    sdn_v,
    wqkv_v,
    wgu2,
    sgu2,
    abuf,
    bsend,
    bbuf,
    csend,
    cbuf,
    dsend,
    dbuf,
    esend,
    edown,
    eup,
    fbuf,
    sbuf,
    ssend,
    tbuf,
    gsend,
    gbuf,
    hbuf,
    lsem,
    ssem,
    rsem,
    essem,
    ersem,
    fssem,
    frsem,
    hrsem,
):
    p = lax.axis_index("pool")
    h = lax.axis_index("head")

    loads = {
        name: pltpu.make_async_copy(src, dst, lsem.at[n])
        for n, (name, src, dst) in enumerate(
            [
                ("queries", queries_hbm, queries_v),
                ("table", table_hbm, table_v.at[pl.ds(0, 320)]),
                ("len", len_hbm, len_v),
                ("cache", cache_hbm, cache_v),
                ("routes", routes_hbm, routes_v),
                ("gates", gates_hbm, gates_v),
                ("fresh", fresh_hbm, fresh_v),
                ("sgu", sgu_hbm, sgu_v),
                ("wgu", wgu_hbm, wgu_v),
                ("wout", wout_hbm, wout_v),
                ("residual", residual_hbm, residual_v),
                ("gain", gain_hbm, gain_v),
                ("wdn", wdn_hbm, wdn_v),
                ("sdn", sdn_hbm, sdn_v),
                ("next_gain", next_gain_hbm, next_gain_v),
                ("wqkv", wqkv_hbm, wqkv_v),
            ]
        )
    }
    loads["queries"].start()

    barrier = pltpu.get_barrier_semaphore()

    def greet_pool(k, carry):
        pl.semaphore_signal(
            barrier, inc=1, device_id={"pool": lax.rem(p + k, NP)}, device_id_type=MESH
        )
        return carry

    def greet_head(k, carry):
        pl.semaphore_signal(
            barrier, inc=1, device_id={"head": lax.rem(h + k, NH)}, device_id_type=MESH
        )
        return carry

    lax.fori_loop(1, NP, greet_pool, 0)
    lax.fori_loop(1, NH, greet_head, 0)
    for name in ("table", "len"):
        loads[name].start()

    waited = set()
    pending = []

    def arrive(*names):
        for name in names:
            loads[name].wait()
            waited.add(name)


    def send_pool(src, buf, n):
        def one(k, carry):
            j = lax.rem(p + k, NP)
            pltpu.make_async_remote_copy(
                src_ref=src(j),
                dst_ref=buf.at[p],
                send_sem=ssem.at[n],
                recv_sem=rsem.at[n],
                device_id={"pool": j},
                device_id_type=MESH,
            ).start()
            return carry

        lax.fori_loop(1, NP, one, 0)
        pending.append(lambda: wait(buf, ssem, n, NP - 1))

    def send_head(src, buf, n):
        def one(k, carry):
            j = lax.rem(h + k, NH)
            pltpu.make_async_remote_copy(
                src_ref=src(j),
                dst_ref=buf.at[h],
                send_sem=ssem.at[n],
                recv_sem=rsem.at[n],
                device_id={"head": j},
                device_id_type=MESH,
            ).start()
            return carry

        lax.fori_loop(1, NH, one, 0)
        pending.append(lambda: wait(buf, ssem, n, NH - 1))

    def wait(buf, sem, n, count):
        view = buf.at[pl.ds(0, count)]
        pltpu.make_async_copy(view, view, sem.at[n]).wait()

    arrive("queries")
    rows_pad = jnp.zeros((TP - T, CW), f32)
    q_own = jnp.concatenate([queries_v[...].astype(f32), rows_pad], axis=0)
    abuf[p] = jnp.concatenate(
        [q_own[0:T, 0:HD], q_own[0:T, HD:CW], rows_pad[0:4, 0:HD]], axis=0
    ).astype(bf16)
    pl.semaphore_wait(barrier, NP - 1 + NH - 1)
    send_pool(lambda j: abuf.at[p], abuf, 0)
    for name in loads:
        if name not in ("queries", "table", "len"):
            loads[name].start()

    table_v[pl.ds(320, 64), :] = jnp.zeros((64, 256), i32)
    arrive("table", "len")
    table = table_v[...].astype(f32)
    heads_t = jnp.transpose(table[:, 0:128])
    lane = iota((1, 384), 1)
    real = lane < 320
    blk = iota((BP, 1), 0)
    ids = jnp.where(blk < BLK, blk + BLK * p, -7).astype(f32)
    len_row = jnp.concatenate(
        [len_v[...].reshape(1, 320).astype(f32), jnp.zeros((1, 64), f32)], axis=1
    )
    hot0 = jnp.where((heads_t[0:1] == ids) & real, 1.0, 0.0)
    hot1 = jnp.where((heads_t[1:2] == ids) & real, 1.0, 0.0)
    is_long = (heads_t[2:3] >= 0.0) & real
    lane_f = lane.astype(f32)
    first = jnp.min(jnp.where(is_long, lane_f, 1e6), axis=1, keepdims=True)
    last = jnp.max(jnp.where(is_long, lane_f, -1.0), axis=1, keepdims=True)
    row_f = iota((384, 1), 0).astype(f32)
    col = iota((1, 256), 1)
    owned = hot0 + hot1
    rank = jnp.sum(hot1, axis=1, keepdims=True)
    for which in (first, last):
        listed = jnp.sum(jnp.where(row_f == which, table, 0.0), axis=0, keepdims=True)
        match = jnp.where((listed == ids) & (col >= 2), 1.0, 0.0)
        found = jnp.max(match, axis=1, keepdims=True)
        rank = rank + jnp.sum(match * col.astype(f32), axis=1, keepdims=True)
        owned = owned + found * jnp.where(lane_f == which, 1.0, 0.0)
    owner_len = jnp.sum(owned * len_row, axis=1, keepdims=True)
    live = jnp.clip(owner_len - BS * rank, 0.0, float(BS))
    mine = owned > 0.5
    blk_f = blk.astype(f32)
    lead = jnp.min(jnp.where(mine, blk_f, 99.0), axis=0, keepdims=True)
    rep = jnp.max(jnp.where(mine & (lead == blk_f), 1.0, 0.0), axis=1, keepdims=True)
    r_in = iota((384, NP * RP), 0)
    group = lax.shift_right_logical(r_in * 205, 11)
    l_out = iota((384, NP * RP), 1)
    owned_b = owned.astype(bf16)
    hot_a = dot(owned_b, hot((l_out == r_in + 14 * group) & (r_in < 320)))
    hot_q = dot(owned_b, hot((l_out == RP * group + 20) & (r_in < 320)))
    hot_b = pltpu.roll(hot_a, T, 1)
    place = jnp.concatenate(
        [hot_a, hot_b, hot_q] + [pltpu.roll(hot_q, q, 1) for q in (1, 2, 3)], axis=0
    )
    place_t = jnp.transpose(place).astype(bf16)
    place = place[0 : 2 * BP].astype(bf16)
    lane_k = lane - 10 * lax.shift_right_logical(lane * 205, 11)
    which_row = jnp.sum(owned * lane_k.astype(f32), axis=1, keepdims=True)
    at_row = iota((BP, 128), 1) == which_row.astype(i32)
    tok = iota((BP, TOK), 1)
    start = blk * BS
    usable = (tok >= start) & (tok < start + live.astype(i32))

    arrive("sgu")
    for t in range(11):
        sgu2[:, t * 128 : (t + 1) * 128] = sgu_v[0, :, :, t * 128 : (t + 1) * 128].reshape(
            2 * CW, 128
        )
    arrive("cache")

    wait(abuf, rsem, 0, NP - 1)
    scale = 1.0 / math.sqrt(HD)
    all_queries = abuf[...].reshape(NP * RP, HD)
    none = jnp.zeros((BP, HD), f32)
    picked = dot(place, all_queries)
    picked = jnp.concatenate(
        [
            jnp.concatenate([picked[0:BP], none], axis=1),
            jnp.concatenate([none, picked[BP:]], axis=1),
        ],
        axis=0,
    ).astype(bf16)
    keys = cache_v[:, 0].reshape(TOK, CW)
    scores = (
        lax.dot_general(picked, keys, (((1,), (1,)), ((), ())), preferred_element_type=f32) * scale
    )
    shifts = []
    totals = []
    weights = []
    for hd in range(2):
        score = jnp.where(usable, scores[hd * BP : (hd + 1) * BP], low)
        top = jnp.max(score, axis=1, keepdims=True)
        req_top = jnp.max(jnp.where(mine, top, low), axis=0, keepdims=True)
        shift = jnp.max(jnp.where(mine, req_top, low), axis=1, keepdims=True)
        shift = shift.astype(bf16).astype(f32)
        weight = jnp.where(usable, jnp.exp(score - shift), 0.0)
        totals.append(jnp.sum(weight, axis=1, keepdims=True))
        shifts.append(shift)
        weights.append(weight.astype(bf16))
    values = cache_v[:, 1].reshape(TOK, CW)
    both_parts = dot(jnp.concatenate(weights, axis=0), values)
    parts = [both_parts[0:BP, 0:HD], both_parts[BP:, HD:CW]]
    tails = [jnp.where(rep > 0.5, shift, 0.0) for shift in shifts] + totals
    message = jnp.concatenate(
        parts + [jnp.where(at_row, tail, 0.0) for tail in tails], axis=0
    ).astype(bf16)
    bsend[...] = dot(place_t, message).astype(bf16).reshape(NP, RP, 128)
    bbuf[p] = bsend[p]
    send_pool(lambda j: bsend.at[j], bbuf, 1)

    arrive("routes", "gates")
    own_lane = iota((TP, 320), 1)
    own_row = iota((TP, 320), 0)
    own = (own_lane == own_row + T * p) & (own_row < T)
    row16 = iota((TP, 1), 0)
    lane_e = iota((TP, 128), 1)
    named = jnp.zeros((TP, 128), f32)
    gate = jnp.zeros((TP, 128), f32)
    routes_t = routes_v[...].astype(f32)
    gates_t = gates_v[...]
    for k in range(6):
        pick = jnp.sum(jnp.where(own, routes_t[k : k + 1], 0.0), axis=1, keepdims=True)
        pick = jnp.where(row16 < T, pick, -1.0).astype(i32)
        amount = jnp.sum(jnp.where(own, gates_t[k : k + 1], 0.0), axis=1, keepdims=True)
        named = named + jnp.where(lane_e == pick, 1.0, 0.0)
        gate = gate + jnp.where(lane_e == pick, amount, 0.0)
    earlier = hot(iota((TP, TP), 1) < iota((TP, TP), 0))
    order = dot(earlier, named.astype(bf16))
    gate_hi = gate.astype(bf16)
    gate_lo = (gate - gate_hi.astype(f32)).astype(bf16)
    l_d = iota((128, 512), 1)
    exp_d = hot(
        iota((128, 512), 0)
        == 2 * lax.shift_right_logical(l_d, 4) + (lax.shift_right_logical(l_d, 1) & 1)
    )
    table_nr = jnp.concatenate([named, order], axis=0).astype(bf16)
    wide = dot(table_nr, exp_d)
    l16 = iota((TP, 512), 1)
    sel = (wide[0:TP] > 0.5) & (wide[TP:].astype(i32) == (l16 & 1))
    quarter = lax.shift_right_logical(l16, 2) & 3
    sel48 = jnp.transpose(
        jnp.concatenate([jnp.where(sel & (quarter == c), 1.0, 0.0) for c in range(3)], axis=0)
    ).astype(bf16)
    l_g = iota((128, 256), 1)
    exp_g = hot(
        iota((128, 256), 0)
        == 2 * lax.shift_right_logical(l_g, 3) + (lax.shift_right_logical(l_g, 1) & 1)
    )
    wide = dot(jnp.concatenate([table_nr, gate_hi, gate_lo], axis=0), exp_g)
    l8 = iota((TP, 256), 1)
    sel = (wide[0:TP] > 0.5) & (wide[TP : 2 * TP].astype(i32) == (l8 & 1))
    half = lax.shift_right_logical(l8, 2) & 1
    combine = jnp.concatenate(
        [
            jnp.where(sel & (half == c), wide[(2 + part) * TP : (3 + part) * TP], 0.0)
            for c in range(2)
            for part in range(2)
        ],
        axis=0,
    ).astype(bf16)
    arrive("wgu")
    for t in range(11):
        wgu2[0, :, t * 128 : (t + 1) * 128] = wgu_v[0, :, :, t * 128 : (t + 1) * 128].reshape(
            2 * CW, 128
        )
    arrive("wout", "fresh", "residual", "gain")

    l_row = iota((128, NP * RP), 1)
    r_row = iota((128, NP * RP), 0)
    take_sums = hot(l_row == (r_row & 31) * RP + 20 + lax.shift_right_logical(r_row, 5))
    l_row = iota((64, NP * RP), 1)
    r_row = iota((64, NP * RP), 0)
    source = lax.shift_right_logical(l_row * 2731, 16)
    keep = (l_row - RP * source) == (r_row & 15) + T * lax.shift_right_logical(r_row, 5)
    widen = hot(source[0:NP] == r_row[0:NP])
    diagonal = iota((TP, 128), 0) == iota((TP, 128), 1)
    k_own = jnp.concatenate([fresh_v[:, 0, :].astype(f32), rows_pad], axis=0)
    v_own = jnp.concatenate([fresh_v[:, 1, :].astype(f32), rows_pad], axis=0)
    wait(bbuf, rsem, 1, NP - 1)
    received = bbuf[...].reshape(NP * RP, 128)
    sums = dot(take_sums, received)
    columns = []
    fresh_ws = []
    for hd in range(2):
        cols = slice(hd * HD, (hd + 1) * HD)
        fresh = jnp.sum(q_own[:, cols] * k_own[:, cols], axis=1, keepdims=True) * scale
        fresh = jnp.sum(jnp.where(diagonal, fresh, 0.0), axis=0, keepdims=True)
        total = sums[(2 + hd) * NP : (3 + hd) * NP]
        tops = jnp.where(total > 0.0, sums[hd * NP : (hd + 1) * NP], low)
        peak = jnp.maximum(jnp.max(tops, axis=0, keepdims=True), fresh)
        share = jnp.exp(tops - peak)
        fresh_w = jnp.exp(fresh - peak)
        denom = jnp.sum(share * total, axis=0, keepdims=True) + fresh_w
        share = (share / denom)[:, 0:TP]
        share_hi = share.astype(bf16).astype(f32)
        columns += [share_hi, share - share_hi]
        fresh_ws.append(
            jnp.sum(jnp.where(diagonal, fresh_w / denom, 0.0), axis=1, keepdims=True)
        )
    spread_w = dot_t(jnp.concatenate(columns, axis=1).astype(bf16), widen)
    mixed = dot(jnp.where(keep, spread_w, 0.0).astype(bf16), received)
    joined = [
        mixed[2 * hd * TP : (2 * hd + 1) * TP]
        + mixed[(2 * hd + 1) * TP : (2 * hd + 2) * TP]
        + fresh_ws[hd] * v_own[:, hd * HD : (hd + 1) * HD]
        for hd in range(2)
    ]
    attended = jnp.concatenate(joined, axis=1).astype(bf16)
    for j in range(NH):
        csend[j] = dot(attended, wout_v[:, j * CW : (j + 1) * CW]).astype(bf16)
    cbuf[h] = csend[h]
    send_head(lambda j: csend.at[j], cbuf, 2)

    for t in range(6):
        wgu2[1, :, t * 128 : (t + 1) * 128] = wgu_v[1, :, :, t * 128 : (t + 1) * 128].reshape(
            2 * CW, 128
        )

    wait(cbuf, rsem, 2, NH - 1)
    own_cols = pl.ds(pl.multiple_of(h * CW, CW), CW)
    after = jnp.concatenate([residual_v[:, own_cols].astype(f32), rows_pad], axis=0)
    for j in range(NH):
        after = after + cbuf[j].astype(f32)
    scaled = (after * gain_v[own_cols].astype(f32).reshape(1, CW)).astype(bf16)
    square = jnp.sum(after * after, axis=1, keepdims=True)
    square_hi = square.astype(bf16).astype(f32)
    lane_t = iota((TP, 128), 1)
    squares = jnp.where(lane_t == 0, square_hi, jnp.where(lane_t == 1, square - square_hi, 0.0))
    rows48 = jnp.concatenate([scaled[:, 0:128], scaled[:, 128:256], squares.astype(bf16)], axis=0)
    dsend[...] = dot(sel48, rows48).astype(bf16).reshape(NP, TP, 128)
    dbuf[p] = dsend[p]
    send_pool(lambda j: dsend.at[j], dbuf, 3)

    d_in = iota((CW, 2 * CW), 0)
    d_out = iota((CW, 2 * CW), 1)
    to_gate = hot(d_out == 2 * d_in)
    to_up = hot(d_out == 2 * d_in + 1)
    spread_own = jnp.concatenate([dot(scaled, to_gate), dot(scaled, to_up)], axis=0).astype(bf16)
    shared = dot(spread_own, sgu2[...]).astype(bf16)
    for j in range(NH):
        width = min(CW, max(0, FFE - j * CW))
        for c in range(2):
            at = c * CW
            if width > 0:
                ssend[j, :, at : at + width] = shared[
                    c * TP : (c + 1) * TP, j * CW : j * CW + width
                ]
            if width < CW:
                ssend[j, :, at + width : at + CW] = jnp.zeros((TP, CW - width), bf16)
        ssend[j, :, 2 * CW :] = squares.astype(bf16)
    sbuf[h] = ssend[h]
    send_head(lambda j: ssend.at[j], sbuf, 6)
    for t in range(6, 11):
        wgu2[1, :, t * 128 : (t + 1) * 128] = wgu_v[1, :, :, t * 128 : (t + 1) * 128].reshape(
            2 * CW, 128
        )
    slot = iota((128, 512), 0)
    from_row = (
        (lax.shift_right_logical(slot, 1) & 31) * TP
        + lax.shift_right_logical(slot, 6) * 2
        + (slot & 1)
    )
    source = iota((128, 512), 1)
    gathers = [hot(source == from_row + 4 * c) for c in range(3)]

    wait(dbuf, rsem, 3, NP - 1)
    arrived = dbuf[...].reshape(NP * TP, 128)
    rows = jnp.concatenate([dot(gathers[0], arrived), dot(gathers[1], arrived)], axis=1).astype(bf16)
    row_squares = dot(gathers[2], arrived)
    for_gate = dot(rows, to_gate).astype(bf16)
    for_up = dot(rows, to_up).astype(bf16)
    boths = [
        jnp.concatenate([for_gate[e * 64 : (e + 1) * 64], for_up[e * 64 : (e + 1) * 64]], axis=0)
        for e in range(2)
    ]

    def ring_copy(src, dst, send_sem, recv_sem, to):
        return pltpu.make_async_remote_copy(
            src_ref=src,
            dst_ref=dst,
            send_sem=send_sem,
            recv_sem=recv_sem,
            device_id={"head": to},
            device_id_type=MESH,
        )

    down = lax.rem(h + NH - 1, NH)
    up = lax.rem(h + 1, NH)
    e_parts = [(0, 896), (896, 1664), (1664, 2432), (2432, 2944)]
    f_cols = [(0, 384), (384, 768), (768, 1152), (1152, 1408)]
    sides = ((down, edown, -1), (up, eup, 1))

    def off(by):
        return lax.rem(h + by + NH, NH)

    def e_copy(n, way, chunk, slot, to):
        lo, hi = e_parts[n]
        land = sides[way][1]
        return ring_copy(
            esend.at[chunk, :, pl.ds(lo, hi - lo)],
            land.at[slot, :, pl.ds(lo, hi - lo)],
            essem.at[way, n],
            ersem.at[way, slot, n],
            to,
        )

    def e_take(n, way, slot):
        lo, hi = e_parts[n]
        e_copy(n, way, h, slot, down).wait_recv()
        return sides[way][1][slot, :, lo:hi].astype(f32)

    for n, (lo, _) in enumerate(e_parts):
        c_lo, c_hi = f_cols[n]
        wide = c_hi - c_lo
        for e in range(2):
            partial = dot(boths[e], wgu2[e, :, c_lo:c_hi]).astype(bf16)
            for j in range(4):
                for c in range(2):
                    esend[4 * e + j, :, lo + c * wide : lo + (c + 1) * wide] = partial[
                        c * 64 + j * TP : c * 64 + (j + 1) * TP
                    ]
        if n == 0:
            for j in range(NH):
                esend[j, :, 768:896] = row_squares[j * TP : (j + 1) * TP].astype(bf16)
        for way, (_, _, sign) in enumerate(sides):
            if n % 2 == way:
                e_copy(n, way, off(4 * sign), 1, off(2 * sign)).start()
            e_copy(n, way, off(3 * sign), 0, off(sign)).start()
            e_copy(n, way, off(sign), 2, off(sign)).start()

    wait(sbuf, rsem, 6, NH - 1)
    total = sbuf[0].astype(f32)
    for j in range(1, NH):
        total = total + sbuf[j].astype(f32)
    ss = total[:, 2 * CW :]
    r_own = lax.rsqrt((ss[:, 0:1] + ss[:, 1:2]) * (1.0 / 2048) + epsilon)
    g = total[:, 0:CW] * r_own
    u = total[:, CW : 2 * CW] * r_own
    tbuf[h] = (g / (1.0 + jnp.exp(-g)) * u).astype(bf16)
    send_head(lambda j: tbuf.at[h], tbuf, 7)

    for n, (lo, hi) in enumerate(e_parts):
        for way, (_, _, sign) in enumerate(sides):
            chunk = off(2 * sign)
            passed = esend[chunk, :, lo:hi].astype(f32) + e_take(n, way, 0)
            if n % 2 == way:
                passed = passed + e_take(n, way, 1)
            esend[chunk, :, lo:hi] = passed.astype(bf16)
            e_copy(n, way, chunk, 3, chunk).start()

    def e_drain():
        for way, land in enumerate((edown, eup)):
            for n, (lo, hi) in enumerate(e_parts):
                view = land.at[pl.ds(0, 4 if n % 2 == way else 3), :, pl.ds(lo, hi - lo)]
                pltpu.make_async_copy(view, view, essem.at[way, n]).wait()

    pending.append(e_drain)
    f_parts = [(0, 768), (768, FFE)]

    def f_send(n, way, origin, hop):
        lo, hi = f_parts[n]
        sign = sides[way][2]
        view = fbuf.at[off(-sign * origin), :, pl.ds(lo, hi - lo)]
        ring_copy(
            view, view, fssem.at[way, n], frsem.at[way, origin + hop - 1, n], off(sign * hop)
        ).start()

    def f_wait(n, way, origin):
        lo, hi = f_parts[n]
        view = fbuf.at[off(-sides[way][2] * origin), :, pl.ds(lo, hi - lo)]
        ring_copy(
            view, view, fssem.at[way, n], frsem.at[way, origin - 1, n], down
        ).wait_recv()

    r_slot = None
    for n, (lo, hi) in enumerate(e_parts):
        piece = esend[h, :, lo:hi].astype(f32)
        for way in range(2):
            piece = piece + e_take(n, way, 2) + e_take(n, way, 3)
        c_lo, c_hi = f_cols[n]
        wide = c_hi - c_lo
        if n == 0:
            r_slot = lax.rsqrt((piece[:, 768:769] + piece[:, 769:770]) * (1.0 / 2048) + epsilon)
        g = piece[:, 0:wide] * r_slot
        u = piece[:, wide : 2 * wide] * r_slot
        fbuf[h, :, c_lo:c_hi] = (g / (1.0 + jnp.exp(-g)) * u).astype(bf16)
        if n % 2 == 1:
            for hop in (2, 1):
                for way in range(2):
                    f_send(n // 2, way, 0, hop)
    for n in range(2):
        for way in range(2):
            f_wait(n, way, 2)
            if n == way:
                f_send(n, way, 2, 2)
            f_send(n, way, 2, 1)

    def f_drain():
        for way in range(2):
            for n, (lo, hi) in enumerate(f_parts):
                view = fbuf.at[pl.ds(0, 4 if n == way else 3), :, pl.ds(lo, hi - lo)]
                pltpu.make_async_copy(view, view, fssem.at[way, n]).wait()

    pending.append(f_drain)
    arrive("wdn", "sdn", "next_gain", "wqkv")
    back = iota((256, 256), 0)
    kk = iota((256, 256), 1)
    slot_of = (
        (lax.shift_right_logical(back, 1) & 1) * 64
        + lax.shift_right_logical(back, 3) * 2
        + (back & 1)
        + (lax.shift_right_logical(back, 2) & 1) * 128
    )
    returns = hot(kk == slot_of)

    outs = [0.0, 0.0]
    for n, (lo, hi) in enumerate(f_parts):
        for way in range(2):
            for origin in (1, 3, 4) if n == way else (1, 3):
                f_wait(n, way, origin)
        for e in range(2):
            rows_e = fbuf[4 * e : 4 * e + 4, :, lo:hi].reshape(64, hi - lo)
            outs[e] = outs[e] + dot(rows_e, wdn_v[e, lo:hi, :])
    outs = [out.astype(bf16) for out in outs]
    stacked = jnp.concatenate(
        [outs[0][:, 0:128], outs[1][:, 0:128], outs[0][:, 128:256], outs[1][:, 128:256]], axis=0
    )
    gsend[...] = dot(returns, stacked).reshape(NP, 8, 128)
    gbuf[p] = gsend[p]
    send_pool(lambda j: gsend.at[j], gbuf, 4)
    wait(tbuf, rsem, 7, NH - 1)
    for j in range(6):
        width = min(CW, FFE - j * CW)
        after = after + dot(tbuf[j, :, 0:width], sdn_v[0, j * CW : j * CW + width, :])
    wait(gbuf, rsem, 4, NP - 1)
    routed = dot(combine, gbuf[...].reshape(NP * 8, 128).astype(bf16))
    routed = jnp.concatenate(
        [routed[0:TP] + routed[TP : 2 * TP], routed[2 * TP : 3 * TP] + routed[3 * TP :]], axis=1
    )
    hbuf[h] = (after + routed).astype(bf16)

    def h_copy(k):
        return pltpu.make_async_remote_copy(
            src_ref=hbuf.at[h],
            dst_ref=hbuf.at[h],
            send_sem=ssem.at[5],
            recv_sem=hrsem.at[k],
            device_id={"head": off(k)},
            device_id_type=MESH,
        )

    for k in (4, 3, 5, 2, 6, 1, 7):
        h_copy(k).start()
    pending.append(lambda: wait(hbuf, ssem, 5, NH - 1))

    mean = jnp.zeros((TP, 1), f32)
    projected = jnp.zeros((TP, 768), f32)
    for k in (0, 1, 7, 2, 6, 3, 5, 4):
        j = off(-k)
        if k > 0:
            view = hbuf.at[j]
            pltpu.make_async_copy(view, view, hrsem.at[k]).wait()
        at = pl.multiple_of(j * CW, CW)
        rounded = hbuf[j]
        piece = rounded.astype(f32)
        hid_ref[:, pl.ds(at, CW)] = rounded[0:T]
        mean = mean + jnp.sum(piece * piece, axis=1, keepdims=True)
        piece = piece * next_gain_v[pl.ds(at, CW)].astype(f32).reshape(1, CW)
        projected = projected + dot(piece.astype(bf16), wqkv_v[pl.ds(at, CW), :])
    r_next = lax.rsqrt(mean * (1.0 / 2048) + epsilon)
    qkv_ref[...] = (projected * r_next)[0:T].astype(bf16)

    for finish in pending:
        finish()


def hand_over(hid_in, qkv_in, hid_out, qkv_out, sem):
    copies = [
        pltpu.make_async_copy(hid_in, hid_out, sem.at[0]),
        pltpu.make_async_copy(qkv_in, qkv_out, sem.at[1]),
    ]
    for copy in copies:
        copy.start()
    for copy in copies:
        copy.wait()


def per_device(
    queries,
    fresh_pair,
    cache_blocks,
    block_table,
    lengths,
    residual,
    w_output,
    norm_gain,
    routes,
    route_gates,
    w_gate_up,
    w_down,
    shared_gate_up,
    shared_down,
    next_gain,
    w_query_key_value,
):
    vmem = pl.BlockSpec(memory_space=pltpu.VMEM)
    hbm = pl.BlockSpec(memory_space=pltpu.HBM)
    return pl.pallas_call(
        kernel,
        out_shape=(pltpu.VMEM((T, 2048), bf16), pltpu.VMEM((T, 768), bf16)),
        in_specs=[hbm] * 16,
        out_specs=(vmem, vmem),
        scratch_shapes=[
            pltpu.VMEM((T, CW), bf16),
            pltpu.VMEM((T, 2, CW), bf16),
            pltpu.VMEM((T, 2048), bf16),
            pltpu.VMEM((2048,), bf16),
            pltpu.VMEM((2048,), bf16),
            pltpu.VMEM((320,), i32),
            pltpu.VMEM((6, 320), i32),
            pltpu.VMEM((6, 320), f32),
            pltpu.VMEM((384, 256), i32),
            pltpu.VMEM((BLK, 2, BS, CW), bf16),
            pltpu.VMEM((CW, 2048), bf16),
            pltpu.VMEM((2, CW, 2, FFE), bf16),
            pltpu.VMEM((2, FFE, CW), bf16),
            pltpu.VMEM((1, CW, 2, FFE), bf16),
            pltpu.VMEM((1, FFE, CW), bf16),
            pltpu.VMEM((2048, 768), bf16),
            pltpu.VMEM((2, 2 * CW, FFE), bf16),
            pltpu.VMEM((2 * CW, FFE), bf16),
            pltpu.VMEM((NP, RP, 128), bf16),
            pltpu.VMEM((NP, RP, 128), bf16),
            pltpu.VMEM((NP, RP, 128), bf16),
            pltpu.VMEM((NH, TP, CW), bf16),
            pltpu.VMEM((NH, TP, CW), bf16),
            pltpu.VMEM((NP, TP, 128), bf16),
            pltpu.VMEM((NP, TP, 128), bf16),
            pltpu.VMEM((NH, TP, EW), bf16),
            pltpu.VMEM((4, TP, EW), bf16),
            pltpu.VMEM((4, TP, EW), bf16),
            pltpu.VMEM((NH, TP, FFE), bf16),
            pltpu.VMEM((NH, TP, SW), bf16),
            pltpu.VMEM((NH, TP, SW), bf16),
            pltpu.VMEM((NH, TP, CW), bf16),
            pltpu.VMEM((NP, 8, 128), f32),
            pltpu.VMEM((NP, 8, 128), f32),
            pltpu.VMEM((NH, TP, CW), bf16),
            pltpu.SemaphoreType.DMA((16,)),
            pltpu.SemaphoreType.DMA((8,)),
            pltpu.SemaphoreType.DMA((8,)),
            pltpu.SemaphoreType.DMA((2, 4)),
            pltpu.SemaphoreType.DMA((2, 4, 4)),
            pltpu.SemaphoreType.DMA((2, 2)),
            pltpu.SemaphoreType.DMA((2, 4, 2)),
            pltpu.SemaphoreType.DMA((NH,)),
        ],
        compiler_params=pltpu.CompilerParams(
            collective_id=0, has_side_effects=True, vmem_limit_bytes=58 << 20
        ),
    )(
        queries,
        fresh_pair,
        residual,
        norm_gain,
        next_gain,
        lengths,
        routes.T,
        route_gates.T,
        block_table,
        cache_blocks,
        w_output,
        w_gate_up,
        w_down,
        shared_gate_up,
        shared_down,
        w_query_key_value,
    )


def solution(mesh):
    in_specs = (
        P("pool", "head"),
        P("pool", None, "head"),
        P("pool", None, None, "head"),
        P(),
        P(),
        P("pool", None),
        P("head", None),
        P(),
        P(),
        P(),
        P("pool", "head", None, None),
        P("pool", None, "head"),
        P(None, "head", None, None),
        P(None, None, "head"),
        P(),
        P(None, "head"),
    )
    out_specs = (P("pool", None), P("pool", "head"))
    return jax.shard_map(
        per_device, mesh=mesh, in_specs=in_specs, out_specs=out_specs, check_vma=False
    )
```

```python
import math

import jax
import jax.numpy as jnp
from jax import lax
from jax.experimental import pallas as pl
from jax.experimental.pallas import tpu as pltpu
from jax.sharding import PartitionSpec as P

HD = 128
NP = 32
NH = 8
T = 10
TP = 16
CW = 256
FFE = 1408
BLK = 36
BP = 40
BS = 64
TOK = BLK * BS
RP = 24
EW = 2 * FFE + 128
SW = 2 * CW + 128
epsilon = 1e-06
low = -1e30
f32 = jnp.float32
bf16 = jnp.bfloat16
i32 = jnp.int32
MESH = pl.DeviceIdType.MESH


def iota(shape, dim):
    return lax.broadcasted_iota(i32, shape, dim)


def dot(a, b):
    return jnp.dot(a, b, preferred_element_type=f32)


def dot_t(a, b):
    return lax.dot_general(a, b, (((0,), (0,)), ((), ())), preferred_element_type=f32)


def hot(cond):
    return jnp.where(cond, 1.0, 0.0).astype(bf16)


def kernel(
    queries_hbm,
    fresh_hbm,
    residual_hbm,
    gain_hbm,
    next_gain_hbm,
    len_hbm,
    routes_hbm,
    gates_hbm,
    table_hbm,
    cache_hbm,
    wout_hbm,
    wgu_hbm,
    wdn_hbm,
    sgu_hbm,
    sdn_hbm,
    wqkv_hbm,
    hid_ref,
    qkv_ref,
    queries_v,
    fresh_v,
    residual_v,
    gain_v,
    next_gain_v,
    len_v,
    routes_v,
    gates_v,
    table_v,
    cache_v,
    wout_v,
    wgu_v,
    wdn_v,
    sgu_v,
    sdn_v,
    wqkv_v,
    wgu2,
    sgu2,
    abuf,
    bsend,
    bbuf,
    csend,
    cbuf,
    dsend,
    dbuf,
    esend,
    edown,
    eup,
    fbuf,
    sbuf,
    ssend,
    tbuf,
    gsend,
    gbuf,
    hbuf,
    lsem,
    ssem,
    rsem,
    essem,
    ersem,
    fssem,
    frsem,
    hrsem,
    fdsem,
    fdrsem,
):
    p = lax.axis_index("pool")
    h = lax.axis_index("head")

    loads = {
        name: pltpu.make_async_copy(src, dst, lsem.at[n])
        for n, (name, src, dst) in enumerate(
            [
                ("queries", queries_hbm, queries_v),
                ("table", table_hbm, table_v.at[pl.ds(0, 320)]),
                ("len", len_hbm, len_v),
                ("cache", cache_hbm, cache_v),
                ("routes", routes_hbm, routes_v),
                ("gates", gates_hbm, gates_v),
                ("fresh", fresh_hbm, fresh_v),
                ("sgu", sgu_hbm, sgu_v),
                ("wgu", wgu_hbm, wgu_v),
                ("wout", wout_hbm, wout_v),
                ("residual", residual_hbm, residual_v),
                ("gain", gain_hbm, gain_v),
                ("wdn", wdn_hbm, wdn_v),
                ("sdn", sdn_hbm, sdn_v),
                ("next_gain", next_gain_hbm, next_gain_v),
                ("wqkv", wqkv_hbm, wqkv_v),
            ]
        )
    }
    loads["queries"].start()

    barrier = pltpu.get_barrier_semaphore()

    def greet_pool(k, carry):
        pl.semaphore_signal(
            barrier, inc=1, device_id={"pool": lax.rem(p + k, NP)}, device_id_type=MESH
        )
        return carry

    def greet_head(k, carry):
        pl.semaphore_signal(
            barrier, inc=1, device_id={"head": lax.rem(h + k, NH)}, device_id_type=MESH
        )
        return carry

    lax.fori_loop(1, NP, greet_pool, 0)
    lax.fori_loop(1, NH, greet_head, 0)
    for name in ("table", "len"):
        loads[name].start()

    waited = set()
    pending = []

    def arrive(*names):
        for name in names:
            loads[name].wait()
            waited.add(name)


    def send_pool(src, buf, n):
        def one(k, carry):
            j = lax.rem(p + k, NP)
            pltpu.make_async_remote_copy(
                src_ref=src(j),
                dst_ref=buf.at[p],
                send_sem=ssem.at[n],
                recv_sem=rsem.at[n],
                device_id={"pool": j},
                device_id_type=MESH,
            ).start()
            return carry

        lax.fori_loop(1, NP, one, 0)
        pending.append(lambda: wait(buf, ssem, n, NP - 1))

    def send_head(src, buf, n):
        def one(k, carry):
            j = lax.rem(h + k, NH)
            pltpu.make_async_remote_copy(
                src_ref=src(j),
                dst_ref=buf.at[h],
                send_sem=ssem.at[n],
                recv_sem=rsem.at[n],
                device_id={"head": j},
                device_id_type=MESH,
            ).start()
            return carry

        lax.fori_loop(1, NH, one, 0)
        pending.append(lambda: wait(buf, ssem, n, NH - 1))

    def wait(buf, sem, n, count):
        view = buf.at[pl.ds(0, count)]
        pltpu.make_async_copy(view, view, sem.at[n]).wait()

    arrive("queries")
    rows_pad = jnp.zeros((TP - T, CW), f32)
    q_own = jnp.concatenate([queries_v[...].astype(f32), rows_pad], axis=0)
    abuf[p] = jnp.concatenate(
        [q_own[0:T, 0:HD], q_own[0:T, HD:CW], rows_pad[0:4, 0:HD]], axis=0
    ).astype(bf16)
    pl.semaphore_wait(barrier, NP - 1 + NH - 1)
    send_pool(lambda j: abuf.at[p], abuf, 0)
    for name in loads:
        if name not in ("queries", "table", "len"):
            loads[name].start()

    table_v[pl.ds(320, 64), :] = jnp.zeros((64, 256), i32)
    arrive("table", "len")
    table = table_v[...].astype(f32)
    heads_t = jnp.transpose(table[:, 0:128])
    lane = iota((1, 384), 1)
    real = lane < 320
    blk = iota((BP, 1), 0)
    ids = jnp.where(blk < BLK, blk + BLK * p, -7).astype(f32)
    len_row = jnp.concatenate(
        [len_v[...].reshape(1, 320).astype(f32), jnp.zeros((1, 64), f32)], axis=1
    )
    hot0 = jnp.where((heads_t[0:1] == ids) & real, 1.0, 0.0)
    hot1 = jnp.where((heads_t[1:2] == ids) & real, 1.0, 0.0)
    is_long = (heads_t[2:3] >= 0.0) & real
    lane_f = lane.astype(f32)
    first = jnp.min(jnp.where(is_long, lane_f, 1e6), axis=1, keepdims=True)
    last = jnp.max(jnp.where(is_long, lane_f, -1.0), axis=1, keepdims=True)
    row_f = iota((384, 1), 0).astype(f32)
    col = iota((1, 256), 1)
    owned = hot0 + hot1
    rank = jnp.sum(hot1, axis=1, keepdims=True)
    for which in (first, last):
        listed = jnp.sum(jnp.where(row_f == which, table, 0.0), axis=0, keepdims=True)
        match = jnp.where((listed == ids) & (col >= 2), 1.0, 0.0)
        found = jnp.max(match, axis=1, keepdims=True)
        rank = rank + jnp.sum(match * col.astype(f32), axis=1, keepdims=True)
        owned = owned + found * jnp.where(lane_f == which, 1.0, 0.0)
    owner_len = jnp.sum(owned * len_row, axis=1, keepdims=True)
    live = jnp.clip(owner_len - BS * rank, 0.0, float(BS))
    mine = owned > 0.5
    blk_f = blk.astype(f32)
    lead = jnp.min(jnp.where(mine, blk_f, 99.0), axis=0, keepdims=True)
    rep = jnp.max(jnp.where(mine & (lead == blk_f), 1.0, 0.0), axis=1, keepdims=True)
    r_in = iota((384, NP * RP), 0)
    group = lax.shift_right_logical(r_in * 205, 11)
    l_out = iota((384, NP * RP), 1)
    owned_b = owned.astype(bf16)
    hot_a = dot(owned_b, hot((l_out == r_in + 14 * group) & (r_in < 320)))
    hot_q = dot(owned_b, hot((l_out == RP * group + 20) & (r_in < 320)))
    hot_b = pltpu.roll(hot_a, T, 1)
    place = jnp.concatenate(
        [hot_a, hot_b, hot_q] + [pltpu.roll(hot_q, q, 1) for q in (1, 2, 3)], axis=0
    )
    place_t = jnp.transpose(place).astype(bf16)
    place = place[0 : 2 * BP].astype(bf16)
    lane_k = lane - 10 * lax.shift_right_logical(lane * 205, 11)
    which_row = jnp.sum(owned * lane_k.astype(f32), axis=1, keepdims=True)
    at_row = iota((BP, 128), 1) == which_row.astype(i32)
    tok = iota((BP, TOK), 1)
    start = blk * BS
    usable = (tok >= start) & (tok < start + live.astype(i32))

    arrive("sgu")
    for t in range(11):
        sgu2[:, t * 128 : (t + 1) * 128] = sgu_v[0, :, :, t * 128 : (t + 1) * 128].reshape(
            2 * CW, 128
        )
    arrive("cache")

    wait(abuf, rsem, 0, NP - 1)
    scale = 1.0 / math.sqrt(HD)
    all_queries = abuf[...].reshape(NP * RP, HD)
    none = jnp.zeros((BP, HD), f32)
    picked = dot(place, all_queries)
    picked = jnp.concatenate(
        [
            jnp.concatenate([picked[0:BP], none], axis=1),
            jnp.concatenate([none, picked[BP:]], axis=1),
        ],
        axis=0,
    ).astype(bf16)
    keys = cache_v[:, 0].reshape(TOK, CW)
    scores = (
        lax.dot_general(picked, keys, (((1,), (1,)), ((), ())), preferred_element_type=f32) * scale
    )
    shifts = []
    totals = []
    weights = []
    for hd in range(2):
        score = jnp.where(usable, scores[hd * BP : (hd + 1) * BP], low)
        top = jnp.max(score, axis=1, keepdims=True)
        req_top = jnp.max(jnp.where(mine, top, low), axis=0, keepdims=True)
        shift = jnp.max(jnp.where(mine, req_top, low), axis=1, keepdims=True)
        shift = shift.astype(bf16).astype(f32)
        weight = jnp.where(usable, jnp.exp(score - shift), 0.0)
        totals.append(jnp.sum(weight, axis=1, keepdims=True))
        shifts.append(shift)
        weights.append(weight.astype(bf16))
    values = cache_v[:, 1].reshape(TOK, CW)
    both_parts = dot(jnp.concatenate(weights, axis=0), values)
    parts = [both_parts[0:BP, 0:HD], both_parts[BP:, HD:CW]]
    tails = [jnp.where(rep > 0.5, shift, 0.0) for shift in shifts] + totals
    message = jnp.concatenate(
        parts + [jnp.where(at_row, tail, 0.0) for tail in tails], axis=0
    ).astype(bf16)
    bsend[...] = dot(place_t, message).astype(bf16).reshape(NP, RP, 128)
    bbuf[p] = bsend[p]
    send_pool(lambda j: bsend.at[j], bbuf, 1)

    arrive("routes", "gates")
    own_lane = iota((TP, 320), 1)
    own_row = iota((TP, 320), 0)
    own = (own_lane == own_row + T * p) & (own_row < T)
    row16 = iota((TP, 1), 0)
    lane_e = iota((TP, 128), 1)
    named = jnp.zeros((TP, 128), f32)
    gate = jnp.zeros((TP, 128), f32)
    routes_t = routes_v[...].astype(f32)
    gates_t = gates_v[...]
    for k in range(6):
        pick = jnp.sum(jnp.where(own, routes_t[k : k + 1], 0.0), axis=1, keepdims=True)
        pick = jnp.where(row16 < T, pick, -1.0).astype(i32)
        amount = jnp.sum(jnp.where(own, gates_t[k : k + 1], 0.0), axis=1, keepdims=True)
        named = named + jnp.where(lane_e == pick, 1.0, 0.0)
        gate = gate + jnp.where(lane_e == pick, amount, 0.0)
    earlier = hot(iota((TP, TP), 1) < iota((TP, TP), 0))
    order = dot(earlier, named.astype(bf16))
    gate_hi = gate.astype(bf16)
    gate_lo = (gate - gate_hi.astype(f32)).astype(bf16)
    table_nr = jnp.concatenate([named, order], axis=0).astype(bf16)
    l_g = iota((128, 256), 1)
    exp_g = hot(
        iota((128, 256), 0)
        == 2 * lax.shift_right_logical(l_g, 3) + (lax.shift_right_logical(l_g, 1) & 1)
    )
    wide = dot(jnp.concatenate([table_nr, gate_hi, gate_lo], axis=0), exp_g)
    l8 = iota((TP, 256), 1)
    sel = (wide[0:TP] > 0.5) & (wide[TP : 2 * TP].astype(i32) == (l8 & 1))
    half = lax.shift_right_logical(l8, 2) & 1
    sel32 = jnp.transpose(
        jnp.concatenate([jnp.where(sel & (half == c), 1.0, 0.0) for c in range(2)], axis=0)
    ).astype(bf16)
    combine = jnp.concatenate(
        [
            jnp.where(sel & (half == c), wide[(2 + part) * TP : (3 + part) * TP], 0.0)
            for c in range(2)
            for part in range(2)
        ],
        axis=0,
    ).astype(bf16)
    arrive("wgu")
    for t in range(11):
        wgu2[0, :, t * 128 : (t + 1) * 128] = wgu_v[0, :, :, t * 128 : (t + 1) * 128].reshape(
            2 * CW, 128
        )
    arrive("wout", "fresh", "residual", "gain")

    l_row = iota((128, NP * RP), 1)
    r_row = iota((128, NP * RP), 0)
    take_sums = hot(l_row == (r_row & 31) * RP + 20 + lax.shift_right_logical(r_row, 5))
    l_row = iota((64, NP * RP), 1)
    r_row = iota((64, NP * RP), 0)
    source = lax.shift_right_logical(l_row * 2731, 16)
    keep = (l_row - RP * source) == (r_row & 15) + T * lax.shift_right_logical(r_row, 5)
    widen = hot(source[0:NP] == r_row[0:NP])
    diagonal = iota((TP, 128), 0) == iota((TP, 128), 1)
    k_own = jnp.concatenate([fresh_v[:, 0, :].astype(f32), rows_pad], axis=0)
    v_own = jnp.concatenate([fresh_v[:, 1, :].astype(f32), rows_pad], axis=0)
    wait(bbuf, rsem, 1, NP - 1)
    received = bbuf[...].reshape(NP * RP, 128)
    sums = dot(take_sums, received)
    columns = []
    fresh_ws = []
    for hd in range(2):
        cols = slice(hd * HD, (hd + 1) * HD)
        fresh = jnp.sum(q_own[:, cols] * k_own[:, cols], axis=1, keepdims=True) * scale
        fresh = jnp.sum(jnp.where(diagonal, fresh, 0.0), axis=0, keepdims=True)
        total = sums[(2 + hd) * NP : (3 + hd) * NP]
        tops = jnp.where(total > 0.0, sums[hd * NP : (hd + 1) * NP], low)
        peak = jnp.maximum(jnp.max(tops, axis=0, keepdims=True), fresh)
        share = jnp.exp(tops - peak)
        fresh_w = jnp.exp(fresh - peak)
        denom = jnp.sum(share * total, axis=0, keepdims=True) + fresh_w
        share = (share / denom)[:, 0:TP]
        share_hi = share.astype(bf16).astype(f32)
        columns += [share_hi, share - share_hi]
        fresh_ws.append(
            jnp.sum(jnp.where(diagonal, fresh_w / denom, 0.0), axis=1, keepdims=True)
        )
    spread_w = dot_t(jnp.concatenate(columns, axis=1).astype(bf16), widen)
    mixed = dot(jnp.where(keep, spread_w, 0.0).astype(bf16), received)
    joined = [
        mixed[2 * hd * TP : (2 * hd + 1) * TP]
        + mixed[(2 * hd + 1) * TP : (2 * hd + 2) * TP]
        + fresh_ws[hd] * v_own[:, hd * HD : (hd + 1) * HD]
        for hd in range(2)
    ]
    attended = jnp.concatenate(joined, axis=1)[0:T]
    blank = jnp.zeros((T, CW), f32)
    attended = jnp.concatenate(
        [
            jnp.concatenate([attended, blank], axis=1),
            jnp.concatenate([blank, attended], axis=1),
            jnp.zeros((RP - 2 * T, 2 * CW), f32),
        ],
        axis=0,
    ).astype(bf16)
    for j in range(NH):
        block = jnp.concatenate(
            [
                wout_v[:, j * CW : j * CW + 128],
                wout_v[:, j * CW + 128 : (j + 1) * CW],
            ],
            axis=0,
        )
        csend[j] = dot(attended, block).astype(bf16)
    cbuf[h] = csend[h]
    send_head(lambda j: csend.at[j], cbuf, 2)

    for t in range(6):
        wgu2[1, :, t * 128 : (t + 1) * 128] = wgu_v[1, :, :, t * 128 : (t + 1) * 128].reshape(
            2 * CW, 128
        )

    wait(cbuf, rsem, 2, NH - 1)
    own_cols = pl.ds(pl.multiple_of(h * CW, CW), CW)
    after = jnp.concatenate([residual_v[:, own_cols].astype(f32), rows_pad], axis=0)
    summed = cbuf[0].astype(f32)
    for j in range(1, NH):
        summed = summed + cbuf[j].astype(f32)
    after = after + jnp.concatenate(
        [jnp.concatenate([summed[0:T], summed[T : 2 * T]], axis=1), rows_pad], axis=0
    )
    gain_own = gain_v[own_cols].astype(f32).reshape(1, CW)
    scaled = (after * gain_own).astype(bf16)
    square = jnp.sum(after * after, axis=1, keepdims=True)
    square_hi = square.astype(bf16).astype(f32)
    lane_t = iota((TP, 128), 1)
    squares = jnp.where(lane_t == 0, square_hi, jnp.where(lane_t == 1, square - square_hi, 0.0))
    rows32 = jnp.concatenate([scaled[:, 0:128], scaled[:, 128:256]], axis=0)
    dsend[...] = dot(sel32, rows32).astype(bf16).reshape(NP, 8, 128)
    dbuf[p] = dsend[p]
    send_pool(lambda j: dsend.at[j], dbuf, 3)

    d_in = iota((CW, 2 * CW), 0)
    d_out = iota((CW, 2 * CW), 1)
    to_gate = hot(d_out == 2 * d_in)
    to_up = hot(d_out == 2 * d_in + 1)
    spread_own = jnp.concatenate([dot(scaled, to_gate), dot(scaled, to_up)], axis=0).astype(bf16)
    shared = dot(spread_own, sgu2[...]).astype(bf16)
    for j in range(NH):
        width = min(CW, max(0, FFE - j * CW))
        for c in range(2):
            at = c * CW
            if width > 0:
                ssend[j, :, at : at + width] = shared[
                    c * TP : (c + 1) * TP, j * CW : j * CW + width
                ]
            if width < CW:
                ssend[j, :, at + width : at + CW] = jnp.zeros((TP, CW - width), bf16)
        ssend[j, :, 2 * CW :] = squares.astype(bf16)
    sbuf[h] = ssend[h]
    send_head(lambda j: ssend.at[j], sbuf, 6)
    for t in range(6, 11):
        wgu2[1, :, t * 128 : (t + 1) * 128] = wgu_v[1, :, :, t * 128 : (t + 1) * 128].reshape(
            2 * CW, 128
        )
    slot = iota((128, 256), 0)
    from_row = (
        (lax.shift_right_logical(slot, 1) & 31) * 8
        + lax.shift_right_logical(slot, 6) * 2
        + (slot & 1)
    )
    source = iota((128, 256), 1)
    gathers = [hot(source == from_row + 4 * c) for c in range(2)]
    lane_s = iota((128, 128), 1)

    wait(dbuf, rsem, 3, NP - 1)
    arrived = dbuf[...].reshape(NP * 8, 128)
    rows = jnp.concatenate([dot(gathers[0], arrived), dot(gathers[1], arrived)], axis=1)
    plain = rows / gain_own
    square = jnp.sum(plain * plain, axis=1, keepdims=True)
    square_hi = square.astype(bf16).astype(f32)
    row_squares = jnp.where(
        lane_s == 0, square_hi, jnp.where(lane_s == 1, square - square_hi, 0.0)
    )
    rows = rows.astype(bf16)
    for_gate = dot(rows, to_gate).astype(bf16)
    for_up = dot(rows, to_up).astype(bf16)
    boths = [
        jnp.concatenate([for_gate[e * 64 : (e + 1) * 64], for_up[e * 64 : (e + 1) * 64]], axis=0)
        for e in range(2)
    ]

    def ring_copy(src, dst, send_sem, recv_sem, to):
        return pltpu.make_async_remote_copy(
            src_ref=src,
            dst_ref=dst,
            send_sem=send_sem,
            recv_sem=recv_sem,
            device_id={"head": to},
            device_id_type=MESH,
        )

    down = lax.rem(h + NH - 1, NH)
    up = lax.rem(h + 1, NH)
    e_parts = [(0, 896), (896, 1664), (1664, 2432), (2432, 2944)]
    f_cols = [(0, 384), (384, 768), (768, 1152), (1152, 1408)]
    sides = ((down, edown, -1), (up, eup, 1))

    def off(by):
        return lax.rem(h + by + NH, NH)

    def e_copy(n, way, chunk, slot, to):
        lo, hi = e_parts[n]
        land = sides[way][1]
        return ring_copy(
            esend.at[chunk, :, pl.ds(lo, hi - lo)],
            land.at[slot, :, pl.ds(lo, hi - lo)],
            essem.at[way, n],
            ersem.at[way, slot, n],
            to,
        )

    def e_take(n, way, slot):
        lo, hi = e_parts[n]
        e_copy(n, way, h, slot, down).wait_recv()
        return sides[way][1][slot, :, lo:hi].astype(f32)

    for n, (lo, _) in enumerate(e_parts):
        c_lo, c_hi = f_cols[n]
        wide = c_hi - c_lo
        for e in range(2):
            partial = dot(boths[e], wgu2[e, :, c_lo:c_hi]).astype(bf16)
            for j in range(4):
                for c in range(2):
                    esend[4 * e + j, :, lo + c * wide : lo + (c + 1) * wide] = partial[
                        c * 64 + j * TP : c * 64 + (j + 1) * TP
                    ]
        if n == 0:
            for j in range(NH):
                esend[j, :, 768:896] = row_squares[j * TP : (j + 1) * TP].astype(bf16)
        for way, (_, _, sign) in enumerate(sides):
            if n % 2 == way:
                e_copy(n, way, off(4 * sign), 1, off(2 * sign)).start()
            e_copy(n, way, off(3 * sign), 0, off(sign)).start()
            e_copy(n, way, off(sign), 2, off(sign)).start()

    for n, (lo, hi) in enumerate(e_parts):
        for way, (_, _, sign) in enumerate(sides):
            chunk = off(2 * sign)
            passed = esend[chunk, :, lo:hi].astype(f32) + e_take(n, way, 0)
            if n % 2 == way:
                passed = passed + e_take(n, way, 1)
            esend[chunk, :, lo:hi] = passed.astype(bf16)
            e_copy(n, way, chunk, 3, chunk).start()

    def e_drain():
        for way, land in enumerate((edown, eup)):
            for n, (lo, hi) in enumerate(e_parts):
                view = land.at[pl.ds(0, 4 if n % 2 == way else 3), :, pl.ds(lo, hi - lo)]
                pltpu.make_async_copy(view, view, essem.at[way, n]).wait()

    pending.append(e_drain)
    f_parts = [(0, 768)]
    f_late = [(768, 1152), (1152, FFE)]

    def f_direct(n, k):
        lo, hi = f_late[n]
        view = fbuf.at[h, :, pl.ds(lo, hi - lo)]
        return ring_copy(view, view, fdsem.at[n], fdrsem.at[n, k], off(k))


    def f_send(n, way, origin, hop):
        lo, hi = f_parts[n]
        sign = sides[way][2]
        view = fbuf.at[off(-sign * origin), :, pl.ds(lo, hi - lo)]
        ring_copy(
            view, view, fssem.at[way, n], frsem.at[way, origin + hop - 1, n], off(sign * hop)
        ).start()

    def f_wait(n, way, origin):
        lo, hi = f_parts[n]
        view = fbuf.at[off(-sides[way][2] * origin), :, pl.ds(lo, hi - lo)]
        ring_copy(
            view, view, fssem.at[way, n], frsem.at[way, origin - 1, n], down
        ).wait_recv()

    r_slot = None
    for n, (lo, hi) in enumerate(e_parts):
        piece = esend[h, :, lo:hi].astype(f32)
        for way in range(2):
            piece = piece + e_take(n, way, 2) + e_take(n, way, 3)
        c_lo, c_hi = f_cols[n]
        wide = c_hi - c_lo
        if n == 0:
            r_slot = lax.rsqrt((piece[:, 768:769] + piece[:, 769:770]) * (1.0 / 2048) + epsilon)
        g = piece[:, 0:wide] * r_slot
        u = piece[:, wide : 2 * wide] * r_slot
        fbuf[h, :, c_lo:c_hi] = (g / (1.0 + jnp.exp(-g)) * u).astype(bf16)
        if n == 1:
            for hop in (2, 1):
                for way in range(2):
                    f_send(0, way, 0, hop)
        if n >= 2:
            for k in (4, 3, 5, 2, 6, 1, 7):
                f_direct(n - 2, k).start()
    for n in range(1):
        for way in range(2):
            f_wait(n, way, 2)
            if n == way:
                f_send(n, way, 2, 2)
            f_send(n, way, 2, 1)

    wait(sbuf, rsem, 6, NH - 1)
    total = sbuf[0].astype(f32)
    for j in range(1, NH):
        total = total + sbuf[j].astype(f32)
    ss = total[:, 2 * CW :]
    r_own = lax.rsqrt((ss[:, 0:1] + ss[:, 1:2]) * (1.0 / 2048) + epsilon)
    g = total[:, 0:CW] * r_own
    u = total[:, CW : 2 * CW] * r_own
    tbuf[h] = (g / (1.0 + jnp.exp(-g)) * u).astype(bf16)
    send_head(lambda j: tbuf.at[h], tbuf, 7)

    def f_drain():
        for way in range(2):
            for n, (lo, hi) in enumerate(f_parts):
                view = fbuf.at[pl.ds(0, 4 if n == way else 3), :, pl.ds(lo, hi - lo)]
                pltpu.make_async_copy(view, view, fssem.at[way, n]).wait()

    pending.append(f_drain)

    def f_late_drain():
        for n, (lo, hi) in enumerate(f_late):
            view = fbuf.at[pl.ds(0, NH - 1), :, pl.ds(lo, hi - lo)]
            pltpu.make_async_copy(view, view, fdsem.at[n]).wait()

    pending.append(f_late_drain)
    arrive("wdn", "sdn", "next_gain", "wqkv")
    back = iota((256, 256), 0)
    kk = iota((256, 256), 1)
    slot_of = (
        (lax.shift_right_logical(back, 1) & 1) * 64
        + lax.shift_right_logical(back, 3) * 2
        + (back & 1)
        + (lax.shift_right_logical(back, 2) & 1) * 128
    )
    returns = hot(kk == slot_of)

    outs = [0.0, 0.0]
    for n, (lo, hi) in enumerate([(0, 768), (768, FFE)]):
        if n == 0:
            for way in range(2):
                for origin in (1, 3, 4) if way == 0 else (1, 3):
                    f_wait(0, way, origin)
        else:
            for late, (a, b) in enumerate(f_late):
                for k in range(1, NH):
                    view = fbuf.at[off(-k), :, pl.ds(a, b - a)]
                    ring_copy(view, view, fdsem.at[late], fdrsem.at[late, k], down).wait_recv()
        for e in range(2):
            rows_e = fbuf[4 * e : 4 * e + 4, :, lo:hi].reshape(64, hi - lo)
            outs[e] = outs[e] + dot(rows_e, wdn_v[e, lo:hi, :])
    outs = [out.astype(bf16) for out in outs]
    stacked = jnp.concatenate(
        [outs[0][:, 0:128], outs[1][:, 0:128], outs[0][:, 128:256], outs[1][:, 128:256]], axis=0
    )
    gsend[...] = dot(returns, stacked).astype(bf16).reshape(NP, 8, 128)
    gbuf[p] = gsend[p]
    send_pool(lambda j: gsend.at[j], gbuf, 4)
    wait(tbuf, rsem, 7, NH - 1)
    for j in range(6):
        width = min(CW, FFE - j * CW)
        after = after + dot(tbuf[j, :, 0:width], sdn_v[0, j * CW : j * CW + width, :])
    wait(gbuf, rsem, 4, NP - 1)
    routed = dot(combine, gbuf[...].reshape(NP * 8, 128))
    routed = jnp.concatenate(
        [routed[0:TP] + routed[TP : 2 * TP], routed[2 * TP : 3 * TP] + routed[3 * TP :]], axis=1
    )
    final = (after + routed)[0:T]
    hbuf[h] = jnp.concatenate(
        [final[:, 0:128], final[:, 128:], jnp.zeros((RP - 2 * T, 128), f32)], axis=0
    ).astype(bf16)

    def h_copy(k):
        return pltpu.make_async_remote_copy(
            src_ref=hbuf.at[h],
            dst_ref=hbuf.at[h],
            send_sem=ssem.at[5],
            recv_sem=hrsem.at[k],
            device_id={"head": off(k)},
            device_id_type=MESH,
        )

    for k in (4, 3, 5, 2, 6, 1, 7):
        h_copy(k).start()
    pending.append(lambda: wait(hbuf, ssem, 5, NH - 1))

    mean = jnp.zeros((T, 1), f32)
    projected = jnp.zeros((T, 768), f32)
    for k in (0, 1, 7, 2, 6, 3, 5, 4):
        j = off(-k)
        if k > 0:
            view = hbuf.at[j]
            pltpu.make_async_copy(view, view, hrsem.at[k]).wait()
        at = pl.multiple_of(j * CW, CW)
        piece = hbuf[j].astype(f32)
        piece = jnp.concatenate([piece[0:T], piece[T : 2 * T]], axis=1)
        hid_ref[:, pl.ds(at, CW)] = piece.astype(bf16)
        mean = mean + jnp.sum(piece * piece, axis=1, keepdims=True)
        piece = piece * next_gain_v[pl.ds(at, CW)].astype(f32).reshape(1, CW)
        projected = projected + dot(piece.astype(bf16), wqkv_v[pl.ds(at, CW), :])
    r_next = lax.rsqrt(mean * (1.0 / 2048) + epsilon)
    qkv_ref[...] = (projected * r_next).astype(bf16)

    for finish in pending:
        finish()


def hand_over(hid_in, qkv_in, hid_out, qkv_out, sem):
    copies = [
        pltpu.make_async_copy(hid_in, hid_out, sem.at[0]),
        pltpu.make_async_copy(qkv_in, qkv_out, sem.at[1]),
    ]
    for copy in copies:
        copy.start()
    for copy in copies:
        copy.wait()


def per_device(
    queries,
    fresh_pair,
    cache_blocks,
    block_table,
    lengths,
    residual,
    w_output,
    norm_gain,
    routes,
    route_gates,
    w_gate_up,
    w_down,
    shared_gate_up,
    shared_down,
    next_gain,
    w_query_key_value,
):
    vmem = pl.BlockSpec(memory_space=pltpu.VMEM)
    hbm = pl.BlockSpec(memory_space=pltpu.HBM)
    return pl.pallas_call(
        kernel,
        out_shape=(pltpu.VMEM((T, 2048), bf16), pltpu.VMEM((T, 768), bf16)),
        in_specs=[hbm] * 16,
        out_specs=(vmem, vmem),
        scratch_shapes=[
            pltpu.VMEM((T, CW), bf16),
            pltpu.VMEM((T, 2, CW), bf16),
            pltpu.VMEM((T, 2048), bf16),
            pltpu.VMEM((2048,), bf16),
            pltpu.VMEM((2048,), bf16),
            pltpu.VMEM((320,), i32),
            pltpu.VMEM((6, 320), i32),
            pltpu.VMEM((6, 320), f32),
            pltpu.VMEM((384, 256), i32),
            pltpu.VMEM((BLK, 2, BS, CW), bf16),
            pltpu.VMEM((CW, 2048), bf16),
            pltpu.VMEM((2, CW, 2, FFE), bf16),
            pltpu.VMEM((2, FFE, CW), bf16),
            pltpu.VMEM((1, CW, 2, FFE), bf16),
            pltpu.VMEM((1, FFE, CW), bf16),
            pltpu.VMEM((2048, 768), bf16),
            pltpu.VMEM((2, 2 * CW, FFE), bf16),
            pltpu.VMEM((2 * CW, FFE), bf16),
            pltpu.VMEM((NP, RP, 128), bf16),
            pltpu.VMEM((NP, RP, 128), bf16),
            pltpu.VMEM((NP, RP, 128), bf16),
            pltpu.VMEM((NH, RP, 128), bf16),
            pltpu.VMEM((NH, RP, 128), bf16),
            pltpu.VMEM((NP, 8, 128), bf16),
            pltpu.VMEM((NP, 8, 128), bf16),
            pltpu.VMEM((NH, TP, EW), bf16),
            pltpu.VMEM((4, TP, EW), bf16),
            pltpu.VMEM((4, TP, EW), bf16),
            pltpu.VMEM((NH, TP, FFE), bf16),
            pltpu.VMEM((NH, TP, SW), bf16),
            pltpu.VMEM((NH, TP, SW), bf16),
            pltpu.VMEM((NH, TP, CW), bf16),
            pltpu.VMEM((NP, 8, 128), bf16),
            pltpu.VMEM((NP, 8, 128), bf16),
            pltpu.VMEM((NH, RP, 128), bf16),
            pltpu.SemaphoreType.DMA((16,)),
            pltpu.SemaphoreType.DMA((8,)),
            pltpu.SemaphoreType.DMA((8,)),
            pltpu.SemaphoreType.DMA((2, 4)),
            pltpu.SemaphoreType.DMA((2, 4, 4)),
            pltpu.SemaphoreType.DMA((2, 2)),
            pltpu.SemaphoreType.DMA((2, 4, 2)),
            pltpu.SemaphoreType.DMA((NH,)),
            pltpu.SemaphoreType.DMA((2,)),
            pltpu.SemaphoreType.DMA((2, NH)),
        ],
        compiler_params=pltpu.CompilerParams(
            collective_id=0, has_side_effects=True, vmem_limit_bytes=58 << 20
        ),
    )(
        queries,
        fresh_pair,
        residual,
        norm_gain,
        next_gain,
        lengths,
        routes.T,
        route_gates.T,
        block_table,
        cache_blocks,
        w_output,
        w_gate_up,
        w_down,
        shared_gate_up,
        shared_down,
        w_query_key_value,
    )


def solution(mesh):
    in_specs = (
        P("pool", "head"),
        P("pool", None, "head"),
        P("pool", None, None, "head"),
        P(),
        P(),
        P("pool", None),
        P("head", None),
        P(),
        P(),
        P(),
        P("pool", "head", None, None),
        P("pool", None, "head"),
        P(None, "head", None, None),
        P(None, None, "head"),
        P(),
        P(None, "head"),
    )
    out_specs = (P("pool", None), P("pool", "head"))
    return jax.shard_map(
        per_device, mesh=mesh, in_specs=in_specs, out_specs=out_specs, check_vma=False
    )
```

```python
import math

import jax
import jax.numpy as jnp
from jax import lax
from jax.experimental import pallas as pl
from jax.experimental.pallas import tpu as pltpu
from jax.sharding import PartitionSpec as P

HD = 128
NP = 32
NH = 8
T = 10
TP = 16
CW = 256
FFE = 1408
BLK = 36
BP = 40
BS = 64
TOK = BLK * BS
RP = 24
EW = 2 * FFE + 128
SW = 2 * CW + 128
epsilon = 1e-06
low = -1e30
f32 = jnp.float32
bf16 = jnp.bfloat16
i32 = jnp.int32
MESH = pl.DeviceIdType.MESH


def iota(shape, dim):
    return lax.broadcasted_iota(i32, shape, dim)


def dot(a, b):
    return jnp.dot(a, b, preferred_element_type=f32)


def dot_t(a, b):
    return lax.dot_general(a, b, (((0,), (0,)), ((), ())), preferred_element_type=f32)


def hot(cond):
    return jnp.where(cond, 1.0, 0.0).astype(bf16)


def kernel(
    queries_hbm,
    fresh_hbm,
    residual_hbm,
    gain_hbm,
    next_gain_hbm,
    len_hbm,
    routes_hbm,
    gates_hbm,
    table_hbm,
    cache_hbm,
    wout_hbm,
    wgu_hbm,
    wdn_hbm,
    sgu_hbm,
    sdn_hbm,
    wqkv_hbm,
    hid_ref,
    qkv_ref,
    queries_v,
    fresh_v,
    residual_v,
    gain_v,
    next_gain_v,
    len_v,
    routes_v,
    gates_v,
    table_v,
    cache_v,
    wout_v,
    wgu_v,
    wdn_v,
    sgu_v,
    sdn_v,
    wqkv_v,
    wgu2,
    sgu2,
    abuf,
    bsend,
    bbuf,
    csend,
    cbuf,
    dsend,
    dbuf,
    esend,
    edown,
    eup,
    fbuf,
    sbuf,
    ssend,
    tbuf,
    gsend,
    gbuf,
    hbuf,
    lsem,
    ssem,
    rsem,
    essem,
    ersem,
    fssem,
    frsem,
    hrsem,
    fdsem,
    fdrsem,
):
    p = lax.axis_index("pool")
    h = lax.axis_index("head")

    loads = {
        name: pltpu.make_async_copy(src, dst, lsem.at[n])
        for n, (name, src, dst) in enumerate(
            [
                ("queries", queries_hbm, queries_v),
                ("table", table_hbm, table_v.at[pl.ds(0, 320)]),
                ("len", len_hbm, len_v),
                ("cache", cache_hbm, cache_v),
                ("routes", routes_hbm, routes_v),
                ("gates", gates_hbm, gates_v),
                ("fresh", fresh_hbm, fresh_v),
                ("sgu", sgu_hbm, sgu_v),
                ("wgu", wgu_hbm, wgu_v),
                ("wout", wout_hbm, wout_v),
                ("residual", residual_hbm, residual_v),
                ("gain", gain_hbm, gain_v),
                ("wdn", wdn_hbm, wdn_v),
                ("sdn", sdn_hbm, sdn_v),
                ("next_gain", next_gain_hbm, next_gain_v),
                ("wqkv", wqkv_hbm, wqkv_v),
            ]
        )
    }
    loads["queries"].start()

    barrier = pltpu.get_barrier_semaphore()

    def greet_pool(k, carry):
        pl.semaphore_signal(
            barrier, inc=1, device_id={"pool": lax.rem(p + k, NP)}, device_id_type=MESH
        )
        return carry

    def greet_head(k, carry):
        pl.semaphore_signal(
            barrier, inc=1, device_id={"head": lax.rem(h + k, NH)}, device_id_type=MESH
        )
        return carry

    lax.fori_loop(1, NP, greet_pool, 0)
    lax.fori_loop(1, NH, greet_head, 0)
    for name in ("table", "len"):
        loads[name].start()

    waited = set()
    pending = []

    def arrive(*names):
        for name in names:
            loads[name].wait()
            waited.add(name)


    def send_pool(src, buf, n):
        def one(k, carry):
            j = lax.rem(p + k, NP)
            pltpu.make_async_remote_copy(
                src_ref=src(j),
                dst_ref=buf.at[p],
                send_sem=ssem.at[n],
                recv_sem=rsem.at[n],
                device_id={"pool": j},
                device_id_type=MESH,
            ).start()
            return carry

        lax.fori_loop(1, NP, one, 0)
        pending.append(lambda: wait(buf, ssem, n, NP - 1))

    def send_head(src, buf, n):
        def one(k, carry):
            j = lax.rem(h + k, NH)
            pltpu.make_async_remote_copy(
                src_ref=src(j),
                dst_ref=buf.at[h],
                send_sem=ssem.at[n],
                recv_sem=rsem.at[n],
                device_id={"head": j},
                device_id_type=MESH,
            ).start()
            return carry

        lax.fori_loop(1, NH, one, 0)
        pending.append(lambda: wait(buf, ssem, n, NH - 1))

    def wait(buf, sem, n, count):
        view = buf.at[pl.ds(0, count)]
        pltpu.make_async_copy(view, view, sem.at[n]).wait()

    arrive("queries")
    rows_pad = jnp.zeros((TP - T, CW), f32)
    q_own = jnp.concatenate([queries_v[...].astype(f32), rows_pad], axis=0)
    abuf[p] = jnp.concatenate(
        [q_own[0:T, 0:HD], q_own[0:T, HD:CW], rows_pad[0:4, 0:HD]], axis=0
    ).astype(bf16)
    pl.semaphore_wait(barrier, NP - 1 + NH - 1)
    send_pool(lambda j: abuf.at[p], abuf, 0)
    for name in loads:
        if name not in ("queries", "table", "len"):
            loads[name].start()

    table_v[pl.ds(320, 64), :] = jnp.zeros((64, 256), i32)
    arrive("table", "len")
    table = table_v[...].astype(f32)
    heads_t = jnp.transpose(table[:, 0:128])
    lane = iota((1, 384), 1)
    real = lane < 320
    blk = iota((BP, 1), 0)
    ids = jnp.where(blk < BLK, blk + BLK * p, -7).astype(f32)
    len_row = jnp.concatenate(
        [len_v[...].reshape(1, 320).astype(f32), jnp.zeros((1, 64), f32)], axis=1
    )
    hot0 = jnp.where((heads_t[0:1] == ids) & real, 1.0, 0.0)
    hot1 = jnp.where((heads_t[1:2] == ids) & real, 1.0, 0.0)
    is_long = (heads_t[2:3] >= 0.0) & real
    lane_f = lane.astype(f32)
    first = jnp.min(jnp.where(is_long, lane_f, 1e6), axis=1, keepdims=True)
    last = jnp.max(jnp.where(is_long, lane_f, -1.0), axis=1, keepdims=True)
    row_f = iota((384, 1), 0).astype(f32)
    col = iota((1, 256), 1)
    owned = hot0 + hot1
    rank = jnp.sum(hot1, axis=1, keepdims=True)
    for which in (first, last):
        listed = jnp.sum(jnp.where(row_f == which, table, 0.0), axis=0, keepdims=True)
        match = jnp.where((listed == ids) & (col >= 2), 1.0, 0.0)
        found = jnp.max(match, axis=1, keepdims=True)
        rank = rank + jnp.sum(match * col.astype(f32), axis=1, keepdims=True)
        owned = owned + found * jnp.where(lane_f == which, 1.0, 0.0)
    owner_len = jnp.sum(owned * len_row, axis=1, keepdims=True)
    live = jnp.clip(owner_len - BS * rank, 0.0, float(BS))
    mine = owned > 0.5
    blk_f = blk.astype(f32)
    lead = jnp.min(jnp.where(mine, blk_f, 99.0), axis=0, keepdims=True)
    rep = jnp.max(jnp.where(mine & (lead == blk_f), 1.0, 0.0), axis=1, keepdims=True)
    r_in = iota((384, NP * RP), 0)
    group = lax.shift_right_logical(r_in * 205, 11)
    l_out = iota((384, NP * RP), 1)
    owned_b = owned.astype(bf16)
    hot_a = dot(owned_b, hot((l_out == r_in + 14 * group) & (r_in < 320)))
    hot_q = dot(owned_b, hot((l_out == RP * group + 20) & (r_in < 320)))
    hot_b = pltpu.roll(hot_a, T, 1)
    place = jnp.concatenate(
        [hot_a, hot_b, hot_q] + [pltpu.roll(hot_q, q, 1) for q in (1, 2, 3)], axis=0
    )
    place_t = jnp.transpose(place).astype(bf16)
    place = place[0 : 2 * BP].astype(bf16)
    lane_k = lane - 10 * lax.shift_right_logical(lane * 205, 11)
    which_row = jnp.sum(owned * lane_k.astype(f32), axis=1, keepdims=True)
    at_row = iota((BP, 128), 1) == which_row.astype(i32)
    tok = iota((BP, TOK), 1)
    start = blk * BS
    usable = (tok >= start) & (tok < start + live.astype(i32))

    arrive("sgu")
    for t in range(11):
        sgu2[:, t * 128 : (t + 1) * 128] = sgu_v[0, :, :, t * 128 : (t + 1) * 128].reshape(
            2 * CW, 128
        )
    arrive("cache")

    wait(abuf, rsem, 0, NP - 1)
    scale = 1.0 / math.sqrt(HD)
    all_queries = abuf[...].reshape(NP * RP, HD)
    none = jnp.zeros((BP, HD), f32)
    picked = dot(place, all_queries)
    picked = jnp.concatenate(
        [
            jnp.concatenate([picked[0:BP], none], axis=1),
            jnp.concatenate([none, picked[BP:]], axis=1),
        ],
        axis=0,
    ).astype(bf16)
    keys = cache_v[:, 0].reshape(TOK, CW)
    scores = (
        lax.dot_general(picked, keys, (((1,), (1,)), ((), ())), preferred_element_type=f32) * scale
    )
    shifts = []
    totals = []
    weights = []
    for hd in range(2):
        score = jnp.where(usable, scores[hd * BP : (hd + 1) * BP], low)
        top = jnp.max(score, axis=1, keepdims=True)
        req_top = jnp.max(jnp.where(mine, top, low), axis=0, keepdims=True)
        shift = jnp.max(jnp.where(mine, req_top, low), axis=1, keepdims=True)
        shift = shift.astype(bf16).astype(f32)
        weight = jnp.where(usable, jnp.exp(score - shift), 0.0)
        totals.append(jnp.sum(weight, axis=1, keepdims=True))
        shifts.append(shift)
        weights.append(weight.astype(bf16))
    values = cache_v[:, 1].reshape(TOK, CW)
    both_parts = dot(jnp.concatenate(weights, axis=0), values)
    parts = [both_parts[0:BP, 0:HD], both_parts[BP:, HD:CW]]
    tails = [jnp.where(rep > 0.5, shift, 0.0) for shift in shifts] + totals
    message = jnp.concatenate(
        parts + [jnp.where(at_row, tail, 0.0) for tail in tails], axis=0
    ).astype(bf16)
    bsend[...] = dot(place_t, message).astype(bf16).reshape(NP, RP, 128)
    bbuf[p] = bsend[p]
    send_pool(lambda j: bsend.at[j], bbuf, 1)

    arrive("routes", "gates")
    own_lane = iota((TP, 320), 1)
    own_row = iota((TP, 320), 0)
    own = (own_lane == own_row + T * p) & (own_row < T)
    row16 = iota((TP, 1), 0)
    lane_e = iota((TP, 128), 1)
    named = jnp.zeros((TP, 128), f32)
    gate = jnp.zeros((TP, 128), f32)
    routes_t = routes_v[...].astype(f32)
    gates_t = gates_v[...]
    for k in range(6):
        pick = jnp.sum(jnp.where(own, routes_t[k : k + 1], 0.0), axis=1, keepdims=True)
        pick = jnp.where(row16 < T, pick, -1.0).astype(i32)
        amount = jnp.sum(jnp.where(own, gates_t[k : k + 1], 0.0), axis=1, keepdims=True)
        named = named + jnp.where(lane_e == pick, 1.0, 0.0)
        gate = gate + jnp.where(lane_e == pick, amount, 0.0)
    earlier = hot(iota((TP, TP), 1) < iota((TP, TP), 0))
    order = dot(earlier, named.astype(bf16))
    gate_hi = gate.astype(bf16)
    gate_lo = (gate - gate_hi.astype(f32)).astype(bf16)
    table_nr = jnp.concatenate([named, order], axis=0).astype(bf16)
    l_g = iota((128, 256), 1)
    exp_g = hot(
        iota((128, 256), 0)
        == 2 * lax.shift_right_logical(l_g, 3) + (lax.shift_right_logical(l_g, 1) & 1)
    )
    wide = dot(jnp.concatenate([table_nr, gate_hi, gate_lo], axis=0), exp_g)
    l8 = iota((TP, 256), 1)
    sel = (wide[0:TP] > 0.5) & (wide[TP : 2 * TP].astype(i32) == (l8 & 1))
    half = lax.shift_right_logical(l8, 2) & 1
    sel32 = jnp.transpose(
        jnp.concatenate([jnp.where(sel & (half == c), 1.0, 0.0) for c in range(2)], axis=0)
    ).astype(bf16)
    combine = jnp.concatenate(
        [
            jnp.where(sel & (half == c), wide[(2 + part) * TP : (3 + part) * TP], 0.0)
            for c in range(2)
            for part in range(2)
        ],
        axis=0,
    ).astype(bf16)
    arrive("wgu")
    for t in range(11):
        wgu2[0, :, t * 128 : (t + 1) * 128] = wgu_v[0, :, :, t * 128 : (t + 1) * 128].reshape(
            2 * CW, 128
        )
    arrive("wout", "fresh", "residual", "gain")

    l_row = iota((128, NP * RP), 1)
    r_row = iota((128, NP * RP), 0)
    take_sums = hot(l_row == (r_row & 31) * RP + 20 + lax.shift_right_logical(r_row, 5))
    l_row = iota((64, NP * RP), 1)
    r_row = iota((64, NP * RP), 0)
    source = lax.shift_right_logical(l_row * 2731, 16)
    keep = (l_row - RP * source) == (r_row & 15) + T * lax.shift_right_logical(r_row, 5)
    widen = hot(source[0:NP] == r_row[0:NP])
    diagonal = iota((TP, 128), 0) == iota((TP, 128), 1)
    k_own = jnp.concatenate([fresh_v[:, 0, :].astype(f32), rows_pad], axis=0)
    v_own = jnp.concatenate([fresh_v[:, 1, :].astype(f32), rows_pad], axis=0)
    wait(bbuf, rsem, 1, NP - 1)
    received = bbuf[...].reshape(NP * RP, 128)
    sums = dot(take_sums, received)
    columns = []
    fresh_ws = []
    for hd in range(2):
        cols = slice(hd * HD, (hd + 1) * HD)
        fresh = jnp.sum(q_own[:, cols] * k_own[:, cols], axis=1, keepdims=True) * scale
        fresh = jnp.sum(jnp.where(diagonal, fresh, 0.0), axis=0, keepdims=True)
        total = sums[(2 + hd) * NP : (3 + hd) * NP]
        tops = jnp.where(total > 0.0, sums[hd * NP : (hd + 1) * NP], low)
        peak = jnp.maximum(jnp.max(tops, axis=0, keepdims=True), fresh)
        share = jnp.exp(tops - peak)
        fresh_w = jnp.exp(fresh - peak)
        denom = jnp.sum(share * total, axis=0, keepdims=True) + fresh_w
        share = (share / denom)[:, 0:TP]
        share_hi = share.astype(bf16).astype(f32)
        columns += [share_hi, share - share_hi]
        fresh_ws.append(
            jnp.sum(jnp.where(diagonal, fresh_w / denom, 0.0), axis=1, keepdims=True)
        )
    spread_w = dot_t(jnp.concatenate(columns, axis=1).astype(bf16), widen)
    mixed = dot(jnp.where(keep, spread_w, 0.0).astype(bf16), received)
    joined = [
        mixed[2 * hd * TP : (2 * hd + 1) * TP]
        + mixed[(2 * hd + 1) * TP : (2 * hd + 2) * TP]
        + fresh_ws[hd] * v_own[:, hd * HD : (hd + 1) * HD]
        for hd in range(2)
    ]
    attended = jnp.concatenate(joined, axis=1)[0:T]
    blank = jnp.zeros((T, CW), f32)
    attended = jnp.concatenate(
        [
            jnp.concatenate([attended, blank], axis=1),
            jnp.concatenate([blank, attended], axis=1),
            jnp.zeros((RP - 2 * T, 2 * CW), f32),
        ],
        axis=0,
    ).astype(bf16)
    for j in range(NH):
        block = jnp.concatenate(
            [
                wout_v[:, j * CW : j * CW + 128],
                wout_v[:, j * CW + 128 : (j + 1) * CW],
            ],
            axis=0,
        )
        csend[j] = dot(attended, block).astype(bf16)
    cbuf[h] = csend[h]
    send_head(lambda j: csend.at[j], cbuf, 2)

    for t in range(6):
        wgu2[1, :, t * 128 : (t + 1) * 128] = wgu_v[1, :, :, t * 128 : (t + 1) * 128].reshape(
            2 * CW, 128
        )

    wait(cbuf, rsem, 2, NH - 1)
    own_cols = pl.ds(pl.multiple_of(h * CW, CW), CW)
    after = jnp.concatenate([residual_v[:, own_cols].astype(f32), rows_pad], axis=0)
    summed = cbuf[0].astype(f32)
    for j in range(1, NH):
        summed = summed + cbuf[j].astype(f32)
    after = after + jnp.concatenate(
        [jnp.concatenate([summed[0:T], summed[T : 2 * T]], axis=1), rows_pad], axis=0
    )
    gain_own = gain_v[own_cols].astype(f32).reshape(1, CW)
    scaled = (after * gain_own).astype(bf16)
    square = jnp.sum(after * after, axis=1, keepdims=True)
    square_hi = square.astype(bf16).astype(f32)
    lane_t = iota((TP, 128), 1)
    squares = jnp.where(lane_t == 0, square_hi, jnp.where(lane_t == 1, square - square_hi, 0.0))
    rows32 = jnp.concatenate([scaled[:, 0:128], scaled[:, 128:256]], axis=0)
    dsend[...] = dot(sel32, rows32).astype(bf16).reshape(NP, 8, 128)
    dbuf[p] = dsend[p]
    send_pool(lambda j: dsend.at[j], dbuf, 3)

    d_in = iota((CW, 2 * CW), 0)
    d_out = iota((CW, 2 * CW), 1)
    to_gate = hot(d_out == 2 * d_in)
    to_up = hot(d_out == 2 * d_in + 1)
    spread_own = jnp.concatenate([dot(scaled, to_gate), dot(scaled, to_up)], axis=0).astype(bf16)
    shared = dot(spread_own, sgu2[...]).astype(bf16)
    for j in range(NH):
        width = min(CW, max(0, FFE - j * CW))
        for c in range(2):
            at = c * CW
            if width > 0:
                ssend[j, :, at : at + width] = shared[
                    c * TP : (c + 1) * TP, j * CW : j * CW + width
                ]
            if width < CW:
                ssend[j, :, at + width : at + CW] = jnp.zeros((TP, CW - width), bf16)
        ssend[j, :, 2 * CW :] = squares.astype(bf16)
    sbuf[h] = ssend[h]
    send_head(lambda j: ssend.at[j], sbuf, 6)
    for t in range(6, 11):
        wgu2[1, :, t * 128 : (t + 1) * 128] = wgu_v[1, :, :, t * 128 : (t + 1) * 128].reshape(
            2 * CW, 128
        )
    slot = iota((128, 256), 0)
    from_row = (
        (lax.shift_right_logical(slot, 1) & 31) * 8
        + lax.shift_right_logical(slot, 6) * 2
        + (slot & 1)
    )
    source = iota((128, 256), 1)
    gathers = [hot(source == from_row + 4 * c) for c in range(2)]
    lane_s = iota((128, 128), 1)

    wait(dbuf, rsem, 3, NP - 1)
    arrived = dbuf[...].reshape(NP * 8, 128)
    rows = jnp.concatenate([dot(gathers[0], arrived), dot(gathers[1], arrived)], axis=1)
    plain = rows / gain_own
    square = jnp.sum(plain * plain, axis=1, keepdims=True)
    square_hi = square.astype(bf16).astype(f32)
    row_squares = jnp.where(
        lane_s == 0, square_hi, jnp.where(lane_s == 1, square - square_hi, 0.0)
    )
    rows = rows.astype(bf16)
    for_gate = dot(rows, to_gate).astype(bf16)
    for_up = dot(rows, to_up).astype(bf16)
    boths = [
        jnp.concatenate([for_gate[e * 64 : (e + 1) * 64], for_up[e * 64 : (e + 1) * 64]], axis=0)
        for e in range(2)
    ]

    def ring_copy(src, dst, send_sem, recv_sem, to):
        return pltpu.make_async_remote_copy(
            src_ref=src,
            dst_ref=dst,
            send_sem=send_sem,
            recv_sem=recv_sem,
            device_id={"head": to},
            device_id_type=MESH,
        )

    down = lax.rem(h + NH - 1, NH)
    up = lax.rem(h + 1, NH)
    e_parts = [(0, 896), (896, 1664), (1664, 2432), (2432, 2944)]
    f_cols = [(0, 384), (384, 768), (768, 1152), (1152, 1408)]
    sides = ((down, edown, -1), (up, eup, 1))

    def off(by):
        return lax.rem(h + by + NH, NH)

    def e_copy(n, way, chunk, slot, to):
        lo, hi = e_parts[n]
        land = sides[way][1]
        return ring_copy(
            esend.at[chunk, :, pl.ds(lo, hi - lo)],
            land.at[slot, :, pl.ds(lo, hi - lo)],
            essem.at[way, n],
            ersem.at[way, slot, n],
            to,
        )

    def e_take(n, way, slot):
        lo, hi = e_parts[n]
        e_copy(n, way, h, slot, down).wait_recv()
        return sides[way][1][slot, :, lo:hi].astype(f32)

    for n, (lo, _) in enumerate(e_parts):
        c_lo, c_hi = f_cols[n]
        wide = c_hi - c_lo
        for e in range(2):
            partial = dot(boths[e], wgu2[e, :, c_lo:c_hi]).astype(bf16)
            for j in range(4):
                for c in range(2):
                    esend[4 * e + j, :, lo + c * wide : lo + (c + 1) * wide] = partial[
                        c * 64 + j * TP : c * 64 + (j + 1) * TP
                    ]
        if n == 0:
            for j in range(NH):
                esend[j, :, 768:896] = row_squares[j * TP : (j + 1) * TP].astype(bf16)
        for way, (_, _, sign) in enumerate(sides):
            if n % 2 == way:
                e_copy(n, way, off(4 * sign), 0, off(sign)).start()
                e_copy(n, way, off(2 * sign), 1, off(sign)).start()
            else:
                e_copy(n, way, off(3 * sign), 0, off(sign)).start()

    for n, (lo, hi) in enumerate(e_parts):
        for way, (_, _, sign) in enumerate(sides):
            longer = n % 2 == way
            chunk = off(3 * sign) if longer else off(2 * sign)
            passed = esend[chunk, :, lo:hi].astype(f32) + e_take(n, way, 0)
            esend[chunk, :, lo:hi] = passed.astype(bf16)
            if longer:
                e_copy(n, way, chunk, 2, off(2 * sign)).start()
            else:
                e_copy(n, way, chunk, 1, off(sign)).start()
    for n, (lo, hi) in enumerate(e_parts):
        for way, (_, _, sign) in enumerate(sides):
            chunk = off(sign)
            passed = esend[chunk, :, lo:hi].astype(f32) + e_take(n, way, 1)
            if n % 2 == way:
                passed = passed + e_take(n, way, 2)
            esend[chunk, :, lo:hi] = passed.astype(bf16)
            e_copy(n, way, chunk, 3, chunk).start()

    def e_drain():
        for way, land in enumerate((edown, eup)):
            for n, (lo, hi) in enumerate(e_parts):
                view = land.at[pl.ds(0, 4 if n % 2 == way else 3), :, pl.ds(lo, hi - lo)]
                pltpu.make_async_copy(view, view, essem.at[way, n]).wait()

    pending.append(e_drain)
    f_parts = [(0, 768)]
    f_late = [(768, 1152), (1152, FFE)]

    def f_direct(n, k):
        lo, hi = f_late[n]
        view = fbuf.at[h, :, pl.ds(lo, hi - lo)]
        return ring_copy(view, view, fdsem.at[n], fdrsem.at[n, k], off(k))


    def f_send(n, way, origin, hop):
        lo, hi = f_parts[n]
        sign = sides[way][2]
        view = fbuf.at[off(-sign * origin), :, pl.ds(lo, hi - lo)]
        ring_copy(
            view, view, fssem.at[way, n], frsem.at[way, origin + hop - 1, n], off(sign * hop)
        ).start()

    def f_wait(n, way, origin):
        lo, hi = f_parts[n]
        view = fbuf.at[off(-sides[way][2] * origin), :, pl.ds(lo, hi - lo)]
        ring_copy(
            view, view, fssem.at[way, n], frsem.at[way, origin - 1, n], down
        ).wait_recv()

    r_slot = None
    for n, (lo, hi) in enumerate(e_parts):
        piece = esend[h, :, lo:hi].astype(f32)
        for way in range(2):
            piece = piece + e_take(n, way, 3)
        c_lo, c_hi = f_cols[n]
        wide = c_hi - c_lo
        if n == 0:
            r_slot = lax.rsqrt((piece[:, 768:769] + piece[:, 769:770]) * (1.0 / 2048) + epsilon)
        g = piece[:, 0:wide] * r_slot
        u = piece[:, wide : 2 * wide] * r_slot
        fbuf[h, :, c_lo:c_hi] = (g / (1.0 + jnp.exp(-g)) * u).astype(bf16)
        if n == 1:
            for hop in (2, 1):
                for way in range(2):
                    f_send(0, way, 0, hop)
        if n >= 2:
            for k in (4, 3, 5, 2, 6, 1, 7):
                f_direct(n - 2, k).start()
    for n in range(1):
        for way in range(2):
            f_wait(n, way, 2)
            if n == way:
                f_send(n, way, 2, 2)
            f_send(n, way, 2, 1)

    wait(sbuf, rsem, 6, NH - 1)
    total = sbuf[0].astype(f32)
    for j in range(1, NH):
        total = total + sbuf[j].astype(f32)
    ss = total[:, 2 * CW :]
    r_own = lax.rsqrt((ss[:, 0:1] + ss[:, 1:2]) * (1.0 / 2048) + epsilon)
    g = total[:, 0:CW] * r_own
    u = total[:, CW : 2 * CW] * r_own
    tbuf[h] = (g / (1.0 + jnp.exp(-g)) * u).astype(bf16)
    send_head(lambda j: tbuf.at[h], tbuf, 7)

    def f_drain():
        for way in range(2):
            for n, (lo, hi) in enumerate(f_parts):
                view = fbuf.at[pl.ds(0, 4 if n == way else 3), :, pl.ds(lo, hi - lo)]
                pltpu.make_async_copy(view, view, fssem.at[way, n]).wait()

    pending.append(f_drain)

    def f_late_drain():
        for n, (lo, hi) in enumerate(f_late):
            view = fbuf.at[pl.ds(0, NH - 1), :, pl.ds(lo, hi - lo)]
            pltpu.make_async_copy(view, view, fdsem.at[n]).wait()

    pending.append(f_late_drain)
    arrive("wdn", "sdn", "next_gain", "wqkv")
    back = iota((256, 256), 0)
    kk = iota((256, 256), 1)
    slot_of = (
        (lax.shift_right_logical(back, 1) & 1) * 64
        + lax.shift_right_logical(back, 3) * 2
        + (back & 1)
        + (lax.shift_right_logical(back, 2) & 1) * 128
    )
    returns = hot(kk == slot_of)

    outs = [0.0, 0.0]
    for n, (lo, hi) in enumerate([(0, 768), (768, FFE)]):
        if n == 0:
            for way in range(2):
                for origin in (1, 3, 4) if way == 0 else (1, 3):
                    f_wait(0, way, origin)
        else:
            for late, (a, b) in enumerate(f_late):
                for k in range(1, NH):
                    view = fbuf.at[off(-k), :, pl.ds(a, b - a)]
                    ring_copy(view, view, fdsem.at[late], fdrsem.at[late, k], down).wait_recv()
        for e in range(2):
            rows_e = fbuf[4 * e : 4 * e + 4, :, lo:hi].reshape(64, hi - lo)
            outs[e] = outs[e] + dot(rows_e, wdn_v[e, lo:hi, :])
    outs = [out.astype(bf16) for out in outs]
    stacked = jnp.concatenate(
        [outs[0][:, 0:128], outs[1][:, 0:128], outs[0][:, 128:256], outs[1][:, 128:256]], axis=0
    )
    gsend[...] = dot(returns, stacked).astype(bf16).reshape(NP, 8, 128)
    gbuf[p] = gsend[p]
    send_pool(lambda j: gsend.at[j], gbuf, 4)
    wait(tbuf, rsem, 7, NH - 1)
    for j in range(6):
        width = min(CW, FFE - j * CW)
        after = after + dot(tbuf[j, :, 0:width], sdn_v[0, j * CW : j * CW + width, :])
    wait(gbuf, rsem, 4, NP - 1)
    routed = dot(combine, gbuf[...].reshape(NP * 8, 128))
    routed = jnp.concatenate(
        [routed[0:TP] + routed[TP : 2 * TP], routed[2 * TP : 3 * TP] + routed[3 * TP :]], axis=1
    )
    final = (after + routed)[0:T]
    hbuf[h] = jnp.concatenate(
        [final[:, 0:128], final[:, 128:], jnp.zeros((RP - 2 * T, 128), f32)], axis=0
    ).astype(bf16)

    def h_copy(k):
        return pltpu.make_async_remote_copy(
            src_ref=hbuf.at[h],
            dst_ref=hbuf.at[h],
            send_sem=ssem.at[5],
            recv_sem=hrsem.at[k],
            device_id={"head": off(k)},
            device_id_type=MESH,
        )

    for k in (4, 3, 5, 2, 6, 1, 7):
        h_copy(k).start()
    pending.append(lambda: wait(hbuf, ssem, 5, NH - 1))

    mean = jnp.zeros((T, 1), f32)
    projected = jnp.zeros((T, 768), f32)
    for k in (0, 1, 7, 2, 6, 3, 5, 4):
        j = off(-k)
        if k > 0:
            view = hbuf.at[j]
            pltpu.make_async_copy(view, view, hrsem.at[k]).wait()
        at = pl.multiple_of(j * CW, CW)
        piece = hbuf[j].astype(f32)
        piece = jnp.concatenate([piece[0:T], piece[T : 2 * T]], axis=1)
        hid_ref[:, pl.ds(at, CW)] = piece.astype(bf16)
        mean = mean + jnp.sum(piece * piece, axis=1, keepdims=True)
        piece = piece * next_gain_v[pl.ds(at, CW)].astype(f32).reshape(1, CW)
        projected = projected + dot(piece.astype(bf16), wqkv_v[pl.ds(at, CW), :])
    r_next = lax.rsqrt(mean * (1.0 / 2048) + epsilon)
    qkv_ref[...] = (projected * r_next).astype(bf16)

    for finish in pending:
        finish()


def hand_over(hid_in, qkv_in, hid_out, qkv_out, sem):
    copies = [
        pltpu.make_async_copy(hid_in, hid_out, sem.at[0]),
        pltpu.make_async_copy(qkv_in, qkv_out, sem.at[1]),
    ]
    for copy in copies:
        copy.start()
    for copy in copies:
        copy.wait()


def per_device(
    queries,
    fresh_pair,
    cache_blocks,
    block_table,
    lengths,
    residual,
    w_output,
    norm_gain,
    routes,
    route_gates,
    w_gate_up,
    w_down,
    shared_gate_up,
    shared_down,
    next_gain,
    w_query_key_value,
):
    vmem = pl.BlockSpec(memory_space=pltpu.VMEM)
    hbm = pl.BlockSpec(memory_space=pltpu.HBM)
    return pl.pallas_call(
        kernel,
        out_shape=(pltpu.VMEM((T, 2048), bf16), pltpu.VMEM((T, 768), bf16)),
        in_specs=[hbm] * 16,
        out_specs=(vmem, vmem),
        scratch_shapes=[
            pltpu.VMEM((T, CW), bf16),
            pltpu.VMEM((T, 2, CW), bf16),
            pltpu.VMEM((T, 2048), bf16),
            pltpu.VMEM((2048,), bf16),
            pltpu.VMEM((2048,), bf16),
            pltpu.VMEM((320,), i32),
            pltpu.VMEM((6, 320), i32),
            pltpu.VMEM((6, 320), f32),
            pltpu.VMEM((384, 256), i32),
            pltpu.VMEM((BLK, 2, BS, CW), bf16),
            pltpu.VMEM((CW, 2048), bf16),
            pltpu.VMEM((2, CW, 2, FFE), bf16),
            pltpu.VMEM((2, FFE, CW), bf16),
            pltpu.VMEM((1, CW, 2, FFE), bf16),
            pltpu.VMEM((1, FFE, CW), bf16),
            pltpu.VMEM((2048, 768), bf16),
            pltpu.VMEM((2, 2 * CW, FFE), bf16),
            pltpu.VMEM((2 * CW, FFE), bf16),
            pltpu.VMEM((NP, RP, 128), bf16),
            pltpu.VMEM((NP, RP, 128), bf16),
            pltpu.VMEM((NP, RP, 128), bf16),
            pltpu.VMEM((NH, RP, 128), bf16),
            pltpu.VMEM((NH, RP, 128), bf16),
            pltpu.VMEM((NP, 8, 128), bf16),
            pltpu.VMEM((NP, 8, 128), bf16),
            pltpu.VMEM((NH, TP, EW), bf16),
            pltpu.VMEM((4, TP, EW), bf16),
            pltpu.VMEM((4, TP, EW), bf16),
            pltpu.VMEM((NH, TP, FFE), bf16),
            pltpu.VMEM((NH, TP, SW), bf16),
            pltpu.VMEM((NH, TP, SW), bf16),
            pltpu.VMEM((NH, TP, CW), bf16),
            pltpu.VMEM((NP, 8, 128), bf16),
            pltpu.VMEM((NP, 8, 128), bf16),
            pltpu.VMEM((NH, RP, 128), bf16),
            pltpu.SemaphoreType.DMA((16,)),
            pltpu.SemaphoreType.DMA((8,)),
            pltpu.SemaphoreType.DMA((8,)),
            pltpu.SemaphoreType.DMA((2, 4)),
            pltpu.SemaphoreType.DMA((2, 4, 4)),
            pltpu.SemaphoreType.DMA((2, 2)),
            pltpu.SemaphoreType.DMA((2, 4, 2)),
            pltpu.SemaphoreType.DMA((NH,)),
            pltpu.SemaphoreType.DMA((2,)),
            pltpu.SemaphoreType.DMA((2, NH)),
        ],
        compiler_params=pltpu.CompilerParams(
            collective_id=0, has_side_effects=True, vmem_limit_bytes=58 << 20
        ),
    )(
        queries,
        fresh_pair,
        residual,
        norm_gain,
        next_gain,
        lengths,
        routes.T,
        route_gates.T,
        block_table,
        cache_blocks,
        w_output,
        w_gate_up,
        w_down,
        shared_gate_up,
        shared_down,
        w_query_key_value,
    )


def solution(mesh):
    in_specs = (
        P("pool", "head"),
        P("pool", None, "head"),
        P("pool", None, None, "head"),
        P(),
        P(),
        P("pool", None),
        P("head", None),
        P(),
        P(),
        P(),
        P("pool", "head", None, None),
        P("pool", None, "head"),
        P(None, "head", None, None),
        P(None, None, "head"),
        P(),
        P(None, "head"),
    )
    out_specs = (P("pool", None), P("pool", "head"))
    return jax.shard_map(
        per_device, mesh=mesh, in_specs=in_specs, out_specs=out_specs, check_vma=False
    )
```
